512 devices in a mesh: rep: 32 (over x, y), tp: 16 (over z, core).
Axes of the slice: x: 4, y: 8, z: 8, core: 2. Of those that a mesh axis runs over, the one named last changes fastest.
Arguments:
- queries: bfloat16 [416, 48, 4096], P('rep', None, 'tp'), may hold values from -33 to 33
- tree_cache: bfloat16 [416, 2, 48, 4096], P('rep', None, None, 'tp'), may hold values from -11 to 11
- tree_mask: int32 [416, 48, 48], P('rep'), may hold values from 0 to 1, as said below
- dest_group: int32 [416, 1], P('rep'), may hold values from 0 to 31; in each aligned block of 13 rows (0 to 12, 13 to 25, ...) at most 2 rows name the same one
- accepted_path: int32 [416, 8], P('rep'), may hold values from 0 to 47
- prompt_cache: bfloat16 [32, 2, 152, 4096], P('rep', None, None, 'tp'), may hold values from -11 to 11
- first_len: int32 [32], P('rep'), may hold values from 2 to 152
- spill_cache: bfloat16 [32, 2, 152, 4096], P('rep', None, None, 'tp'), may hold values from -6 to 6
- spill_len: int32 [32], P('rep'), may hold values from 76 to 152
- out_weight: bfloat16 [4096, 4096], P(None, 'tp'), may hold values from -0.09375 to 0.09375
Outputs:
- projected: bfloat16 [416, 48, 4096], P('rep', None, 'tp')
- accepted_cache: bfloat16 [416, 2, 8, 4096], P('rep', None, None, 'tp')
The draws below stay inside these ranges and needn't reach their ends.
Inputs may be any that keep to these rules, and one draw needn't show every extreme that they name: `dest_group`: in each aligned block of 13 requests (those of one index of rep) no group is named more than 2 times. Row t of tree_mask[r] marks token t and its ancestors in a tree whose parents come before their children.
All inputs are finite; a program needn't handle non-finite values.
Results may differ from the reference program's by a relative error of at most 0.014.
Values may be sent and summed in bfloat16 or wider, within the bound.
A program may use at most 64 MiB of HBM per device.

```python
import math
from functools import partial
import jax
import jax.numpy as jnp
import numpy as np
from jax import lax

HD = 128
HEADS = 32
DW = 4096
TREE = 48
ACC = 8
PCAP = 152
REQ_DEV = 13
CAP = 2
REQUESTS = 416
GROUPS = 32
C = 4096


def draw_queries(key, part):
    base_key = jax.random.fold_in(key, 11)
    values = jnp.clip(jax.random.normal(base_key, (REQUESTS, TREE, HEADS * HD), jnp.float32), -4.5, 4.5)
    return values.astype(jnp.bfloat16)


def draw_prompt_cache(key, part):
    base_key = jax.random.fold_in(key, 17)
    values = jnp.clip(jax.random.normal(base_key, (GROUPS, 2, PCAP, HEADS * HD), jnp.float32), -4.5, 4.5)
    return values.astype(jnp.bfloat16)


def draw_tree_cache(key, part):
    base_key = jax.random.fold_in(key, 19)
    values = jnp.clip(jax.random.normal(base_key, (REQUESTS, 2, TREE, HEADS * HD), jnp.float32), -6.0, 6.0)
    return values.astype(jnp.bfloat16)


def draw_tree_mask(key, part):
    limits = jnp.maximum(jnp.arange(TREE, dtype=jnp.int32), 1)
    parents = jax.random.randint(key, (REQUESTS, TREE), 0, limits[None, :])

    def build_rows(parent_row):

        def extend(mask_rows, token):
            new_row = mask_rows[parent_row[token]].at[token].set(1)
            return (mask_rows.at[token].set(new_row), None)
        mask_rows, unused = lax.scan(extend, jnp.zeros((TREE, TREE), jnp.int32), jnp.arange(TREE, dtype=jnp.int32))
        return mask_rows
    return jax.vmap(build_rows)(parents)


def draw_first_len(key, part):
    lengths = jax.random.randint(key, (GROUPS,), 2, PCAP + 1)
    chosen = jax.random.randint(jax.random.fold_in(key, 3), (), 0, GROUPS)
    return lengths.at[chosen].set(PCAP)


def draw_spill_len(key, part):
    lengths = jax.random.randint(key, (GROUPS,), PCAP // 2, PCAP + 1)
    chosen = jax.random.randint(jax.random.fold_in(key, 3), (), 0, GROUPS)
    return lengths.at[chosen].set(PCAP)


def place_ends(values, rng, smallest, high):
    extent = values.shape
    index_at = [jax.random.randint(jax.random.fold_in(rng, axis), (), 0, extent[axis]) for axis in range(len(extent))]
    values = values.at[tuple(index_at)].set(smallest)
    longest = extent.index(max(extent))
    index_at[longest] = (index_at[longest] + 1) % extent[longest]
    return values.at[tuple(index_at)].set(high)


def block_levels(own_key, shape, pieces, low, largest):
    def one(axis_at, blocks):
        heights = jax.random.uniform(jax.random.fold_in(jax.random.fold_in(own_key, 6), axis_at), (blocks,), jnp.float32, low / len(pieces), largest / len(pieces))
        return jnp.repeat(jnp.exp(heights), shape[axis_at] // blocks).reshape((-1,) + (1,) * (len(shape) - axis_at - 1))

    gain = one(*pieces[0])
    for cut in pieces[1:]:
        gain = gain * one(*cut)
    return gain


def assign_block(stream_key, own, number, rows, number_of, top, limit, lean):
    order = jax.random.permutation(stream_key, number_of)
    crowded, common = shares(number_of, rows * top, limit, lean, True), shares(number_of, rows * top, limit, lean, False)
    places = jnp.arange(number_of)

    def named(sizes, rotation):
        used = int((sizes > 0).sum())
        fixed = max(1, used // 4)
        moved = fixed + (places - fixed + rotation * (used - fixed)) % max(1, number_of - fixed)
        return jnp.zeros((number_of,), jnp.int32).at[order[jnp.where(places < fixed, places, moved)]].set(jnp.asarray(sizes, jnp.int32))

    sizes = jnp.where(number % 4 == 0, named(crowded, number // 4), named(common, number - number // 4 - 1))
    mixed = jax.random.permutation(jax.random.fold_in(own, 3), number_of)
    source_of, taker = mixed[0:number_of // 2 * 2:2], mixed[1:number_of // 2 * 2:2]
    room = jnp.minimum(sizes[source_of] - 1, limit - sizes[taker]) // 2
    room = jnp.where((source_of == order[0]) | (taker == order[0]) | (sizes[taker] == 0), 0, jnp.maximum(room, 0))
    moved = jax.random.randint(jax.random.fold_in(own, 4), (number_of // 2,), 0, 1 << 20) % (room + 1)
    sizes = sizes.at[source_of].add(-moved).at[taker].add(moved)
    items = jnp.searchsorted(jnp.cumsum(sizes), jnp.arange(rows * top), side="right").astype(jnp.int32)
    table = items.reshape(top, rows).T
    table = table[jax.random.permutation(jax.random.fold_in(own, 1), rows)]
    rotation = jax.random.randint(jax.random.fold_in(own, 2), (rows, 1), 0, top)
    return jnp.take_along_axis(table, (jnp.arange(top)[None, :] + rotation) % top, axis=1)


def shares(number_of, total, bound, lean, full):
    weights = [(1 << 20) // math.isqrt(standing ** lean) + 1 for standing in range(1, number_of + 1)]
    largest = bound if full else min(bound, max(-(-total // number_of), total * weights[0] // sum(weights)))
    least = 1 if total - largest >= number_of - 1 else 0
    given, spare = [largest] + [least] * (number_of - 1), total - largest - least * (number_of - 1)
    while spare > 0:
        free = [i for i in range(1, number_of) if given[i] < largest] or [i for i in range(1, number_of) if given[i] < bound]
        pool, budget = sum([weights[i] for i in free]), spare
        for i in free:
            extra = min(bound - given[i], max(1, budget * weights[i] // pool), spare)
            given[i] = given[i] + extra
            spare = spare - extra
    return np.array(given)


def normal_values(stream_key, dims, spread, reach, shards=(), held_as=jnp.bfloat16):
    gain = block_levels(stream_key, dims, shards, -0.22, 0.18) if shards else 1.0
    entries = jax.random.normal(stream_key, dims, jnp.float32) * spread * gain
    return jnp.minimum(jnp.maximum(entries, -reach), reach).astype(held_as)


def setup_inputs(seed: int = 0) -> dict:
    key_list = jax.random.split(jax.random.key(seed), 11)
    queries = draw_queries(jax.random.fold_in(key_list[10], 71), 0)
    tree_cache = draw_tree_cache(jax.random.fold_in(key_list[10], 71), 0)
    tree_mask = draw_tree_mask(jax.random.fold_in(key_list[10], 71), 0)
    dest_group_keys = jax.random.split(jax.random.fold_in(key_list[3], 1), REQUESTS // REQ_DEV)
    dest_group_turns = jax.random.permutation(jax.random.fold_in(key_list[3], 3), REQUESTS // REQ_DEV)
    dest_group = jax.vmap(lambda own, number: assign_block(jax.random.fold_in(key_list[3], 2), own, number, REQ_DEV, GROUPS, 1, CAP, 2))(dest_group_keys, dest_group_turns).reshape((REQUESTS, 1))
    accepted_path = place_ends(jax.random.randint(key_list[4], (REQUESTS, ACC), 0, TREE), jax.random.fold_in(key_list[4], 1), 0, TREE - 1).astype(jnp.int32)
    prompt_cache = draw_prompt_cache(jax.random.fold_in(key_list[10], 71), 0)
    first_len = draw_first_len(jax.random.fold_in(key_list[10], 71), 0)
    spill_cache = normal_values(key_list[7], (GROUPS, 2, PCAP, C), 1.0, 6.0, ((0, 32), (3, 16)))
    spill_len = draw_spill_len(jax.random.fold_in(key_list[10], 71), 0)
    out_weight = normal_values(key_list[9], (C, DW), C ** -0.5, 0.09375, ((1, 16),))
    return dict(queries=queries, tree_cache=tree_cache, tree_mask=tree_mask, dest_group=dest_group, accepted_path=accepted_path, prompt_cache=prompt_cache, first_len=first_len, spill_cache=spill_cache, spill_len=spill_len, out_weight=out_weight)


NEG_FILL = -1e+30

def attend_request(inputs, prompt_cache, first_len, spill_cache, spill_len):
    query_block, tree_block, mask_block, group_id = inputs
    partner_id = jnp.bitwise_xor(group_id, 1).astype(jnp.int32)
    prompt_block = prompt_cache[group_id]
    spill_block = spill_cache[partner_id]
    positions = jnp.arange(PCAP, dtype=jnp.int32)
    prompt_seen = positions < first_len[group_id]
    spill_seen = positions < spill_len[partner_id]
    key_rows = jnp.concatenate([prompt_block[0], spill_block[0], tree_block[0]], axis=0).astype(jnp.float32)
    value_rows = jnp.concatenate([prompt_block[1], spill_block[1], tree_block[1]], axis=0).astype(jnp.float32)
    visible = jnp.concatenate([jnp.broadcast_to(prompt_seen[None, :], (TREE, PCAP)), jnp.broadcast_to(spill_seen[None, :], (TREE, PCAP)), mask_block == 1], axis=1)
    query_heads = query_block.astype(jnp.float32).reshape(TREE, HEADS, HD)
    key_heads = key_rows.reshape(-1, HEADS, HD)
    value_heads = value_rows.reshape(-1, HEADS, HD)
    scores = jnp.einsum('thd,lhd->htl', query_heads, key_heads) * (1.0 / math.sqrt(HD))
    scores = jnp.where(visible[None], scores, NEG_FILL)
    peaks = lax.optimization_barrier(jnp.max(scores, axis=2, keepdims=True))
    raw_weights = jnp.where(visible[None], jnp.exp(scores - peaks), 0.0)
    totals = lax.optimization_barrier(jnp.sum(raw_weights, axis=2))
    rounded = lax.optimization_barrier(raw_weights.astype(jnp.bfloat16)).astype(jnp.float32)
    accum = jnp.einsum('htl,lhd->thd', rounded, value_heads)
    attn = accum / jnp.transpose(totals)[:, :, None]
    return attn.reshape(TREE, HEADS * HD).astype(jnp.bfloat16)

def reference(queries, tree_cache, tree_mask, dest_group, accepted_path, prompt_cache, first_len, spill_cache, spill_len, out_weight):
    worker = partial(attend_request, prompt_cache=prompt_cache, first_len=first_len, spill_cache=spill_cache, spill_len=spill_len)
    attn = lax.map(worker, (queries, tree_cache, tree_mask, dest_group[:, 0].astype(jnp.int32)))
    flat_attn = attn.reshape(REQUESTS * TREE, HEADS * HD)
    projected = jnp.dot(flat_attn, out_weight, preferred_element_type=jnp.float32).astype(jnp.bfloat16)
    projected = projected.reshape(REQUESTS, TREE, DW)
    accepted_cache = jnp.take_along_axis(tree_cache, accepted_path[:, None, :, None].astype(jnp.int32), axis=2)
    return (projected, accepted_cache)
```

```python
import math

import jax
import jax.numpy as jnp
from jax import lax
from jax.sharding import PartitionSpec as P

HD = 128
TREE = 48
PCAP = 152


NEG_FILL = -1e30


def swapped(value, axis, apart):
    mask = 2**apart
    pairs = [(source, source ^ mask) for source in range(lax.axis_size(axis))]
    return lax.ppermute(value, axis, pairs)


def split_heads(rows):
    return rows.reshape(rows.shape[:-1] + (rows.shape[-1] // HD, HD))


def prompt_attend(query_rows, key_rows, value_rows, seen):
    q = split_heads(query_rows)
    k = split_heads(key_rows)
    v = split_heads(value_rows)
    scores = jnp.einsum("qhd,khd->hqk", q, k, preferred_element_type=jnp.float32) * (
        1.0 / math.sqrt(HD)
    )
    scores = jnp.where(seen[None, None, :], scores, NEG_FILL)
    peaks = jnp.max(scores, axis=2, keepdims=True)
    raw = jnp.where(seen[None, None, :], jnp.exp(scores - peaks), 0.0)
    totals = jnp.sum(raw, axis=2)
    accum = jnp.einsum(
        "hqk,khd->qhd", raw.astype(jnp.bfloat16), v, preferred_element_type=jnp.float32
    )
    normed = accum / jnp.transpose(totals)[:, :, None]
    lse = jnp.transpose(peaks[:, :, 0] + jnp.log(totals))
    return normed.reshape(query_rows.shape).astype(jnp.bfloat16), lse


def tree_attend(queries, keys, values, seen):
    q = split_heads(queries)
    k = split_heads(keys)
    v = split_heads(values)
    scores = jnp.einsum("rthd,rshd->rhts", q, k, preferred_element_type=jnp.float32) * (
        1.0 / math.sqrt(HD)
    )
    scores = jnp.where(seen[:, None], scores, NEG_FILL)
    peaks = jnp.max(scores, axis=3, keepdims=True)
    raw = jnp.where(seen[:, None], jnp.exp(scores - peaks), 0.0)
    totals = jnp.sum(raw, axis=3)
    accum = jnp.einsum(
        "rhts,rshd->rthd", raw.astype(jnp.bfloat16), v, preferred_element_type=jnp.float32
    )
    return jnp.swapaxes(peaks[..., 0], 1, 2), jnp.swapaxes(totals, 1, 2), accum


def local(
    queries,
    tree_cache,
    tree_mask,
    dest_group,
    accepted_path,
    prompt_cache,
    first_len,
    spill_cache,
    spill_len,
    out_weight,
):
    req_here = queries.shape[0]
    local_cols = queries.shape[2]
    heads_here = local_cols // HD
    groups = lax.axis_size("rep")
    per_group = max(2, (req_here + groups - 1) // groups)
    n_slots = groups * per_group
    positions = jnp.arange(PCAP, dtype=jnp.int32)
    live_flag = (positions < spill_len[0]).astype(jnp.bfloat16)
    partner_cache, partner_flag = swapped((spill_cache, live_flag), "rep", 0)

    target = dest_group[:, 0]
    same_target = target[:, None] == target[None, :]
    earlier = jnp.arange(req_here)[None, :] < jnp.arange(req_here)[:, None]
    rank_index = jnp.sum(jnp.logical_and(same_target, earlier), axis=1)
    slot_index = target * per_group + rank_index
    selector = (jnp.arange(n_slots, dtype=jnp.int32)[:, None] == slot_index[None, :]).astype(
        jnp.bfloat16
    )
    outbound = jnp.einsum(
        "sr,rtc->stc", selector, queries, preferred_element_type=jnp.float32
    ).astype(jnp.bfloat16)
    outbound = outbound.reshape(groups, per_group, TREE, local_cols)
    inbound = lax.all_to_all(outbound, "rep", split_axis=0, concat_axis=0, tiled=True)
    routed_rows = inbound.reshape(n_slots * TREE, local_cols)

    key_rows = jnp.concatenate([prompt_cache[0, 0], partner_cache[0, 0]], axis=0)
    value_rows = jnp.concatenate([prompt_cache[0, 1], partner_cache[0, 1]], axis=0)
    seen = jnp.concatenate([positions < first_len[0], partner_flag > 0.5], axis=0)
    normed, lse = prompt_attend(routed_rows, key_rows, value_rows, seen)

    back_out = lax.all_to_all(
        normed.reshape(groups, per_group, TREE, local_cols),
        "rep",
        split_axis=0,
        concat_axis=0,
        tiled=True,
    ).reshape(n_slots, TREE, local_cols)
    back_lse = lax.all_to_all(
        lse.reshape(groups, per_group, TREE, heads_here),
        "rep",
        split_axis=0,
        concat_axis=0,
        tiled=True,
    ).reshape(n_slots, TREE, heads_here)
    remote_out = split_heads(jnp.take(back_out, slot_index, axis=0)).astype(jnp.float32)
    remote_lse = jnp.take(back_lse, slot_index, axis=0)

    tree_max, tree_total, tree_accum = tree_attend(
        queries, tree_cache[:, 0], tree_cache[:, 1], tree_mask == 1
    )
    peaks = jnp.maximum(remote_lse, tree_max)
    factor_remote = jnp.exp(remote_lse - peaks)
    factor_tree = jnp.exp(tree_max - peaks)
    totals = factor_remote + tree_total * factor_tree
    accum = remote_out * factor_remote[..., None] + tree_accum * factor_tree[..., None]
    attn = (accum / totals[..., None]).reshape(req_here * TREE, local_cols).astype(jnp.bfloat16)
    summed = jnp.dot(
        lax.all_gather(attn, "tp", axis=1, tiled=True),
        out_weight,
        preferred_element_type=jnp.float32,
    )
    projected = summed.astype(jnp.bfloat16).reshape(req_here, TREE, out_weight.shape[1])
    accepted_cache = jnp.take_along_axis(tree_cache, accepted_path[:, None, :, None], axis=2)
    return (projected, accepted_cache)


def solution(mesh):
    return jax.shard_map(
        local,
        mesh=mesh,
        in_specs=(
            P("rep", None, "tp"),
            P("rep", None, None, "tp"),
            P("rep", None, None),
            P("rep", None),
            P("rep", None),
            P("rep", None, None, "tp"),
            P("rep"),
            P("rep", None, None, "tp"),
            P("rep"),
            P(None, "tp"),
        ),
        out_specs=(P("rep", None, "tp"), P("rep", None, None, "tp")),
        check_vma=False,
    )
```

```python
import math

import jax
import jax.numpy as jnp
from jax import lax
from jax.experimental import pallas as pl
from jax.experimental.pallas import tpu as pltpu
from jax.sharding import PartitionSpec as P

MESH = pl.DeviceIdType.MESH

HD = 128
TREE = 48
PCAP = 152


NEG_FILL = -1e30


def swapped(value, axis, apart):
    mask = 2**apart
    pairs = [(source, source ^ mask) for source in range(lax.axis_size(axis))]
    return lax.ppermute(value, axis, pairs)


def exchange_kernel(n, count, *refs):
    sources = refs[:count]
    targets = refs[count : 2 * count]
    send_sem, recv_sem, local_sem = refs[2 * count :]
    me = lax.axis_index("rep")
    barrier = pltpu.get_barrier_semaphore()
    for offset in range(1, n):
        pl.semaphore_signal(
            barrier, inc=1, device_id={"rep": lax.rem(me + offset, n)}, device_id_type=MESH
        )
    pl.semaphore_wait(barrier, n - 1)
    copies = []
    for index in range(count):
        local = pltpu.make_async_copy(
            sources[index].at[me], targets[index].at[me], local_sem.at[index]
        )
        local.start()
        copies.append(local)
        for offset in range(1, n):
            peer = lax.rem(me + offset, n)
            remote = pltpu.make_async_remote_copy(
                src_ref=sources[index].at[peer],
                dst_ref=targets[index].at[me],
                send_sem=send_sem.at[index, offset],
                recv_sem=recv_sem.at[index, offset],
                device_id={"rep": peer},
                device_id_type=MESH,
            )
            remote.start()
            copies.append(remote)
    for copy in copies:
        copy.wait()


def exchange(arrays, tag):
    n = lax.axis_size("rep")
    count = len(arrays)
    return pl.pallas_call(
        lambda *refs: exchange_kernel(n, count, *refs),
        out_shape=[jax.ShapeDtypeStruct(a.shape, a.dtype) for a in arrays],
        in_specs=[pl.BlockSpec(memory_space=pl.ANY)] * count,
        out_specs=[pl.BlockSpec(memory_space=pl.ANY)] * count,
        scratch_shapes=[
            pltpu.SemaphoreType.DMA((count, n)),
            pltpu.SemaphoreType.DMA((count, n)),
            pltpu.SemaphoreType.DMA((count,)),
        ],
        compiler_params=pltpu.CompilerParams(collective_id=tag, has_side_effects=True),
    )(*arrays)


def split_heads(rows):
    return rows.reshape(rows.shape[:-1] + (rows.shape[-1] // HD, HD))


def prompt_attend(query_rows, key_rows, value_rows, seen):
    q = split_heads(query_rows)
    k = split_heads(key_rows)
    v = split_heads(value_rows)
    scores = jnp.einsum("qhd,khd->hqk", q, k, preferred_element_type=jnp.float32) * (
        1.0 / math.sqrt(HD)
    )
    scores = jnp.where(seen[None, None, :], scores, NEG_FILL)
    peaks = jnp.max(scores, axis=2, keepdims=True)
    raw = jnp.where(seen[None, None, :], jnp.exp(scores - peaks), 0.0)
    totals = jnp.sum(raw, axis=2)
    accum = jnp.einsum(
        "hqk,khd->qhd", raw.astype(jnp.bfloat16), v, preferred_element_type=jnp.float32
    )
    normed = accum / jnp.transpose(totals)[:, :, None]
    lse = jnp.transpose(peaks[:, :, 0] + jnp.log(totals))
    return normed.reshape(query_rows.shape).astype(jnp.bfloat16), lse


def tree_attend(queries, keys, values, seen):
    q = split_heads(queries)
    k = split_heads(keys)
    v = split_heads(values)
    scores = jnp.einsum("rthd,rshd->rhts", q, k, preferred_element_type=jnp.float32) * (
        1.0 / math.sqrt(HD)
    )
    scores = jnp.where(seen[:, None], scores, NEG_FILL)
    peaks = jnp.max(scores, axis=3, keepdims=True)
    raw = jnp.where(seen[:, None], jnp.exp(scores - peaks), 0.0)
    totals = jnp.sum(raw, axis=3)
    accum = jnp.einsum(
        "rhts,rshd->rthd", raw.astype(jnp.bfloat16), v, preferred_element_type=jnp.float32
    )
    return jnp.swapaxes(peaks[..., 0], 1, 2), jnp.swapaxes(totals, 1, 2), accum


def local(
    queries,
    tree_cache,
    tree_mask,
    dest_group,
    accepted_path,
    prompt_cache,
    first_len,
    spill_cache,
    spill_len,
    out_weight,
):
    req_here = queries.shape[0]
    local_cols = queries.shape[2]
    heads_here = local_cols // HD
    groups = lax.axis_size("rep")
    per_group = max(2, (req_here + groups - 1) // groups)
    n_slots = groups * per_group
    positions = jnp.arange(PCAP, dtype=jnp.int32)
    live_flag = (positions < spill_len[0]).astype(jnp.bfloat16)
    partner_cache, partner_flag = swapped((spill_cache, live_flag), "rep", 0)

    target = dest_group[:, 0]
    same_target = target[:, None] == target[None, :]
    earlier = jnp.arange(req_here)[None, :] < jnp.arange(req_here)[:, None]
    rank_index = jnp.sum(jnp.logical_and(same_target, earlier), axis=1)
    slot_index = target * per_group + rank_index
    selector = (jnp.arange(n_slots, dtype=jnp.int32)[:, None] == slot_index[None, :]).astype(
        jnp.bfloat16
    )
    outbound = jnp.einsum(
        "sr,rtc->stc", selector, queries, preferred_element_type=jnp.float32
    ).astype(jnp.bfloat16)
    outbound = outbound.reshape(groups, per_group, TREE, local_cols)
    (inbound,) = exchange([outbound], 0)
    routed_rows = inbound.reshape(n_slots * TREE, local_cols)

    key_rows = jnp.concatenate([prompt_cache[0, 0], partner_cache[0, 0]], axis=0)
    value_rows = jnp.concatenate([prompt_cache[0, 1], partner_cache[0, 1]], axis=0)
    seen = jnp.concatenate([positions < first_len[0], partner_flag > 0.5], axis=0)
    normed, lse = prompt_attend(routed_rows, key_rows, value_rows, seen)

    back_out, back_lse = exchange(
        [
            normed.reshape(groups, per_group, TREE, local_cols),
            lse.reshape(groups, per_group, TREE, heads_here),
        ],
        1,
    )
    back_out = back_out.reshape(n_slots, TREE, local_cols)
    back_lse = back_lse.reshape(n_slots, TREE, heads_here)
    remote_out = split_heads(jnp.take(back_out, slot_index, axis=0)).astype(jnp.float32)
    remote_lse = jnp.take(back_lse, slot_index, axis=0)

    tree_max, tree_total, tree_accum = tree_attend(
        queries, tree_cache[:, 0], tree_cache[:, 1], tree_mask == 1
    )
    peaks = jnp.maximum(remote_lse, tree_max)
    factor_remote = jnp.exp(remote_lse - peaks)
    factor_tree = jnp.exp(tree_max - peaks)
    totals = factor_remote + tree_total * factor_tree
    accum = remote_out * factor_remote[..., None] + tree_accum * factor_tree[..., None]
    attn = (accum / totals[..., None]).reshape(req_here * TREE, local_cols).astype(jnp.bfloat16)
    summed = jnp.dot(
        lax.all_gather(attn, "tp", axis=1, tiled=True),
        out_weight,
        preferred_element_type=jnp.float32,
    )
    projected = summed.astype(jnp.bfloat16).reshape(req_here, TREE, out_weight.shape[1])
    accepted_cache = jnp.take_along_axis(tree_cache, accepted_path[:, None, :, None], axis=2)
    return (projected, accepted_cache)


def solution(mesh):
    return jax.shard_map(
        local,
        mesh=mesh,
        in_specs=(
            P("rep", None, "tp"),
            P("rep", None, None, "tp"),
            P("rep", None, None),
            P("rep", None),
            P("rep", None),
            P("rep", None, None, "tp"),
            P("rep"),
            P("rep", None, None, "tp"),
            P("rep"),
            P(None, "tp"),
        ),
        out_specs=(P("rep", None, "tp"), P("rep", None, None, "tp")),
        check_vma=False,
    )
```

```python
import math

import jax
import jax.numpy as jnp
from jax import lax
from jax.experimental import pallas as pl
from jax.experimental.pallas import tpu as pltpu
from jax.sharding import PartitionSpec as P

MESH = pl.DeviceIdType.MESH

HD = 128
TREE = 48
PCAP = 152


NEG_FILL = -1e30


def swapped(value, axis, apart):
    mask = 2**apart
    pairs = [(source, source ^ mask) for source in range(lax.axis_size(axis))]
    return lax.ppermute(value, axis, pairs)


def exchange_kernel(n, count, *refs):
    sources = refs[:count]
    targets = refs[count : 2 * count]
    send_sem, recv_sem, local_sem = refs[2 * count :]
    me = lax.axis_index("rep")
    barrier = pltpu.get_barrier_semaphore()
    for offset in range(1, n):
        pl.semaphore_signal(
            barrier, inc=1, device_id={"rep": lax.rem(me + offset, n)}, device_id_type=MESH
        )
    pl.semaphore_wait(barrier, n - 1)
    copies = []
    for index in range(count):
        local = pltpu.make_async_copy(
            sources[index].at[me], targets[index].at[me], local_sem.at[index]
        )
        local.start()
        copies.append(local)
        for offset in range(1, n):
            peer = lax.rem(me + offset, n)
            remote = pltpu.make_async_remote_copy(
                src_ref=sources[index].at[peer],
                dst_ref=targets[index].at[me],
                send_sem=send_sem.at[index, offset],
                recv_sem=recv_sem.at[index, offset],
                device_id={"rep": peer},
                device_id_type=MESH,
            )
            remote.start()
            copies.append(remote)
    for copy in copies:
        copy.wait()


def exchange(arrays, tag):
    n = lax.axis_size("rep")
    count = len(arrays)
    return pl.pallas_call(
        lambda *refs: exchange_kernel(n, count, *refs),
        out_shape=[jax.ShapeDtypeStruct(a.shape, a.dtype) for a in arrays],
        in_specs=[pl.BlockSpec(memory_space=pl.ANY)] * count,
        out_specs=[pl.BlockSpec(memory_space=pl.ANY)] * count,
        scratch_shapes=[
            pltpu.SemaphoreType.DMA((count, n)),
            pltpu.SemaphoreType.DMA((count, n)),
            pltpu.SemaphoreType.DMA((count,)),
        ],
        compiler_params=pltpu.CompilerParams(collective_id=tag, has_side_effects=True),
    )(*arrays)


def split_heads(rows):
    return rows.reshape(rows.shape[:-1] + (rows.shape[-1] // HD, HD))


def prompt_attend(query_rows, key_rows, value_rows, seen):
    q = split_heads(query_rows)
    k = split_heads(key_rows)
    v = split_heads(value_rows)
    scores = jnp.einsum("qhd,khd->hqk", q, k, preferred_element_type=jnp.float32) * (
        1.0 / math.sqrt(HD)
    )
    scores = jnp.where(seen[None, None, :], scores, NEG_FILL)
    peaks = jnp.max(scores, axis=2, keepdims=True)
    raw = jnp.where(seen[None, None, :], jnp.exp(scores - peaks), 0.0)
    totals = jnp.sum(raw, axis=2)
    accum = jnp.einsum(
        "hqk,khd->qhd", raw.astype(jnp.bfloat16), v, preferred_element_type=jnp.float32
    )
    normed = accum / jnp.transpose(totals)[:, :, None]
    lse = jnp.transpose(peaks[:, :, 0] + jnp.log(totals))
    return normed.reshape(query_rows.shape).astype(jnp.bfloat16), lse


def tree_attend(queries, keys, values, seen):
    q = split_heads(queries)
    k = split_heads(keys)
    v = split_heads(values)
    scores = jnp.einsum("rthd,rshd->rhts", q, k, preferred_element_type=jnp.float32) * (
        1.0 / math.sqrt(HD)
    )
    scores = jnp.where(seen[:, None], scores, NEG_FILL)
    peaks = jnp.max(scores, axis=3, keepdims=True)
    raw = jnp.where(seen[:, None], jnp.exp(scores - peaks), 0.0)
    totals = jnp.sum(raw, axis=3)
    accum = jnp.einsum(
        "rhts,rshd->rthd", raw.astype(jnp.bfloat16), v, preferred_element_type=jnp.float32
    )
    return jnp.swapaxes(peaks[..., 0], 1, 2), jnp.swapaxes(totals, 1, 2), accum


def local(
    queries,
    tree_cache,
    tree_mask,
    dest_group,
    accepted_path,
    prompt_cache,
    first_len,
    spill_cache,
    spill_len,
    out_weight,
):
    req_here = queries.shape[0]
    local_cols = queries.shape[2]
    heads_here = local_cols // HD
    groups = lax.axis_size("rep")
    per_group = max(2, (req_here + groups - 1) // groups)
    n_slots = groups * per_group
    positions = jnp.arange(PCAP, dtype=jnp.int32)
    live_flag = (positions < spill_len[0]).astype(jnp.bfloat16)
    partner_cache, partner_flag = swapped((spill_cache, live_flag), "rep", 0)

    target = dest_group[:, 0]
    same_target = target[:, None] == target[None, :]
    earlier = jnp.arange(req_here)[None, :] < jnp.arange(req_here)[:, None]
    rank_index = jnp.sum(jnp.logical_and(same_target, earlier), axis=1)
    slot_index = target * per_group + rank_index
    selector = (jnp.arange(n_slots, dtype=jnp.int32)[:, None] == slot_index[None, :]).astype(
        jnp.bfloat16
    )
    outbound = jnp.einsum(
        "sr,rtc->stc", selector, queries, preferred_element_type=jnp.float32
    ).astype(jnp.bfloat16)
    outbound = outbound.reshape(groups, per_group, TREE, local_cols)
    (inbound,) = exchange([outbound], 0)
    routed_rows = inbound.reshape(n_slots * TREE, local_cols)

    key_rows = jnp.concatenate([prompt_cache[0, 0], partner_cache[0, 0]], axis=0)
    value_rows = jnp.concatenate([prompt_cache[0, 1], partner_cache[0, 1]], axis=0)
    seen = jnp.concatenate([positions < first_len[0], partner_flag > 0.5], axis=0)
    normed, lse = prompt_attend(routed_rows, key_rows, value_rows, seen)

    lse_width = per_group * TREE * heads_here
    lse_tile = -(-lse_width // 1024) * 1024
    lse_block = jnp.pad(lse.reshape(groups, lse_width), ((0, 0), (0, lse_tile - lse_width)))
    back_out, back_lse = exchange(
        [
            normed.reshape(groups, per_group, TREE, local_cols),
            lse_block.reshape(groups, lse_tile // 128, 128),
        ],
        1,
    )
    back_out = back_out.reshape(n_slots, TREE, local_cols)
    back_lse = back_lse.reshape(groups, lse_tile)[:, :lse_width].reshape(n_slots, TREE, heads_here)
    remote_out = split_heads(jnp.take(back_out, slot_index, axis=0)).astype(jnp.float32)
    remote_lse = jnp.take(back_lse, slot_index, axis=0)

    tree_max, tree_total, tree_accum = tree_attend(
        queries, tree_cache[:, 0], tree_cache[:, 1], tree_mask == 1
    )
    peaks = jnp.maximum(remote_lse, tree_max)
    factor_remote = jnp.exp(remote_lse - peaks)
    factor_tree = jnp.exp(tree_max - peaks)
    totals = factor_remote + tree_total * factor_tree
    accum = remote_out * factor_remote[..., None] + tree_accum * factor_tree[..., None]
    attn = (accum / totals[..., None]).reshape(req_here * TREE, local_cols).astype(jnp.bfloat16)
    summed = jnp.dot(
        lax.all_gather(attn, "tp", axis=1, tiled=True),
        out_weight,
        preferred_element_type=jnp.float32,
    )
    projected = summed.astype(jnp.bfloat16).reshape(req_here, TREE, out_weight.shape[1])
    accepted_cache = jnp.take_along_axis(tree_cache, accepted_path[:, None, :, None], axis=2)
    return (projected, accepted_cache)


def solution(mesh):
    return jax.shard_map(
        local,
        mesh=mesh,
        in_specs=(
            P("rep", None, "tp"),
            P("rep", None, None, "tp"),
            P("rep", None, None),
            P("rep", None),
            P("rep", None),
            P("rep", None, None, "tp"),
            P("rep"),
            P("rep", None, None, "tp"),
            P("rep"),
            P(None, "tp"),
        ),
        out_specs=(P("rep", None, "tp"), P("rep", None, None, "tp")),
        check_vma=False,
    )
```

```python
import math

import jax
import jax.numpy as jnp
from jax import lax
from jax.experimental import pallas as pl
from jax.experimental.pallas import tpu as pltpu
from jax.sharding import PartitionSpec as P

MESH = pl.DeviceIdType.MESH

HD = 128
TREE = 48
PCAP = 152


NEG_FILL = -1e30


def swapped(value, axis, apart):
    mask = 2**apart
    pairs = [(source, source ^ mask) for source in range(lax.axis_size(axis))]
    return lax.ppermute(value, axis, pairs)


def exchange_kernel(n, count, *refs):
    sources = refs[:count]
    targets = refs[count : 2 * count]
    send_sem, recv_sem, local_sem = refs[2 * count :]
    me = lax.axis_index("rep")
    barrier = pltpu.get_barrier_semaphore()
    for offset in range(1, n):
        pl.semaphore_signal(
            barrier, inc=1, device_id={"rep": lax.rem(me + offset, n)}, device_id_type=MESH
        )
    pl.semaphore_wait(barrier, n - 1)
    copies = []
    for index in range(count):
        local = pltpu.make_async_copy(
            sources[index].at[me], targets[index].at[me], local_sem.at[index]
        )
        local.start()
        copies.append(local)
        for offset in range(1, n):
            peer = lax.rem(me + offset, n)
            remote = pltpu.make_async_remote_copy(
                src_ref=sources[index].at[peer],
                dst_ref=targets[index].at[me],
                send_sem=send_sem.at[index, offset],
                recv_sem=recv_sem.at[index, offset],
                device_id={"rep": peer},
                device_id_type=MESH,
            )
            remote.start()
            copies.append(remote)
    for copy in copies:
        copy.wait()


def exchange(arrays, tag):
    n = lax.axis_size("rep")
    count = len(arrays)
    return pl.pallas_call(
        lambda *refs: exchange_kernel(n, count, *refs),
        out_shape=[jax.ShapeDtypeStruct(a.shape, a.dtype) for a in arrays],
        in_specs=[pl.BlockSpec(memory_space=pl.ANY)] * count,
        out_specs=[pl.BlockSpec(memory_space=pl.ANY)] * count,
        scratch_shapes=[
            pltpu.SemaphoreType.DMA((count, n)),
            pltpu.SemaphoreType.DMA((count, n)),
            pltpu.SemaphoreType.DMA((count,)),
        ],
        compiler_params=pltpu.CompilerParams(collective_id=tag, has_side_effects=True),
    )(*arrays)


def split_heads(rows):
    return rows.reshape(rows.shape[:-1] + (rows.shape[-1] // HD, HD))


def prompt_kernel(q_ref, k_ref, v_ref, seen_ref, o_ref, lse_ref):
    rows = q_ref.shape[0]
    heads = q_ref.shape[1] // HD
    visible = seen_ref[...] > 0.5
    column = lax.broadcasted_iota(jnp.int32, (rows, 128), 1)
    lse_cols = jnp.zeros((rows, 128), jnp.float32)
    for head in range(heads):
        cols = slice(head * HD, (head + 1) * HD)
        scores = lax.dot_general(
            q_ref[:, cols],
            k_ref[:, cols],
            (((1,), (1,)), ((), ())),
            preferred_element_type=jnp.float32,
        ) * (1.0 / math.sqrt(HD))
        scores = jnp.where(visible, scores, NEG_FILL)
        peaks = jnp.max(scores, axis=1, keepdims=True)
        raw = jnp.where(visible, jnp.exp(scores - peaks), 0.0)
        totals = jnp.sum(raw, axis=1, keepdims=True)
        accum = jnp.dot(raw.astype(jnp.bfloat16), v_ref[:, cols], preferred_element_type=jnp.float32)
        o_ref[:, cols] = (accum / totals).astype(o_ref.dtype)
        lse_cols = jnp.where(column == head, peaks + jnp.log(totals), lse_cols)
    lse_ref[...] = jnp.transpose(lse_cols)[0:8, :]


def prompt_attend(query_rows, key_rows, value_rows, seen):
    n_rows, cols = query_rows.shape
    n_keys = key_rows.shape[0]
    padded = -(-n_keys // 128) * 128
    key_rows = jnp.pad(key_rows, ((0, padded - n_keys), (0, 0)))
    value_rows = jnp.pad(value_rows, ((0, padded - n_keys), (0, 0)))
    seen_row = jnp.pad(seen.astype(jnp.float32), (0, padded - n_keys)).reshape(1, padded)
    block = 384
    return pl.pallas_call(
        prompt_kernel,
        out_shape=[
            jax.ShapeDtypeStruct((n_rows, cols), jnp.bfloat16),
            jax.ShapeDtypeStruct((8, n_rows), jnp.float32),
        ],
        grid=(n_rows // block,),
        in_specs=[
            pl.BlockSpec((block, cols), lambda i: (i, 0)),
            pl.BlockSpec((padded, cols), lambda i: (0, 0)),
            pl.BlockSpec((padded, cols), lambda i: (0, 0)),
            pl.BlockSpec((1, padded), lambda i: (0, 0)),
        ],
        out_specs=[
            pl.BlockSpec((block, cols), lambda i: (i, 0)),
            pl.BlockSpec((8, block), lambda i: (0, i)),
        ],
    )(query_rows, key_rows, value_rows, seen_row)


def tree_attend(queries, keys, values, seen):
    q = split_heads(queries)
    k = split_heads(keys)
    v = split_heads(values)
    scores = jnp.einsum("rthd,rshd->rhts", q, k, preferred_element_type=jnp.float32) * (
        1.0 / math.sqrt(HD)
    )
    scores = jnp.where(seen[:, None], scores, NEG_FILL)
    peaks = jnp.max(scores, axis=3, keepdims=True)
    raw = jnp.where(seen[:, None], jnp.exp(scores - peaks), 0.0)
    totals = jnp.sum(raw, axis=3)
    accum = jnp.einsum(
        "rhts,rshd->rthd", raw.astype(jnp.bfloat16), v, preferred_element_type=jnp.float32
    )
    return jnp.swapaxes(peaks[..., 0], 1, 2), jnp.swapaxes(totals, 1, 2), accum


def local(
    queries,
    tree_cache,
    tree_mask,
    dest_group,
    accepted_path,
    prompt_cache,
    first_len,
    spill_cache,
    spill_len,
    out_weight,
):
    req_here = queries.shape[0]
    local_cols = queries.shape[2]
    heads_here = local_cols // HD
    groups = lax.axis_size("rep")
    per_group = max(2, (req_here + groups - 1) // groups)
    n_slots = groups * per_group
    positions = jnp.arange(PCAP, dtype=jnp.int32)
    live_flag = (positions < spill_len[0]).astype(jnp.bfloat16)
    partner_cache, partner_flag = swapped((spill_cache, live_flag), "rep", 0)

    target = dest_group[:, 0]
    same_target = target[:, None] == target[None, :]
    earlier = jnp.arange(req_here)[None, :] < jnp.arange(req_here)[:, None]
    rank_index = jnp.sum(jnp.logical_and(same_target, earlier), axis=1)
    slot_index = target * per_group + rank_index
    selector = (jnp.arange(n_slots, dtype=jnp.int32)[:, None] == slot_index[None, :]).astype(
        jnp.bfloat16
    )
    outbound = jnp.einsum(
        "sr,rtc->stc", selector, queries, preferred_element_type=jnp.float32
    ).astype(jnp.bfloat16)
    outbound = outbound.reshape(groups, per_group, TREE, local_cols)
    (inbound,) = exchange([outbound], 0)
    routed_rows = inbound.reshape(n_slots * TREE, local_cols)

    key_rows = jnp.concatenate([prompt_cache[0, 0], partner_cache[0, 0]], axis=0)
    value_rows = jnp.concatenate([prompt_cache[0, 1], partner_cache[0, 1]], axis=0)
    seen = jnp.concatenate([positions < first_len[0], partner_flag > 0.5], axis=0)
    normed, lse = prompt_attend(routed_rows, key_rows, value_rows, seen)

    lse_width = per_group * TREE * heads_here
    lse_tile = -(-lse_width // 1024) * 1024
    lse = jnp.swapaxes(lse[:heads_here].reshape(heads_here, groups, per_group * TREE), 0, 1)
    lse_block = jnp.pad(lse.reshape(groups, lse_width), ((0, 0), (0, lse_tile - lse_width)))
    back_out, back_lse = exchange(
        [
            normed.reshape(groups, per_group, TREE, local_cols),
            lse_block.reshape(groups, lse_tile // 128, 128),
        ],
        1,
    )
    back_out = back_out.reshape(n_slots, TREE, local_cols)
    back_lse = back_lse.reshape(groups, lse_tile)[:, :lse_width]
    back_lse = jnp.moveaxis(back_lse.reshape(groups, heads_here, per_group, TREE), 1, 3)
    back_lse = back_lse.reshape(n_slots, TREE, heads_here)
    remote_out = split_heads(jnp.take(back_out, slot_index, axis=0)).astype(jnp.float32)
    remote_lse = jnp.take(back_lse, slot_index, axis=0)

    tree_max, tree_total, tree_accum = tree_attend(
        queries, tree_cache[:, 0], tree_cache[:, 1], tree_mask == 1
    )
    peaks = jnp.maximum(remote_lse, tree_max)
    factor_remote = jnp.exp(remote_lse - peaks)
    factor_tree = jnp.exp(tree_max - peaks)
    totals = factor_remote + tree_total * factor_tree
    accum = remote_out * factor_remote[..., None] + tree_accum * factor_tree[..., None]
    attn = (accum / totals[..., None]).reshape(req_here * TREE, local_cols).astype(jnp.bfloat16)
    summed = jnp.dot(
        lax.all_gather(attn, "tp", axis=1, tiled=True),
        out_weight,
        preferred_element_type=jnp.float32,
    )
    projected = summed.astype(jnp.bfloat16).reshape(req_here, TREE, out_weight.shape[1])
    accepted_cache = jnp.take_along_axis(tree_cache, accepted_path[:, None, :, None], axis=2)
    return (projected, accepted_cache)


def solution(mesh):
    return jax.shard_map(
        local,
        mesh=mesh,
        in_specs=(
            P("rep", None, "tp"),
            P("rep", None, None, "tp"),
            P("rep", None, None),
            P("rep", None),
            P("rep", None),
            P("rep", None, None, "tp"),
            P("rep"),
            P("rep", None, None, "tp"),
            P("rep"),
            P(None, "tp"),
        ),
        out_specs=(P("rep", None, "tp"), P("rep", None, None, "tp")),
        check_vma=False,
    )
```

```python
import math

import jax
import jax.numpy as jnp
from jax import lax
from jax.experimental import pallas as pl
from jax.experimental.pallas import tpu as pltpu
from jax.sharding import PartitionSpec as P

MESH = pl.DeviceIdType.MESH

HD = 128
TREE = 48
PCAP = 152


NEG_FILL = -1e30


def swapped(value, axis, apart):
    mask = 2**apart
    pairs = [(source, source ^ mask) for source in range(lax.axis_size(axis))]
    return lax.ppermute(value, axis, pairs)


def exchange_kernel(n, count, extra, *refs):
    sources = refs[:count]
    targets = refs[count + extra : 2 * count + extra]
    send_sem, recv_sem, local_sem = refs[2 * count + extra :]
    me = lax.axis_index("rep")
    barrier = pltpu.get_barrier_semaphore()
    for offset in range(1, n):
        pl.semaphore_signal(
            barrier, inc=1, device_id={"rep": lax.rem(me + offset, n)}, device_id_type=MESH
        )
    pl.semaphore_wait(barrier, n - 1)
    copies = []
    for index in range(count):
        local = pltpu.make_async_copy(
            sources[index].at[me], targets[index].at[me], local_sem.at[index]
        )
        local.start()
        copies.append(local)
        for offset in range(1, n):
            peer = lax.rem(me + offset, n)
            remote = pltpu.make_async_remote_copy(
                src_ref=sources[index].at[peer],
                dst_ref=targets[index].at[me],
                send_sem=send_sem.at[index, offset],
                recv_sem=recv_sem.at[index, offset],
                device_id={"rep": peer},
                device_id_type=MESH,
            )
            remote.start()
            copies.append(remote)
    for copy in copies:
        copy.wait()


def exchange(arrays, tag, after=()):
    n = lax.axis_size("rep")
    count = len(arrays)
    extra = len(after)
    return pl.pallas_call(
        lambda *refs: exchange_kernel(n, count, extra, *refs),
        out_shape=[jax.ShapeDtypeStruct(a.shape, a.dtype) for a in arrays],
        in_specs=[pl.BlockSpec(memory_space=pl.ANY)] * (count + extra),
        out_specs=[pl.BlockSpec(memory_space=pl.ANY)] * count,
        scratch_shapes=[
            pltpu.SemaphoreType.DMA((count, n)),
            pltpu.SemaphoreType.DMA((count, n)),
            pltpu.SemaphoreType.DMA((count,)),
        ],
        compiler_params=pltpu.CompilerParams(collective_id=tag, has_side_effects=True),
    )(*arrays, *after)


def split_heads(rows):
    return rows.reshape(rows.shape[:-1] + (rows.shape[-1] // HD, HD))


def prompt_kernel(q_ref, k_ref, v_ref, seen_ref, o_ref, lse_ref):
    rows = q_ref.shape[0]
    heads = q_ref.shape[1] // HD
    visible = seen_ref[...] > 0.5
    column = lax.broadcasted_iota(jnp.int32, (rows, 128), 1)
    lse_cols = jnp.zeros((rows, 128), jnp.float32)
    for head in range(heads):
        cols = slice(head * HD, (head + 1) * HD)
        scores = lax.dot_general(
            q_ref[:, cols],
            k_ref[:, cols],
            (((1,), (1,)), ((), ())),
            preferred_element_type=jnp.float32,
        ) * (1.0 / math.sqrt(HD))
        scores = jnp.where(visible, scores, NEG_FILL)
        peaks = jnp.max(scores, axis=1, keepdims=True)
        raw = jnp.where(visible, jnp.exp(scores - peaks), 0.0)
        totals = jnp.sum(raw, axis=1, keepdims=True)
        accum = jnp.dot(raw.astype(jnp.bfloat16), v_ref[:, cols], preferred_element_type=jnp.float32)
        o_ref[head] = (accum / totals).astype(o_ref.dtype)
        lse_cols = jnp.where(column == head, peaks + jnp.log(totals), lse_cols)
    lse_ref[...] = jnp.transpose(lse_cols)[0:8, :]


def prompt_attend(query_rows, key_rows, value_rows, seen):
    n_rows, cols = query_rows.shape
    n_keys = key_rows.shape[0]
    padded = -(-n_keys // 128) * 128
    key_rows = jnp.pad(key_rows, ((0, padded - n_keys), (0, 0)))
    value_rows = jnp.pad(value_rows, ((0, padded - n_keys), (0, 0)))
    seen_row = jnp.pad(seen.astype(jnp.float32), (0, padded - n_keys)).reshape(1, padded)
    block = 384
    return pl.pallas_call(
        prompt_kernel,
        out_shape=[
            jax.ShapeDtypeStruct((cols // HD, n_rows, HD), jnp.bfloat16),
            jax.ShapeDtypeStruct((8, n_rows), jnp.float32),
        ],
        grid=(n_rows // block,),
        in_specs=[
            pl.BlockSpec((block, cols), lambda i: (i, 0)),
            pl.BlockSpec((padded, cols), lambda i: (0, 0)),
            pl.BlockSpec((padded, cols), lambda i: (0, 0)),
            pl.BlockSpec((1, padded), lambda i: (0, 0)),
        ],
        out_specs=[
            pl.BlockSpec((cols // HD, block, HD), lambda i: (0, i, 0)),
            pl.BlockSpec((8, block), lambda i: (0, i)),
        ],
    )(query_rows, key_rows, value_rows, seen_row)


def tree_attend(queries, keys, values, seen):
    q = split_heads(queries)
    k = split_heads(keys)
    v = split_heads(values)
    scores = jnp.einsum("rthd,rshd->rhts", q, k, preferred_element_type=jnp.float32) * (
        1.0 / math.sqrt(HD)
    )
    scores = jnp.where(seen[:, None], scores, NEG_FILL)
    peaks = jnp.max(scores, axis=3, keepdims=True)
    raw = jnp.where(seen[:, None], jnp.exp(scores - peaks), 0.0)
    totals = jnp.sum(raw, axis=3)
    accum = jnp.einsum(
        "rhts,rshd->rthd", raw.astype(jnp.bfloat16), v, preferred_element_type=jnp.float32
    )
    return jnp.swapaxes(peaks[..., 0], 1, 2), jnp.swapaxes(totals, 1, 2), accum


def local(
    queries,
    tree_cache,
    tree_mask,
    dest_group,
    accepted_path,
    prompt_cache,
    first_len,
    spill_cache,
    spill_len,
    out_weight,
):
    req_here = queries.shape[0]
    local_cols = queries.shape[2]
    heads_here = local_cols // HD
    groups = lax.axis_size("rep")
    per_group = max(2, (req_here + groups - 1) // groups)
    n_slots = groups * per_group
    positions = jnp.arange(PCAP, dtype=jnp.int32)
    live_flag = (positions < spill_len[0]).astype(jnp.bfloat16)
    partner_cache, partner_flag = swapped((spill_cache, live_flag), "rep", 0)

    target = dest_group[:, 0]
    same_target = target[:, None] == target[None, :]
    earlier = jnp.arange(req_here)[None, :] < jnp.arange(req_here)[:, None]
    rank_index = jnp.sum(jnp.logical_and(same_target, earlier), axis=1)
    slot_index = target * per_group + rank_index
    selector = (jnp.arange(n_slots, dtype=jnp.int32)[:, None] == slot_index[None, :]).astype(
        jnp.bfloat16
    )
    outbound = jnp.einsum(
        "sr,rtc->stc", selector, queries, preferred_element_type=jnp.float32
    ).astype(jnp.bfloat16)
    outbound = outbound.reshape(groups, per_group, TREE, local_cols)
    (inbound,) = exchange([outbound], 0)
    routed_rows = inbound.reshape(n_slots * TREE, local_cols)

    key_rows = jnp.concatenate([prompt_cache[0, 0], partner_cache[0, 0]], axis=0)
    value_rows = jnp.concatenate([prompt_cache[0, 1], partner_cache[0, 1]], axis=0)
    seen = jnp.concatenate([positions < first_len[0], partner_flag > 0.5], axis=0)
    normed, lse = prompt_attend(routed_rows, key_rows, value_rows, seen)

    lse_width = per_group * TREE
    lse_tile = -(-lse_width // 1024) * 1024
    lse = lse[:heads_here].reshape(heads_here, groups, lse_width)
    lse = jnp.pad(lse, ((0, 0), (0, 0), (0, lse_tile - lse_width)))
    lse = lse.reshape(heads_here, groups, lse_tile // 128, 128)

    tree_max, tree_total, tree_accum = tree_attend(
        queries, tree_cache[:, 0], tree_cache[:, 1], tree_mask == 1
    )
    tp_size = lax.axis_size("tp")
    weight_rows = out_weight.reshape(tp_size, heads_here, HD, out_weight.shape[1])
    summed = None
    previous = ()
    for head in range(heads_here):
        back_out, back_lse = exchange(
            [normed[head].reshape(groups, per_group, TREE, HD), lse[head]], 1 + head, previous
        )
        back_lse = back_lse.reshape(groups, lse_tile)[:, :lse_width].reshape(n_slots, TREE)
        remote_out = jnp.take(back_out.reshape(n_slots, TREE, HD), slot_index, axis=0)
        remote_lse = jnp.take(back_lse, slot_index, axis=0)
        peaks = jnp.maximum(remote_lse, tree_max[..., head])
        factor_remote = jnp.exp(remote_lse - peaks)
        factor_tree = jnp.exp(tree_max[..., head] - peaks)
        totals = factor_remote + tree_total[..., head] * factor_tree
        accum = (
            remote_out.astype(jnp.float32) * factor_remote[..., None]
            + tree_accum[:, :, head] * factor_tree[..., None]
        )
        attn = (accum / totals[..., None]).reshape(req_here * TREE, HD).astype(jnp.bfloat16)
        previous = (attn,)
        part = jnp.dot(
            lax.all_gather(attn, "tp", axis=1, tiled=True),
            weight_rows[:, head].reshape(tp_size * HD, out_weight.shape[1]),
            preferred_element_type=jnp.float32,
        )
        summed = part if summed is None else summed + part
    projected = summed.astype(jnp.bfloat16).reshape(req_here, TREE, out_weight.shape[1])
    accepted_cache = jnp.take_along_axis(tree_cache, accepted_path[:, None, :, None], axis=2)
    return (projected, accepted_cache)


def solution(mesh):
    return jax.shard_map(
        local,
        mesh=mesh,
        in_specs=(
            P("rep", None, "tp"),
            P("rep", None, None, "tp"),
            P("rep", None, None),
            P("rep", None),
            P("rep", None),
            P("rep", None, None, "tp"),
            P("rep"),
            P("rep", None, None, "tp"),
            P("rep"),
            P(None, "tp"),
        ),
        out_specs=(P("rep", None, "tp"), P("rep", None, None, "tp")),
        check_vma=False,
    )
```

```python
import math

import jax
import jax.numpy as jnp
from jax import lax
from jax.experimental import pallas as pl
from jax.experimental.pallas import tpu as pltpu
from jax.sharding import PartitionSpec as P

MESH = pl.DeviceIdType.MESH

HD = 128
TREE = 48
PCAP = 152


NEG_FILL = -1e30


def swapped(value, axis, apart):
    mask = 2**apart
    pairs = [(source, source ^ mask) for source in range(lax.axis_size(axis))]
    return lax.ppermute(value, axis, pairs)


def exchange_kernel(n, count, *refs):
    sources = refs[:count]
    targets = refs[count : 2 * count]
    send_sem, recv_sem, local_sem = refs[2 * count :]
    me = lax.axis_index("rep")
    barrier = pltpu.get_barrier_semaphore()
    for offset in range(1, n):
        pl.semaphore_signal(
            barrier, inc=1, device_id={"rep": lax.rem(me + offset, n)}, device_id_type=MESH
        )
    pl.semaphore_wait(barrier, n - 1)
    copies = []
    for index in range(count):
        local = pltpu.make_async_copy(
            sources[index].at[me], targets[index].at[me], local_sem.at[index]
        )
        local.start()
        copies.append(local)
        for offset in range(1, n):
            peer = lax.rem(me + offset, n)
            remote = pltpu.make_async_remote_copy(
                src_ref=sources[index].at[peer],
                dst_ref=targets[index].at[me],
                send_sem=send_sem.at[index, offset],
                recv_sem=recv_sem.at[index, offset],
                device_id={"rep": peer},
                device_id_type=MESH,
            )
            remote.start()
            copies.append(remote)
    for copy in copies:
        copy.wait()


def exchange(arrays, tag):
    n = lax.axis_size("rep")
    count = len(arrays)
    return pl.pallas_call(
        lambda *refs: exchange_kernel(n, count, *refs),
        out_shape=[jax.ShapeDtypeStruct(a.shape, a.dtype) for a in arrays],
        in_specs=[pl.BlockSpec(memory_space=pl.ANY)] * count,
        out_specs=[pl.BlockSpec(memory_space=pl.ANY)] * count,
        scratch_shapes=[
            pltpu.SemaphoreType.DMA((count, n)),
            pltpu.SemaphoreType.DMA((count, n)),
            pltpu.SemaphoreType.DMA((count,)),
        ],
        compiler_params=pltpu.CompilerParams(collective_id=tag, has_side_effects=True),
    )(*arrays)


def gather_project_kernel(n_z, a_ref, w_ref, o_ref, slots, send_sem, recv_sem):
    me = lax.axis_index("tp")
    z = me // 2
    core = me % 2
    step_z = 1 - 2 * core
    ring_next = lax.rem(z + step_z + n_z, n_z) * 2 + core
    ring_prev = lax.rem(z - step_z + n_z, n_z) * 2 + core
    sibling = z * 2 + (1 - core)
    barrier = pltpu.get_barrier_semaphore()
    for peer in (ring_next, ring_prev, sibling):
        pl.semaphore_signal(barrier, inc=1, device_id={"tp": peer}, device_id_type=MESH)
    pl.semaphore_wait(barrier, 3)
    slots[me] = a_ref[...]

    def origin(step):
        return lax.rem(z - step * step_z + 2 * n_z, n_z) * 2 + core

    sends = []
    for step in range(n_z):
        slot = origin(step)
        if step == 0:
            source = a_ref
        else:
            source = slots.at[slot]
            pltpu.make_async_remote_copy(
                src_ref=slots.at[slot],
                dst_ref=slots.at[slot],
                send_sem=send_sem.at[0, step],
                recv_sem=recv_sem.at[slot],
                device_id={"tp": ring_prev},
                device_id_type=MESH,
            ).wait_recv()
        targets = [(1, sibling)] + ([(0, ring_next)] if step < n_z - 1 else [])
        for kind, peer in targets:
            copy = pltpu.make_async_remote_copy(
                src_ref=source,
                dst_ref=slots.at[slot],
                send_sem=send_sem.at[kind, step],
                recv_sem=recv_sem.at[slot],
                device_id={"tp": peer},
                device_id_type=MESH,
            )
            copy.start()
            sends.append(copy)
    for step in range(n_z):
        slot = lax.rem(z - step * step_z + 2 * n_z, n_z) * 2 + (1 - core)
        pltpu.make_async_remote_copy(
            src_ref=slots.at[slot],
            dst_ref=slots.at[slot],
            send_sem=send_sem.at[1, step],
            recv_sem=recv_sem.at[slot],
            device_id={"tp": sibling},
            device_id_type=MESH,
        ).wait_recv()
    for copy in sends:
        copy.wait_send()
    width = a_ref.shape[1]
    total = jnp.zeros(o_ref.shape, jnp.float32)
    for index in range(slots.shape[0]):
        total = total + jnp.dot(
            slots[index], w_ref[index * width : (index + 1) * width, :], preferred_element_type=jnp.float32
        )
    o_ref[...] = total.astype(o_ref.dtype)


def gather_project(attn, weight):
    tp_size = lax.axis_size("tp")
    rows, width = attn.shape
    return pl.pallas_call(
        lambda *refs: gather_project_kernel(tp_size // 2, *refs),
        out_shape=jax.ShapeDtypeStruct((rows, weight.shape[1]), jnp.bfloat16),
        in_specs=[pl.BlockSpec(memory_space=pltpu.VMEM)] * 2,
        out_specs=pl.BlockSpec(memory_space=pltpu.VMEM),
        scratch_shapes=[
            pltpu.VMEM((tp_size, rows, width), jnp.bfloat16),
            pltpu.SemaphoreType.DMA((2, tp_size // 2)),
            pltpu.SemaphoreType.DMA((tp_size,)),
        ],
        compiler_params=pltpu.CompilerParams(collective_id=3, has_side_effects=True),
    )(attn, weight)


def split_heads(rows):
    return rows.reshape(rows.shape[:-1] + (rows.shape[-1] // HD, HD))


def prompt_kernel(q_ref, k_ref, v_ref, seen_ref, o_ref, lse_ref):
    rows = q_ref.shape[0]
    heads = q_ref.shape[1] // HD
    visible = seen_ref[...] > 0.5
    column = lax.broadcasted_iota(jnp.int32, (rows, 128), 1)
    lse_cols = jnp.zeros((rows, 128), jnp.float32)
    for head in range(heads):
        cols = slice(head * HD, (head + 1) * HD)
        scores = lax.dot_general(
            q_ref[:, cols],
            k_ref[:, cols],
            (((1,), (1,)), ((), ())),
            preferred_element_type=jnp.float32,
        ) * (1.0 / math.sqrt(HD))
        scores = jnp.where(visible, scores, NEG_FILL)
        peaks = jnp.max(scores, axis=1, keepdims=True)
        raw = jnp.where(visible, jnp.exp(scores - peaks), 0.0)
        totals = jnp.sum(raw, axis=1, keepdims=True)
        accum = jnp.dot(raw.astype(jnp.bfloat16), v_ref[:, cols], preferred_element_type=jnp.float32)
        o_ref[:, cols] = (accum / totals).astype(o_ref.dtype)
        lse_cols = jnp.where(column == head, peaks + jnp.log(totals), lse_cols)
    lse_ref[...] = jnp.transpose(lse_cols)[0:8, :]


def prompt_attend(query_rows, key_rows, value_rows, seen):
    n_rows, cols = query_rows.shape
    n_keys = key_rows.shape[0]
    padded = -(-n_keys // 128) * 128
    key_rows = jnp.pad(key_rows, ((0, padded - n_keys), (0, 0)))
    value_rows = jnp.pad(value_rows, ((0, padded - n_keys), (0, 0)))
    seen_row = jnp.pad(seen.astype(jnp.float32), (0, padded - n_keys)).reshape(1, padded)
    block = 384
    return pl.pallas_call(
        prompt_kernel,
        out_shape=[
            jax.ShapeDtypeStruct((n_rows, cols), jnp.bfloat16),
            jax.ShapeDtypeStruct((8, n_rows), jnp.float32),
        ],
        grid=(n_rows // block,),
        in_specs=[
            pl.BlockSpec((block, cols), lambda i: (i, 0)),
            pl.BlockSpec((padded, cols), lambda i: (0, 0)),
            pl.BlockSpec((padded, cols), lambda i: (0, 0)),
            pl.BlockSpec((1, padded), lambda i: (0, 0)),
        ],
        out_specs=[
            pl.BlockSpec((block, cols), lambda i: (i, 0)),
            pl.BlockSpec((8, block), lambda i: (0, i)),
        ],
    )(query_rows, key_rows, value_rows, seen_row)


def tree_attend(queries, keys, values, seen):
    q = split_heads(queries)
    k = split_heads(keys)
    v = split_heads(values)
    scores = jnp.einsum("rthd,rshd->rhts", q, k, preferred_element_type=jnp.float32) * (
        1.0 / math.sqrt(HD)
    )
    scores = jnp.where(seen[:, None], scores, NEG_FILL)
    peaks = jnp.max(scores, axis=3, keepdims=True)
    raw = jnp.where(seen[:, None], jnp.exp(scores - peaks), 0.0)
    totals = jnp.sum(raw, axis=3)
    accum = jnp.einsum(
        "rhts,rshd->rthd", raw.astype(jnp.bfloat16), v, preferred_element_type=jnp.float32
    )
    return jnp.swapaxes(peaks[..., 0], 1, 2), jnp.swapaxes(totals, 1, 2), accum


def local(
    queries,
    tree_cache,
    tree_mask,
    dest_group,
    accepted_path,
    prompt_cache,
    first_len,
    spill_cache,
    spill_len,
    out_weight,
):
    req_here = queries.shape[0]
    local_cols = queries.shape[2]
    heads_here = local_cols // HD
    groups = lax.axis_size("rep")
    per_group = max(2, (req_here + groups - 1) // groups)
    n_slots = groups * per_group
    positions = jnp.arange(PCAP, dtype=jnp.int32)
    live_flag = (positions < spill_len[0]).astype(jnp.bfloat16)
    partner_cache, partner_flag = swapped((spill_cache, live_flag), "rep", 0)

    target = dest_group[:, 0]
    same_target = target[:, None] == target[None, :]
    earlier = jnp.arange(req_here)[None, :] < jnp.arange(req_here)[:, None]
    rank_index = jnp.sum(jnp.logical_and(same_target, earlier), axis=1)
    slot_index = target * per_group + rank_index
    selector = (jnp.arange(n_slots, dtype=jnp.int32)[:, None] == slot_index[None, :]).astype(
        jnp.bfloat16
    )
    outbound = jnp.einsum(
        "sr,rtc->stc", selector, queries, preferred_element_type=jnp.float32
    ).astype(jnp.bfloat16)
    outbound = outbound.reshape(groups, per_group, TREE, local_cols)
    (inbound,) = exchange([outbound], 0)
    routed_rows = inbound.reshape(n_slots * TREE, local_cols)

    key_rows = jnp.concatenate([prompt_cache[0, 0], partner_cache[0, 0]], axis=0)
    value_rows = jnp.concatenate([prompt_cache[0, 1], partner_cache[0, 1]], axis=0)
    seen = jnp.concatenate([positions < first_len[0], partner_flag > 0.5], axis=0)
    normed, lse = prompt_attend(routed_rows, key_rows, value_rows, seen)

    lse_width = per_group * TREE * heads_here
    lse_tile = -(-lse_width // 1024) * 1024
    lse = jnp.swapaxes(lse[:heads_here].reshape(heads_here, groups, per_group * TREE), 0, 1)
    lse_block = jnp.pad(lse.reshape(groups, lse_width), ((0, 0), (0, lse_tile - lse_width)))
    back_out, back_lse = exchange(
        [
            normed.reshape(groups, per_group, TREE, local_cols),
            lse_block.reshape(groups, lse_tile // 128, 128),
        ],
        1,
    )
    back_out = back_out.reshape(n_slots, TREE, local_cols)
    back_lse = back_lse.reshape(groups, lse_tile)[:, :lse_width]
    back_lse = jnp.moveaxis(back_lse.reshape(groups, heads_here, per_group, TREE), 1, 3)
    back_lse = back_lse.reshape(n_slots, TREE, heads_here)
    remote_out = split_heads(jnp.take(back_out, slot_index, axis=0)).astype(jnp.float32)
    remote_lse = jnp.take(back_lse, slot_index, axis=0)

    tree_max, tree_total, tree_accum = tree_attend(
        queries, tree_cache[:, 0], tree_cache[:, 1], tree_mask == 1
    )
    peaks = jnp.maximum(remote_lse, tree_max)
    factor_remote = jnp.exp(remote_lse - peaks)
    factor_tree = jnp.exp(tree_max - peaks)
    totals = factor_remote + tree_total * factor_tree
    accum = remote_out * factor_remote[..., None] + tree_accum * factor_tree[..., None]
    attn = (accum / totals[..., None]).reshape(req_here * TREE, local_cols).astype(jnp.bfloat16)
    projected = gather_project(attn, out_weight).reshape(req_here, TREE, out_weight.shape[1])
    accepted_cache = jnp.take_along_axis(tree_cache, accepted_path[:, None, :, None], axis=2)
    return (projected, accepted_cache)


def solution(mesh):
    return jax.shard_map(
        local,
        mesh=mesh,
        in_specs=(
            P("rep", None, "tp"),
            P("rep", None, None, "tp"),
            P("rep", None, None),
            P("rep", None),
            P("rep", None),
            P("rep", None, None, "tp"),
            P("rep"),
            P("rep", None, None, "tp"),
            P("rep"),
            P(None, "tp"),
        ),
        out_specs=(P("rep", None, "tp"), P("rep", None, None, "tp")),
        check_vma=False,
    )
```

```python
import math

import jax
import jax.numpy as jnp
from jax import lax
from jax.experimental import pallas as pl
from jax.experimental.pallas import tpu as pltpu
from jax.sharding import PartitionSpec as P

MESH = pl.DeviceIdType.MESH

HD = 128
TREE = 48
PCAP = 152


NEG_FILL = -1e30


def swapped(value, axis, apart):
    mask = 2**apart
    pairs = [(source, source ^ mask) for source in range(lax.axis_size(axis))]
    return lax.ppermute(value, axis, pairs)


def exchange_kernel(n, count, *refs):
    sources = refs[:count]
    targets = refs[count : 2 * count]
    send_sem, recv_sem, local_sem = refs[2 * count :]
    me = lax.axis_index("rep")
    barrier = pltpu.get_barrier_semaphore()
    for offset in range(1, n):
        pl.semaphore_signal(
            barrier, inc=1, device_id={"rep": lax.rem(me + offset, n)}, device_id_type=MESH
        )
    pl.semaphore_wait(barrier, n - 1)
    copies = []
    for index in range(count):
        local = pltpu.make_async_copy(
            sources[index].at[me], targets[index].at[me], local_sem.at[index]
        )
        local.start()
        copies.append(local)
        for offset in range(1, n):
            peer = lax.rem(me + offset, n)
            remote = pltpu.make_async_remote_copy(
                src_ref=sources[index].at[peer],
                dst_ref=targets[index].at[me],
                send_sem=send_sem.at[index, offset],
                recv_sem=recv_sem.at[index, offset],
                device_id={"rep": peer},
                device_id_type=MESH,
            )
            remote.start()
            copies.append(remote)
    for copy in copies:
        copy.wait()


def exchange(arrays, tag):
    n = lax.axis_size("rep")
    count = len(arrays)
    return pl.pallas_call(
        lambda *refs: exchange_kernel(n, count, *refs),
        out_shape=[jax.ShapeDtypeStruct(a.shape, a.dtype) for a in arrays],
        in_specs=[pl.BlockSpec(memory_space=pl.ANY)] * count,
        out_specs=[pl.BlockSpec(memory_space=pl.ANY)] * count,
        scratch_shapes=[
            pltpu.SemaphoreType.DMA((count, n)),
            pltpu.SemaphoreType.DMA((count, n)),
            pltpu.SemaphoreType.DMA((count,)),
        ],
        compiler_params=pltpu.CompilerParams(collective_id=tag, has_side_effects=True),
    )(*arrays)


def gather_project_kernel(n_z, a_ref, w_ref, o_ref, slots, send_sem, recv_sem):
    me = lax.axis_index("tp")
    z = me // 2
    core = me % 2
    up = lax.rem(z + 1, n_z) * 2 + core
    down = lax.rem(z + n_z - 1, n_z) * 2 + core
    sibling = z * 2 + (1 - core)
    barrier = pltpu.get_barrier_semaphore()
    for peer in (up, down, sibling):
        pl.semaphore_signal(barrier, inc=1, device_id={"tp": peer}, device_id_type=MESH)
    pl.semaphore_wait(barrier, 3)
    slots[me] = a_ref[...]
    chains = ((0, 1, up, down), (1, -1, down, up))

    def arrival(slot, half, sender):
        pltpu.make_async_remote_copy(
            src_ref=slots.at[slot, half],
            dst_ref=slots.at[slot, half],
            send_sem=send_sem.at[half, 0],
            recv_sem=recv_sem.at[slot, half],
            device_id={"tp": sender},
            device_id_type=MESH,
        ).wait_recv()

    sends = []
    for step in range(n_z):
        for half, direction, ahead, behind in chains:
            slot = lax.rem(z - step * direction + 2 * n_z, n_z) * 2 + core
            if step == 0:
                source = a_ref.at[half]
            else:
                arrival(slot, half, behind)
                source = slots.at[slot, half]
            targets = ([(half, ahead)] if step < n_z - 1 else []) + [(2 + half, sibling)]
            for kind, peer in targets:
                copy = pltpu.make_async_remote_copy(
                    src_ref=source,
                    dst_ref=slots.at[slot, half],
                    send_sem=send_sem.at[kind, step],
                    recv_sem=recv_sem.at[slot, half],
                    device_id={"tp": peer},
                    device_id_type=MESH,
                )
                copy.start()
                sends.append(copy)
    for step in range(n_z):
        for half, direction, ahead, behind in chains:
            slot = lax.rem(z - step * direction + 2 * n_z, n_z) * 2 + (1 - core)
            arrival(slot, half, sibling)
    for copy in sends:
        copy.wait_send()
    width = a_ref.shape[2]
    total = jnp.zeros(o_ref.shape, jnp.float32)
    for index in range(slots.shape[0]):
        for half in range(slots.shape[1]):
            row = (index * slots.shape[1] + half) * width
            total = total + jnp.dot(
                slots[index, half], w_ref[row : row + width, :], preferred_element_type=jnp.float32
            )
    o_ref[...] = total.astype(o_ref.dtype)


def gather_project(attn, weight):
    tp_size = lax.axis_size("tp")
    halves, rows, width = attn.shape
    return pl.pallas_call(
        lambda *refs: gather_project_kernel(tp_size // 2, *refs),
        out_shape=jax.ShapeDtypeStruct((rows, weight.shape[1]), jnp.bfloat16),
        in_specs=[pl.BlockSpec(memory_space=pltpu.VMEM)] * 2,
        out_specs=pl.BlockSpec(memory_space=pltpu.VMEM),
        scratch_shapes=[
            pltpu.VMEM((tp_size, halves, rows, width), jnp.bfloat16),
            pltpu.SemaphoreType.DMA((4, tp_size // 2)),
            pltpu.SemaphoreType.DMA((tp_size, halves)),
        ],
        compiler_params=pltpu.CompilerParams(collective_id=3, has_side_effects=True),
    )(attn, weight)


def split_heads(rows):
    return rows.reshape(rows.shape[:-1] + (rows.shape[-1] // HD, HD))


def prompt_kernel(q_ref, k_ref, v_ref, seen_ref, o_ref, lse_ref):
    rows = q_ref.shape[0]
    heads = q_ref.shape[1] // HD
    visible = seen_ref[...] > 0.5
    column = lax.broadcasted_iota(jnp.int32, (rows, 128), 1)
    lse_cols = jnp.zeros((rows, 128), jnp.float32)
    for head in range(heads):
        cols = slice(head * HD, (head + 1) * HD)
        scores = lax.dot_general(
            q_ref[:, cols],
            k_ref[:, cols],
            (((1,), (1,)), ((), ())),
            preferred_element_type=jnp.float32,
        ) * (1.0 / math.sqrt(HD))
        scores = jnp.where(visible, scores, NEG_FILL)
        peaks = jnp.max(scores, axis=1, keepdims=True)
        raw = jnp.where(visible, jnp.exp(scores - peaks), 0.0)
        totals = jnp.sum(raw, axis=1, keepdims=True)
        accum = jnp.dot(raw.astype(jnp.bfloat16), v_ref[:, cols], preferred_element_type=jnp.float32)
        o_ref[:, cols] = (accum / totals).astype(o_ref.dtype)
        lse_cols = jnp.where(column == head, peaks + jnp.log(totals), lse_cols)
    lse_ref[...] = jnp.transpose(lse_cols)[0:8, :]


def prompt_attend(query_rows, key_rows, value_rows, seen):
    n_rows, cols = query_rows.shape
    n_keys = key_rows.shape[0]
    padded = -(-n_keys // 128) * 128
    key_rows = jnp.pad(key_rows, ((0, padded - n_keys), (0, 0)))
    value_rows = jnp.pad(value_rows, ((0, padded - n_keys), (0, 0)))
    seen_row = jnp.pad(seen.astype(jnp.float32), (0, padded - n_keys)).reshape(1, padded)
    block = 384
    return pl.pallas_call(
        prompt_kernel,
        out_shape=[
            jax.ShapeDtypeStruct((n_rows, cols), jnp.bfloat16),
            jax.ShapeDtypeStruct((8, n_rows), jnp.float32),
        ],
        grid=(n_rows // block,),
        in_specs=[
            pl.BlockSpec((block, cols), lambda i: (i, 0)),
            pl.BlockSpec((padded, cols), lambda i: (0, 0)),
            pl.BlockSpec((padded, cols), lambda i: (0, 0)),
            pl.BlockSpec((1, padded), lambda i: (0, 0)),
        ],
        out_specs=[
            pl.BlockSpec((block, cols), lambda i: (i, 0)),
            pl.BlockSpec((8, block), lambda i: (0, i)),
        ],
    )(query_rows, key_rows, value_rows, seen_row)


def tree_attend(queries, keys, values, seen):
    q = split_heads(queries)
    k = split_heads(keys)
    v = split_heads(values)
    scores = jnp.einsum("rthd,rshd->rhts", q, k, preferred_element_type=jnp.float32) * (
        1.0 / math.sqrt(HD)
    )
    scores = jnp.where(seen[:, None], scores, NEG_FILL)
    peaks = jnp.max(scores, axis=3, keepdims=True)
    raw = jnp.where(seen[:, None], jnp.exp(scores - peaks), 0.0)
    totals = jnp.sum(raw, axis=3)
    accum = jnp.einsum(
        "rhts,rshd->rthd", raw.astype(jnp.bfloat16), v, preferred_element_type=jnp.float32
    )
    return jnp.swapaxes(peaks[..., 0], 1, 2), jnp.swapaxes(totals, 1, 2), accum


def local(
    queries,
    tree_cache,
    tree_mask,
    dest_group,
    accepted_path,
    prompt_cache,
    first_len,
    spill_cache,
    spill_len,
    out_weight,
):
    req_here = queries.shape[0]
    local_cols = queries.shape[2]
    heads_here = local_cols // HD
    groups = lax.axis_size("rep")
    per_group = max(2, (req_here + groups - 1) // groups)
    n_slots = groups * per_group
    positions = jnp.arange(PCAP, dtype=jnp.int32)
    live_flag = (positions < spill_len[0]).astype(jnp.bfloat16)
    partner_cache, partner_flag = swapped((spill_cache, live_flag), "rep", 0)

    target = dest_group[:, 0]
    same_target = target[:, None] == target[None, :]
    earlier = jnp.arange(req_here)[None, :] < jnp.arange(req_here)[:, None]
    rank_index = jnp.sum(jnp.logical_and(same_target, earlier), axis=1)
    slot_index = target * per_group + rank_index
    selector = (jnp.arange(n_slots, dtype=jnp.int32)[:, None] == slot_index[None, :]).astype(
        jnp.bfloat16
    )
    outbound = jnp.einsum(
        "sr,rtc->stc", selector, queries, preferred_element_type=jnp.float32
    ).astype(jnp.bfloat16)
    outbound = outbound.reshape(groups, per_group, TREE, local_cols)
    (inbound,) = exchange([outbound], 0)
    routed_rows = inbound.reshape(n_slots * TREE, local_cols)

    key_rows = jnp.concatenate([prompt_cache[0, 0], partner_cache[0, 0]], axis=0)
    value_rows = jnp.concatenate([prompt_cache[0, 1], partner_cache[0, 1]], axis=0)
    seen = jnp.concatenate([positions < first_len[0], partner_flag > 0.5], axis=0)
    normed, lse = prompt_attend(routed_rows, key_rows, value_rows, seen)

    lse_width = per_group * TREE * heads_here
    lse_tile = -(-lse_width // 1024) * 1024
    lse = jnp.swapaxes(lse[:heads_here].reshape(heads_here, groups, per_group * TREE), 0, 1)
    lse_block = jnp.pad(lse.reshape(groups, lse_width), ((0, 0), (0, lse_tile - lse_width)))
    back_out, back_lse = exchange(
        [
            normed.reshape(groups, per_group, TREE, local_cols),
            lse_block.reshape(groups, lse_tile // 128, 128),
        ],
        1,
    )
    back_out = back_out.reshape(n_slots, TREE, local_cols)
    back_lse = back_lse.reshape(groups, lse_tile)[:, :lse_width]
    back_lse = jnp.moveaxis(back_lse.reshape(groups, heads_here, per_group, TREE), 1, 3)
    back_lse = back_lse.reshape(n_slots, TREE, heads_here)
    remote_out = split_heads(jnp.take(back_out, slot_index, axis=0)).astype(jnp.float32)
    remote_lse = jnp.take(back_lse, slot_index, axis=0)

    tree_max, tree_total, tree_accum = tree_attend(
        queries, tree_cache[:, 0], tree_cache[:, 1], tree_mask == 1
    )
    peaks = jnp.maximum(remote_lse, tree_max)
    factor_remote = jnp.exp(remote_lse - peaks)
    factor_tree = jnp.exp(tree_max - peaks)
    totals = factor_remote + tree_total * factor_tree
    accum = remote_out * factor_remote[..., None] + tree_accum * factor_tree[..., None]
    attn = jnp.moveaxis(accum / totals[..., None], 2, 0).astype(jnp.bfloat16)
    attn = attn.reshape(heads_here, req_here * TREE, HD)
    projected = gather_project(attn, out_weight).reshape(req_here, TREE, out_weight.shape[1])
    accepted_cache = jnp.take_along_axis(tree_cache, accepted_path[:, None, :, None], axis=2)
    return (projected, accepted_cache)


def solution(mesh):
    return jax.shard_map(
        local,
        mesh=mesh,
        in_specs=(
            P("rep", None, "tp"),
            P("rep", None, None, "tp"),
            P("rep", None, None),
            P("rep", None),
            P("rep", None),
            P("rep", None, None, "tp"),
            P("rep"),
            P("rep", None, None, "tp"),
            P("rep"),
            P(None, "tp"),
        ),
        out_specs=(P("rep", None, "tp"), P("rep", None, None, "tp")),
        check_vma=False,
    )
```

```python
import math

import jax
import jax.numpy as jnp
from jax import lax
from jax.experimental import pallas as pl
from jax.experimental.pallas import tpu as pltpu
from jax.sharding import PartitionSpec as P

MESH = pl.DeviceIdType.MESH

HD = 128
TREE = 48
PCAP = 152


NEG_FILL = -1e30


def exchange_kernel(n, count, paired, *refs):
    sources = refs[:count]
    pair_sources = refs[count : count + paired]
    targets = refs[count + paired : 2 * count + paired]
    pair_targets = refs[2 * count + paired : 2 * count + 2 * paired]
    send_sem, recv_sem, local_sem, pair_send, pair_recv = refs[2 * count + 2 * paired :]
    me = lax.axis_index("rep")
    partner = me + 1 - 2 * (me % 2)
    barrier = pltpu.get_barrier_semaphore()
    for offset in range(1, n):
        pl.semaphore_signal(
            barrier, inc=1, device_id={"rep": lax.rem(me + offset, n)}, device_id_type=MESH
        )
    pl.semaphore_wait(barrier, n - 1)
    copies = []
    for index in range(paired):
        remote = pltpu.make_async_remote_copy(
            src_ref=pair_sources[index],
            dst_ref=pair_targets[index],
            send_sem=pair_send.at[index],
            recv_sem=pair_recv.at[index],
            device_id={"rep": partner},
            device_id_type=MESH,
        )
        remote.start()
        copies.append(remote)
    for index in range(count):
        local = pltpu.make_async_copy(
            sources[index].at[me], targets[index].at[me], local_sem.at[index]
        )
        local.start()
        copies.append(local)
        for offset in range(1, n):
            peer = lax.rem(me + offset, n)
            remote = pltpu.make_async_remote_copy(
                src_ref=sources[index].at[peer],
                dst_ref=targets[index].at[me],
                send_sem=send_sem.at[index, offset],
                recv_sem=recv_sem.at[index, offset],
                device_id={"rep": peer},
                device_id_type=MESH,
            )
            remote.start()
            copies.append(remote)
    for copy in copies:
        copy.wait()


def exchange(arrays, tag, pairs=()):
    n = lax.axis_size("rep")
    count = len(arrays)
    paired = len(pairs)
    every = list(arrays) + list(pairs)
    outs = pl.pallas_call(
        lambda *refs: exchange_kernel(n, count, paired, *refs),
        out_shape=[jax.ShapeDtypeStruct(a.shape, a.dtype) for a in every],
        in_specs=[pl.BlockSpec(memory_space=pl.ANY)] * len(every),
        out_specs=[pl.BlockSpec(memory_space=pl.ANY)] * len(every),
        scratch_shapes=[
            pltpu.SemaphoreType.DMA((count, n)),
            pltpu.SemaphoreType.DMA((count, n)),
            pltpu.SemaphoreType.DMA((count,)),
            pltpu.SemaphoreType.DMA((max(paired, 1),)),
            pltpu.SemaphoreType.DMA((max(paired, 1),)),
        ],
        compiler_params=pltpu.CompilerParams(collective_id=tag, has_side_effects=True),
    )(*every)
    return outs[:count], outs[count:]


def gather_project_kernel(n_z, a_ref, w_ref, o_ref, slots, send_sem, recv_sem):
    me = lax.axis_index("tp")
    z = me // 2
    core = me % 2
    up = lax.rem(z + 1, n_z) * 2 + core
    down = lax.rem(z + n_z - 1, n_z) * 2 + core
    sibling = z * 2 + (1 - core)
    barrier = pltpu.get_barrier_semaphore()
    for peer in (up, down, sibling):
        pl.semaphore_signal(barrier, inc=1, device_id={"tp": peer}, device_id_type=MESH)
    pl.semaphore_wait(barrier, 3)
    slots[me] = a_ref[...]
    chains = ((0, 1, up, down), (1, -1, down, up))
    width = a_ref.shape[2]
    halves = slots.shape[1]

    def product(slot, half, block):
        row = pl.multiple_of((slot * halves + half) * width, width)
        return jnp.dot(block, w_ref[pl.ds(row, width), :], preferred_element_type=jnp.float32)

    total = jnp.zeros(o_ref.shape, jnp.float32)

    def arrival(slot, half, sender):
        pltpu.make_async_remote_copy(
            src_ref=slots.at[slot, half],
            dst_ref=slots.at[slot, half],
            send_sem=send_sem.at[half, 0],
            recv_sem=recv_sem.at[slot, half],
            device_id={"tp": sender},
            device_id_type=MESH,
        ).wait_recv()

    sends = []
    for step in range(n_z):
        for half, direction, ahead, behind in chains:
            slot = lax.rem(z - step * direction + 2 * n_z, n_z) * 2 + core
            if step == 0:
                source = a_ref.at[half]
            else:
                arrival(slot, half, behind)
                source = slots.at[slot, half]
            targets = ([(half, ahead)] if step < n_z - 1 else []) + [(2 + half, sibling)]
            for kind, peer in targets:
                copy = pltpu.make_async_remote_copy(
                    src_ref=source,
                    dst_ref=slots.at[slot, half],
                    send_sem=send_sem.at[kind, step],
                    recv_sem=recv_sem.at[slot, half],
                    device_id={"tp": peer},
                    device_id_type=MESH,
                )
                copy.start()
                sends.append(copy)
            total = total + product(slot, half, source[...])
    for step in range(n_z):
        for half, direction, ahead, behind in chains:
            slot = lax.rem(z - step * direction + 2 * n_z, n_z) * 2 + (1 - core)
            arrival(slot, half, sibling)
            total = total + product(slot, half, slots[slot, half])
    for copy in sends:
        copy.wait_send()
    o_ref[...] = total.astype(o_ref.dtype)


def gather_project(attn, weight):
    tp_size = lax.axis_size("tp")
    halves, rows, width = attn.shape
    return pl.pallas_call(
        lambda *refs: gather_project_kernel(tp_size // 2, *refs),
        out_shape=jax.ShapeDtypeStruct((rows, weight.shape[1]), jnp.bfloat16),
        in_specs=[pl.BlockSpec(memory_space=pltpu.VMEM)] * 2,
        out_specs=pl.BlockSpec(memory_space=pltpu.VMEM),
        scratch_shapes=[
            pltpu.VMEM((tp_size, halves, rows, width), jnp.bfloat16),
            pltpu.SemaphoreType.DMA((4, tp_size // 2)),
            pltpu.SemaphoreType.DMA((tp_size, halves)),
        ],
        compiler_params=pltpu.CompilerParams(collective_id=3, has_side_effects=True),
    )(attn, weight)


def split_heads(rows):
    return rows.reshape(rows.shape[:-1] + (rows.shape[-1] // HD, HD))


def prompt_kernel(q_ref, k_ref, v_ref, seen_ref, o_ref, lse_ref):
    rows = q_ref.shape[0]
    heads = q_ref.shape[1] // HD
    visible = seen_ref[...] > 0.5
    column = lax.broadcasted_iota(jnp.int32, (rows, 128), 1)
    lse_cols = jnp.zeros((rows, 128), jnp.float32)
    for head in range(heads):
        cols = slice(head * HD, (head + 1) * HD)
        scores = lax.dot_general(
            q_ref[:, cols],
            k_ref[:, cols],
            (((1,), (1,)), ((), ())),
            preferred_element_type=jnp.float32,
        ) * (1.0 / math.sqrt(HD))
        scores = jnp.where(visible, scores, NEG_FILL)
        peaks = jnp.max(scores, axis=1, keepdims=True)
        raw = jnp.where(visible, jnp.exp(scores - peaks), 0.0)
        totals = jnp.sum(raw, axis=1, keepdims=True)
        accum = jnp.dot(raw.astype(jnp.bfloat16), v_ref[:, cols], preferred_element_type=jnp.float32)
        o_ref[:, cols] = (accum / totals).astype(o_ref.dtype)
        lse_cols = jnp.where(column == head, peaks + jnp.log(totals), lse_cols)
    lse_ref[...] = jnp.transpose(lse_cols)[0:8, :]


def prompt_attend(query_rows, key_rows, value_rows, seen):
    n_rows, cols = query_rows.shape
    n_keys = key_rows.shape[0]
    padded = -(-n_keys // 128) * 128
    key_rows = jnp.pad(key_rows, ((0, padded - n_keys), (0, 0)))
    value_rows = jnp.pad(value_rows, ((0, padded - n_keys), (0, 0)))
    seen_row = jnp.pad(seen.astype(jnp.float32), (0, padded - n_keys)).reshape(1, padded)
    block = 384
    return pl.pallas_call(
        prompt_kernel,
        out_shape=[
            jax.ShapeDtypeStruct((n_rows, cols), jnp.bfloat16),
            jax.ShapeDtypeStruct((8, n_rows), jnp.float32),
        ],
        grid=(n_rows // block,),
        in_specs=[
            pl.BlockSpec((block, cols), lambda i: (i, 0)),
            pl.BlockSpec((padded, cols), lambda i: (0, 0)),
            pl.BlockSpec((padded, cols), lambda i: (0, 0)),
            pl.BlockSpec((1, padded), lambda i: (0, 0)),
        ],
        out_specs=[
            pl.BlockSpec((block, cols), lambda i: (i, 0)),
            pl.BlockSpec((8, block), lambda i: (0, i)),
        ],
    )(query_rows, key_rows, value_rows, seen_row)


def tree_attend(queries, keys, values, seen):
    q = split_heads(queries)
    k = split_heads(keys)
    v = split_heads(values)
    scores = jnp.einsum("rthd,rshd->rhts", q, k, preferred_element_type=jnp.float32) * (
        1.0 / math.sqrt(HD)
    )
    scores = jnp.where(seen[:, None], scores, NEG_FILL)
    peaks = jnp.max(scores, axis=3, keepdims=True)
    raw = jnp.where(seen[:, None], jnp.exp(scores - peaks), 0.0)
    totals = jnp.sum(raw, axis=3)
    accum = jnp.einsum(
        "rhts,rshd->rthd", raw.astype(jnp.bfloat16), v, preferred_element_type=jnp.float32
    )
    return jnp.swapaxes(peaks[..., 0], 1, 2), jnp.swapaxes(totals, 1, 2), accum


def local(
    queries,
    tree_cache,
    tree_mask,
    dest_group,
    accepted_path,
    prompt_cache,
    first_len,
    spill_cache,
    spill_len,
    out_weight,
):
    req_here = queries.shape[0]
    local_cols = queries.shape[2]
    heads_here = local_cols // HD
    groups = lax.axis_size("rep")
    per_group = max(2, (req_here + groups - 1) // groups)
    n_slots = groups * per_group
    positions = jnp.arange(PCAP, dtype=jnp.int32)
    own_len = jnp.full((8, 128), spill_len[0], jnp.float32)

    target = dest_group[:, 0]
    same_target = target[:, None] == target[None, :]
    earlier = jnp.arange(req_here)[None, :] < jnp.arange(req_here)[:, None]
    rank_index = jnp.sum(jnp.logical_and(same_target, earlier), axis=1)
    slot_index = target * per_group + rank_index
    selector = (jnp.arange(n_slots, dtype=jnp.int32)[:, None] == slot_index[None, :]).astype(
        jnp.bfloat16
    )
    outbound = jnp.einsum(
        "sr,rtc->stc", selector, queries, preferred_element_type=jnp.float32
    ).astype(jnp.bfloat16)
    outbound = outbound.reshape(groups, per_group, TREE, local_cols)
    (inbound,), (partner_cache, partner_len) = exchange([outbound], 0, (spill_cache, own_len))
    routed_rows = inbound.reshape(n_slots * TREE, local_cols)

    key_rows = jnp.concatenate([prompt_cache[0, 0], partner_cache[0, 0]], axis=0)
    value_rows = jnp.concatenate([prompt_cache[0, 1], partner_cache[0, 1]], axis=0)
    seen = jnp.concatenate([positions < first_len[0], positions.astype(jnp.float32) < partner_len[0, 0]], axis=0)
    normed, lse = prompt_attend(routed_rows, key_rows, value_rows, seen)

    lse_width = per_group * TREE * heads_here
    lse_tile = -(-lse_width // 1024) * 1024
    lse = jnp.swapaxes(lse[:heads_here].reshape(heads_here, groups, per_group * TREE), 0, 1)
    lse_block = jnp.pad(lse.reshape(groups, lse_width), ((0, 0), (0, lse_tile - lse_width)))
    (back_out, back_lse), _ = exchange(
        [
            normed.reshape(groups, per_group, TREE, local_cols),
            lse_block.reshape(groups, lse_tile // 128, 128),
        ],
        1,
    )
    back_out = back_out.reshape(n_slots, TREE, local_cols)
    back_lse = back_lse.reshape(groups, lse_tile)[:, :lse_width]
    back_lse = jnp.moveaxis(back_lse.reshape(groups, heads_here, per_group, TREE), 1, 3)
    back_lse = back_lse.reshape(n_slots, TREE, heads_here)
    remote_out = split_heads(jnp.take(back_out, slot_index, axis=0)).astype(jnp.float32)
    remote_lse = jnp.take(back_lse, slot_index, axis=0)

    tree_max, tree_total, tree_accum = tree_attend(
        queries, tree_cache[:, 0], tree_cache[:, 1], tree_mask == 1
    )
    peaks = jnp.maximum(remote_lse, tree_max)
    factor_remote = jnp.exp(remote_lse - peaks)
    factor_tree = jnp.exp(tree_max - peaks)
    totals = factor_remote + tree_total * factor_tree
    accum = remote_out * factor_remote[..., None] + tree_accum * factor_tree[..., None]
    attn = jnp.moveaxis(accum / totals[..., None], 2, 0).astype(jnp.bfloat16)
    attn = attn.reshape(heads_here, req_here * TREE, HD)
    projected = gather_project(attn, out_weight).reshape(req_here, TREE, out_weight.shape[1])
    accepted_cache = jnp.take_along_axis(tree_cache, accepted_path[:, None, :, None], axis=2)
    return (projected, accepted_cache)


def solution(mesh):
    return jax.shard_map(
        local,
        mesh=mesh,
        in_specs=(
            P("rep", None, "tp"),
            P("rep", None, None, "tp"),
            P("rep", None, None),
            P("rep", None),
            P("rep", None),
            P("rep", None, None, "tp"),
            P("rep"),
            P("rep", None, None, "tp"),
            P("rep"),
            P(None, "tp"),
        ),
        out_specs=(P("rep", None, "tp"), P("rep", None, None, "tp")),
        check_vma=False,
    )
```

```python
import math

import jax
import jax.numpy as jnp
from jax import lax
from jax.experimental import pallas as pl
from jax.experimental.pallas import tpu as pltpu
from jax.sharding import PartitionSpec as P

MESH = pl.DeviceIdType.MESH

HD = 128
TREE = 48
PCAP = 152


NEG_FILL = -1e30


def exchange_kernel(n, count, paired, *refs):
    sources = refs[:count]
    pair_sources = refs[count : count + paired]
    targets = refs[count + paired : 2 * count + paired]
    pair_targets = refs[2 * count + paired : 2 * count + 2 * paired]
    send_sem, recv_sem, local_sem, pair_send, pair_recv = refs[2 * count + 2 * paired :]
    me = lax.axis_index("rep")
    partner = me + 1 - 2 * (me % 2)
    barrier = pltpu.get_barrier_semaphore()
    for offset in range(1, n):
        pl.semaphore_signal(
            barrier, inc=1, device_id={"rep": lax.rem(me + offset, n)}, device_id_type=MESH
        )
    pl.semaphore_wait(barrier, n - 1)
    copies = []
    for index in range(paired):
        remote = pltpu.make_async_remote_copy(
            src_ref=pair_sources[index],
            dst_ref=pair_targets[index],
            send_sem=pair_send.at[index],
            recv_sem=pair_recv.at[index],
            device_id={"rep": partner},
            device_id_type=MESH,
        )
        remote.start()
        copies.append(remote)
    for index in range(count):
        local = pltpu.make_async_copy(
            sources[index].at[me], targets[index].at[me], local_sem.at[index]
        )
        local.start()
        copies.append(local)
        for offset in range(1, n):
            peer = lax.rem(me + offset, n)
            remote = pltpu.make_async_remote_copy(
                src_ref=sources[index].at[peer],
                dst_ref=targets[index].at[me],
                send_sem=send_sem.at[index, offset],
                recv_sem=recv_sem.at[index, offset],
                device_id={"rep": peer},
                device_id_type=MESH,
            )
            remote.start()
            copies.append(remote)
    for copy in copies:
        copy.wait()


def exchange(arrays, tag, pairs=()):
    n = lax.axis_size("rep")
    count = len(arrays)
    paired = len(pairs)
    every = list(arrays) + list(pairs)
    outs = pl.pallas_call(
        lambda *refs: exchange_kernel(n, count, paired, *refs),
        out_shape=[jax.ShapeDtypeStruct(a.shape, a.dtype) for a in every],
        in_specs=[pl.BlockSpec(memory_space=pl.ANY)] * len(every),
        out_specs=[pl.BlockSpec(memory_space=pl.ANY)] * len(every),
        scratch_shapes=[
            pltpu.SemaphoreType.DMA((count, n)),
            pltpu.SemaphoreType.DMA((count, n)),
            pltpu.SemaphoreType.DMA((count,)),
            pltpu.SemaphoreType.DMA((max(paired, 1),)),
            pltpu.SemaphoreType.DMA((max(paired, 1),)),
        ],
        compiler_params=pltpu.CompilerParams(collective_id=tag, has_side_effects=True),
    )(*every)
    return outs[:count], outs[count:]


def ring_exchange_kernel(n_rep, n_z, count, head, has_partial, *refs):
    sources = refs[:count]
    a_ref, w_ref = refs[count : count + 2]
    partial_ref = refs[count + 2] if has_partial else None
    rest = refs[count + 2 + has_partial :]
    targets = rest[:count]
    o_ref = rest[count]
    scratch = rest[count + 1 :]
    if count:
        ex_send, ex_recv, ex_local = scratch[:3]
        scratch = scratch[3:]
    slots, send_sem, recv_sem = scratch
    me_rep = lax.axis_index("rep")
    me = lax.axis_index("tp")
    z = me // 2
    core = me % 2
    step_z = 1 - 2 * core
    ring_next = lax.rem(z + step_z + n_z, n_z) * 2 + core
    ring_prev = lax.rem(z - step_z + n_z, n_z) * 2 + core
    sibling = z * 2 + (1 - core)
    barrier = pltpu.get_barrier_semaphore()
    for peer in (ring_next, ring_prev, sibling):
        pl.semaphore_signal(barrier, inc=1, device_id={"tp": peer}, device_id_type=MESH)
    if count:
        for offset in range(1, n_rep):
            pl.semaphore_signal(
                barrier, inc=1, device_id={"rep": lax.rem(me_rep + offset, n_rep)}, device_id_type=MESH
            )
    pl.semaphore_wait(barrier, 3 + (n_rep - 1 if count else 0))
    copies = []
    for index in range(count):
        local = pltpu.make_async_copy(
            sources[index].at[me_rep], targets[index].at[me_rep], ex_local.at[index]
        )
        local.start()
        copies.append(local)
        for offset in range(1, n_rep):
            peer = lax.rem(me_rep + offset, n_rep)
            remote = pltpu.make_async_remote_copy(
                src_ref=sources[index].at[peer],
                dst_ref=targets[index].at[me_rep],
                send_sem=ex_send.at[index, offset],
                recv_sem=ex_recv.at[index, offset],
                device_id={"rep": peer},
                device_id_type=MESH,
            )
            remote.start()
            copies.append(remote)
    slots[me] = a_ref[...]
    width = a_ref.shape[1]

    def product(slot, block):
        row = pl.multiple_of(slot * 2 * width + head * width, width)
        return jnp.dot(block, w_ref[pl.ds(row, width), :], preferred_element_type=jnp.float32)

    def arrival(slot, sender):
        pltpu.make_async_remote_copy(
            src_ref=slots.at[slot],
            dst_ref=slots.at[slot],
            send_sem=send_sem.at[0, 0],
            recv_sem=recv_sem.at[slot],
            device_id={"tp": sender},
            device_id_type=MESH,
        ).wait_recv()

    total = partial_ref[...] if has_partial else jnp.zeros(o_ref.shape, jnp.float32)
    for step in range(n_z):
        slot = lax.rem(z - step * step_z + 2 * n_z, n_z) * 2 + core
        if step == 0:
            source = a_ref
        else:
            arrival(slot, ring_prev)
            source = slots.at[slot]
        targets_here = ([(0, ring_next)] if step < n_z - 1 else []) + [(1, sibling)]
        for kind, peer in targets_here:
            copy = pltpu.make_async_remote_copy(
                src_ref=source,
                dst_ref=slots.at[slot],
                send_sem=send_sem.at[kind, step],
                recv_sem=recv_sem.at[slot],
                device_id={"tp": peer},
                device_id_type=MESH,
            )
            copy.start()
            copies.append(copy)
        total = total + product(slot, source[...])
    for step in range(n_z):
        slot = lax.rem(z - step * step_z + 2 * n_z, n_z) * 2 + (1 - core)
        arrival(slot, sibling)
        total = total + product(slot, slots[slot])
    o_ref[...] = total.astype(o_ref.dtype)
    for copy in copies[: count * n_rep]:
        copy.wait()
    for copy in copies[count * n_rep :]:
        copy.wait_send()


def ring_exchange(arrays, attn, weight, head, tag, partial=None, out_dtype=jnp.float32):
    n_rep = lax.axis_size("rep")
    tp_size = lax.axis_size("tp")
    count = len(arrays)
    rows, width = attn.shape
    extra = [] if partial is None else [partial]
    scratch = []
    if count:
        scratch += [
            pltpu.SemaphoreType.DMA((count, n_rep)),
            pltpu.SemaphoreType.DMA((count, n_rep)),
            pltpu.SemaphoreType.DMA((count,)),
        ]
    scratch += [
        pltpu.VMEM((tp_size, rows, width), jnp.bfloat16),
        pltpu.SemaphoreType.DMA((2, tp_size // 2)),
        pltpu.SemaphoreType.DMA((tp_size,)),
    ]
    outs = pl.pallas_call(
        lambda *refs: ring_exchange_kernel(n_rep, tp_size // 2, count, head, len(extra), *refs),
        out_shape=[jax.ShapeDtypeStruct(a.shape, a.dtype) for a in arrays]
        + [jax.ShapeDtypeStruct((rows, weight.shape[1]), out_dtype)],
        in_specs=[pl.BlockSpec(memory_space=pl.ANY)] * count
        + [pl.BlockSpec(memory_space=pltpu.VMEM)] * (2 + len(extra)),
        out_specs=[pl.BlockSpec(memory_space=pl.ANY)] * count
        + [pl.BlockSpec(memory_space=pltpu.VMEM)],
        scratch_shapes=scratch,
        compiler_params=pltpu.CompilerParams(collective_id=tag, has_side_effects=True),
    )(*arrays, attn, weight, *extra)
    return outs[:count], outs[count]


def split_heads(rows):
    return rows.reshape(rows.shape[:-1] + (rows.shape[-1] // HD, HD))


def prompt_kernel(q_ref, k_ref, v_ref, seen_ref, o_ref, lse_ref):
    rows = q_ref.shape[0]
    heads = q_ref.shape[1] // HD
    visible = seen_ref[...] > 0.5
    column = lax.broadcasted_iota(jnp.int32, (rows, 128), 1)
    lse_cols = jnp.zeros((rows, 128), jnp.float32)
    for head in range(heads):
        cols = slice(head * HD, (head + 1) * HD)
        scores = lax.dot_general(
            q_ref[:, cols],
            k_ref[:, cols],
            (((1,), (1,)), ((), ())),
            preferred_element_type=jnp.float32,
        ) * (1.0 / math.sqrt(HD))
        scores = jnp.where(visible, scores, NEG_FILL)
        peaks = jnp.max(scores, axis=1, keepdims=True)
        raw = jnp.where(visible, jnp.exp(scores - peaks), 0.0)
        totals = jnp.sum(raw, axis=1, keepdims=True)
        accum = jnp.dot(raw.astype(jnp.bfloat16), v_ref[:, cols], preferred_element_type=jnp.float32)
        o_ref[head] = (accum / totals).astype(o_ref.dtype)
        lse_cols = jnp.where(column == head, peaks + jnp.log(totals), lse_cols)
    lse_ref[...] = jnp.transpose(lse_cols)[0:8, :]


def prompt_attend(query_rows, key_rows, value_rows, seen):
    n_rows, cols = query_rows.shape
    n_keys = key_rows.shape[0]
    padded = -(-n_keys // 128) * 128
    key_rows = jnp.pad(key_rows, ((0, padded - n_keys), (0, 0)))
    value_rows = jnp.pad(value_rows, ((0, padded - n_keys), (0, 0)))
    seen_row = jnp.pad(seen.astype(jnp.float32), (0, padded - n_keys)).reshape(1, padded)
    block = 384
    return pl.pallas_call(
        prompt_kernel,
        out_shape=[
            jax.ShapeDtypeStruct((cols // HD, n_rows, HD), jnp.bfloat16),
            jax.ShapeDtypeStruct((8, n_rows), jnp.float32),
        ],
        grid=(n_rows // block,),
        in_specs=[
            pl.BlockSpec((block, cols), lambda i: (i, 0)),
            pl.BlockSpec((padded, cols), lambda i: (0, 0)),
            pl.BlockSpec((padded, cols), lambda i: (0, 0)),
            pl.BlockSpec((1, padded), lambda i: (0, 0)),
        ],
        out_specs=[
            pl.BlockSpec((cols // HD, block, HD), lambda i: (0, i, 0)),
            pl.BlockSpec((8, block), lambda i: (0, i)),
        ],
    )(query_rows, key_rows, value_rows, seen_row)


def tree_attend(queries, keys, values, seen):
    q = split_heads(queries)
    k = split_heads(keys)
    v = split_heads(values)
    scores = jnp.einsum("rthd,rshd->rhts", q, k, preferred_element_type=jnp.float32) * (
        1.0 / math.sqrt(HD)
    )
    scores = jnp.where(seen[:, None], scores, NEG_FILL)
    peaks = jnp.max(scores, axis=3, keepdims=True)
    raw = jnp.where(seen[:, None], jnp.exp(scores - peaks), 0.0)
    totals = jnp.sum(raw, axis=3)
    accum = jnp.einsum(
        "rhts,rshd->rthd", raw.astype(jnp.bfloat16), v, preferred_element_type=jnp.float32
    )
    return jnp.swapaxes(peaks[..., 0], 1, 2), jnp.swapaxes(totals, 1, 2), accum


def local(
    queries,
    tree_cache,
    tree_mask,
    dest_group,
    accepted_path,
    prompt_cache,
    first_len,
    spill_cache,
    spill_len,
    out_weight,
):
    req_here = queries.shape[0]
    local_cols = queries.shape[2]
    heads_here = local_cols // HD
    groups = lax.axis_size("rep")
    per_group = max(2, (req_here + groups - 1) // groups)
    n_slots = groups * per_group
    positions = jnp.arange(PCAP, dtype=jnp.int32)
    own_len = jnp.full((8, 128), spill_len[0], jnp.float32)

    target = dest_group[:, 0]
    same_target = target[:, None] == target[None, :]
    earlier = jnp.arange(req_here)[None, :] < jnp.arange(req_here)[:, None]
    rank_index = jnp.sum(jnp.logical_and(same_target, earlier), axis=1)
    slot_index = target * per_group + rank_index
    selector = (jnp.arange(n_slots, dtype=jnp.int32)[:, None] == slot_index[None, :]).astype(
        jnp.bfloat16
    )
    outbound = jnp.einsum(
        "sr,rtc->stc", selector, queries, preferred_element_type=jnp.float32
    ).astype(jnp.bfloat16)
    outbound = outbound.reshape(groups, per_group, TREE, local_cols)
    (inbound,), (partner_cache, partner_len) = exchange([outbound], 0, (spill_cache, own_len))
    routed_rows = inbound.reshape(n_slots * TREE, local_cols)

    key_rows = jnp.concatenate([prompt_cache[0, 0], partner_cache[0, 0]], axis=0)
    value_rows = jnp.concatenate([prompt_cache[0, 1], partner_cache[0, 1]], axis=0)
    seen = jnp.concatenate([positions < first_len[0], positions.astype(jnp.float32) < partner_len[0, 0]], axis=0)
    normed, lse = prompt_attend(routed_rows, key_rows, value_rows, seen)

    lse_width = per_group * TREE
    lse_tile = -(-lse_width // 1024) * 1024
    lse = lse[:heads_here].reshape(heads_here, groups, lse_width)
    lse = jnp.pad(lse, ((0, 0), (0, 0), (0, lse_tile - lse_width)))
    lse = lse.reshape(heads_here, groups, lse_tile // 128, 128)

    tree_max, tree_total, tree_accum = tree_attend(
        queries, tree_cache[:, 0], tree_cache[:, 1], tree_mask == 1
    )

    def returned(head):
        return [normed[head].reshape(groups, per_group, TREE, HD), lse[head]]

    def combined(head, back_out, back_lse):
        back_lse = back_lse.reshape(groups, lse_tile)[:, :lse_width].reshape(n_slots, TREE)
        remote_out = jnp.take(back_out.reshape(n_slots, TREE, HD), slot_index, axis=0)
        remote_lse = jnp.take(back_lse, slot_index, axis=0)
        peaks = jnp.maximum(remote_lse, tree_max[..., head])
        factor_remote = jnp.exp(remote_lse - peaks)
        factor_tree = jnp.exp(tree_max[..., head] - peaks)
        totals = factor_remote + tree_total[..., head] * factor_tree
        accum = (
            remote_out.astype(jnp.float32) * factor_remote[..., None]
            + tree_accum[:, :, head] * factor_tree[..., None]
        )
        return (accum / totals[..., None]).reshape(req_here * TREE, HD).astype(jnp.bfloat16)

    assert heads_here == 2
    (back_out, back_lse), _ = exchange(returned(0), 1)
    attn_first = combined(0, back_out, back_lse)
    (back_out, back_lse), partial = ring_exchange(returned(1), attn_first, out_weight, 0, 2)
    attn_second = combined(1, back_out, back_lse)
    _, projected = ring_exchange(
        [], attn_second, out_weight, 1, 3, partial=partial, out_dtype=jnp.bfloat16
    )
    projected = projected.reshape(req_here, TREE, out_weight.shape[1])
    accepted_cache = jnp.take_along_axis(tree_cache, accepted_path[:, None, :, None], axis=2)
    return (projected, accepted_cache)


def solution(mesh):
    return jax.shard_map(
        local,
        mesh=mesh,
        in_specs=(
            P("rep", None, "tp"),
            P("rep", None, None, "tp"),
            P("rep", None, None),
            P("rep", None),
            P("rep", None),
            P("rep", None, None, "tp"),
            P("rep"),
            P("rep", None, None, "tp"),
            P("rep"),
            P(None, "tp"),
        ),
        out_specs=(P("rep", None, "tp"), P("rep", None, None, "tp")),
        check_vma=False,
    )
```

```python
import math

import jax
import jax.numpy as jnp
from jax import lax
from jax.experimental import pallas as pl
from jax.experimental.pallas import tpu as pltpu
from jax.sharding import PartitionSpec as P

MESH = pl.DeviceIdType.MESH

HD = 128
TREE = 48
PCAP = 152


NEG_FILL = -1e30


def exchange_kernel(n, count, paired, *refs):
    sources = refs[:count]
    pair_sources = refs[count : count + paired]
    targets = refs[count + paired : 2 * count + paired]
    pair_targets = refs[2 * count + paired : 2 * count + 2 * paired]
    send_sem, recv_sem, local_sem, pair_send, pair_recv = refs[2 * count + 2 * paired :]
    me = lax.axis_index("rep")
    partner = me + 1 - 2 * (me % 2)
    barrier = pltpu.get_barrier_semaphore()
    for offset in range(1, n):
        pl.semaphore_signal(
            barrier, inc=1, device_id={"rep": lax.rem(me + offset, n)}, device_id_type=MESH
        )
    pl.semaphore_wait(barrier, n - 1)
    copies = []
    for index in range(paired):
        remote = pltpu.make_async_remote_copy(
            src_ref=pair_sources[index],
            dst_ref=pair_targets[index],
            send_sem=pair_send.at[index],
            recv_sem=pair_recv.at[index],
            device_id={"rep": partner},
            device_id_type=MESH,
        )
        remote.start()
        copies.append(remote)
    for index in range(count):
        local = pltpu.make_async_copy(
            sources[index].at[me], targets[index].at[me], local_sem.at[index]
        )
        local.start()
        copies.append(local)
        for offset in range(1, n):
            peer = lax.rem(me + offset, n)
            remote = pltpu.make_async_remote_copy(
                src_ref=sources[index].at[peer],
                dst_ref=targets[index].at[me],
                send_sem=send_sem.at[index, offset],
                recv_sem=recv_sem.at[index, offset],
                device_id={"rep": peer},
                device_id_type=MESH,
            )
            remote.start()
            copies.append(remote)
    for copy in copies:
        copy.wait()


def exchange(arrays, tag, pairs=()):
    n = lax.axis_size("rep")
    count = len(arrays)
    paired = len(pairs)
    every = list(arrays) + list(pairs)
    outs = pl.pallas_call(
        lambda *refs: exchange_kernel(n, count, paired, *refs),
        out_shape=[jax.ShapeDtypeStruct(a.shape, a.dtype) for a in every],
        in_specs=[pl.BlockSpec(memory_space=pl.ANY)] * len(every),
        out_specs=[pl.BlockSpec(memory_space=pl.ANY)] * len(every),
        scratch_shapes=[
            pltpu.SemaphoreType.DMA((count, n)),
            pltpu.SemaphoreType.DMA((count, n)),
            pltpu.SemaphoreType.DMA((count,)),
            pltpu.SemaphoreType.DMA((max(paired, 1),)),
            pltpu.SemaphoreType.DMA((max(paired, 1),)),
        ],
        compiler_params=pltpu.CompilerParams(collective_id=tag, has_side_effects=True),
    )(*every)
    return outs[:count], outs[count:]


def gather_project_kernel(n_z, a_ref, w_ref, o_ref, slots, send_sem, recv_sem):
    me = lax.axis_index("tp")
    z = me // 2
    core = me % 2
    up = lax.rem(z + 1, n_z) * 2 + core
    down = lax.rem(z + n_z - 1, n_z) * 2 + core
    sibling = z * 2 + (1 - core)
    barrier = pltpu.get_barrier_semaphore()
    for peer in (up, down, sibling):
        pl.semaphore_signal(barrier, inc=1, device_id={"tp": peer}, device_id_type=MESH)
    pl.semaphore_wait(barrier, 3)
    slots[me] = a_ref[...]
    far = n_z // 2
    near = n_z - 1 - far
    chains = ((0, 1, up, down, far), (0, -1, down, up, near), (1, 1, up, down, near), (1, -1, down, up, far))
    width = a_ref.shape[2]
    halves = slots.shape[1]

    def product(slot, half, block):
        row = pl.multiple_of((slot * halves + half) * width, width)
        return jnp.dot(block, w_ref[pl.ds(row, width), :], preferred_element_type=jnp.float32)

    def arrival(slot, half, sender):
        pltpu.make_async_remote_copy(
            src_ref=slots.at[slot, half],
            dst_ref=slots.at[slot, half],
            send_sem=send_sem.at[0, 0, 0],
            recv_sem=recv_sem.at[slot, half],
            device_id={"tp": sender},
            device_id_type=MESH,
        ).wait_recv()

    total = jnp.zeros(o_ref.shape, jnp.float32)
    sends = []
    for step in range(far + 1):
        for chain, (half, direction, ahead, behind, hops) in enumerate(chains):
            if step > hops or (step == 0 and direction < 0):
                continue
            slot = lax.rem(z - step * direction + 2 * n_z, n_z) * 2 + core
            if step == 0:
                source = a_ref.at[half]
            else:
                arrival(slot, half, behind)
                source = slots.at[slot, half]
            targets = [(1, sibling)]
            if step < hops:
                targets = [(0, ahead)] + targets
            if step == 0:
                targets = targets + [(0, down)]
            for kind, peer in targets:
                copy = pltpu.make_async_remote_copy(
                    src_ref=source,
                    dst_ref=slots.at[slot, half],
                    send_sem=send_sem.at[chain + (1 if peer is down and step == 0 else 0), kind, step],
                    recv_sem=recv_sem.at[slot, half],
                    device_id={"tp": peer},
                    device_id_type=MESH,
                )
                copy.start()
                sends.append(copy)
            total = total + product(slot, half, source[...])
    for half, direction, ahead, behind, hops in chains:
        for step in range(hops + 1):
            if step == 0 and direction < 0:
                continue
            slot = lax.rem(z - step * direction + 2 * n_z, n_z) * 2 + (1 - core)
            arrival(slot, half, sibling)
            total = total + product(slot, half, slots[slot, half])
    for copy in sends:
        copy.wait_send()
    o_ref[...] = total.astype(o_ref.dtype)


def gather_project(attn, weight):
    tp_size = lax.axis_size("tp")
    halves, rows, width = attn.shape
    return pl.pallas_call(
        lambda *refs: gather_project_kernel(tp_size // 2, *refs),
        out_shape=jax.ShapeDtypeStruct((rows, weight.shape[1]), jnp.bfloat16),
        in_specs=[pl.BlockSpec(memory_space=pltpu.VMEM)] * 2,
        out_specs=pl.BlockSpec(memory_space=pltpu.VMEM),
        scratch_shapes=[
            pltpu.VMEM((tp_size, halves, rows, width), jnp.bfloat16),
            pltpu.SemaphoreType.DMA((4, 2, tp_size // 4 + 1)),
            pltpu.SemaphoreType.DMA((tp_size, halves)),
        ],
        compiler_params=pltpu.CompilerParams(collective_id=3, has_side_effects=True),
    )(attn, weight)


def split_heads(rows):
    return rows.reshape(rows.shape[:-1] + (rows.shape[-1] // HD, HD))


def prompt_kernel(q_ref, k_ref, v_ref, seen_ref, o_ref, lse_ref):
    rows = q_ref.shape[0]
    heads = q_ref.shape[1] // HD
    visible = seen_ref[...] > 0.5
    column = lax.broadcasted_iota(jnp.int32, (rows, 128), 1)
    lse_cols = jnp.zeros((rows, 128), jnp.float32)
    for head in range(heads):
        cols = slice(head * HD, (head + 1) * HD)
        scores = lax.dot_general(
            q_ref[:, cols],
            k_ref[:, cols],
            (((1,), (1,)), ((), ())),
            preferred_element_type=jnp.float32,
        ) * (1.0 / math.sqrt(HD))
        scores = jnp.where(visible, scores, NEG_FILL)
        peaks = jnp.max(scores, axis=1, keepdims=True)
        raw = jnp.where(visible, jnp.exp(scores - peaks), 0.0)
        totals = jnp.sum(raw, axis=1, keepdims=True)
        accum = jnp.dot(raw.astype(jnp.bfloat16), v_ref[:, cols], preferred_element_type=jnp.float32)
        o_ref[:, cols] = (accum / totals).astype(o_ref.dtype)
        lse_cols = jnp.where(column == head, peaks + jnp.log(totals), lse_cols)
    lse_ref[...] = jnp.transpose(lse_cols)[0:8, :]


def prompt_attend(query_rows, key_rows, value_rows, seen):
    n_rows, cols = query_rows.shape
    n_keys = key_rows.shape[0]
    padded = -(-n_keys // 128) * 128
    key_rows = jnp.pad(key_rows, ((0, padded - n_keys), (0, 0)))
    value_rows = jnp.pad(value_rows, ((0, padded - n_keys), (0, 0)))
    seen_row = jnp.pad(seen.astype(jnp.float32), (0, padded - n_keys)).reshape(1, padded)
    block = 384
    return pl.pallas_call(
        prompt_kernel,
        out_shape=[
            jax.ShapeDtypeStruct((n_rows, cols), jnp.bfloat16),
            jax.ShapeDtypeStruct((8, n_rows), jnp.float32),
        ],
        grid=(n_rows // block,),
        in_specs=[
            pl.BlockSpec((block, cols), lambda i: (i, 0)),
            pl.BlockSpec((padded, cols), lambda i: (0, 0)),
            pl.BlockSpec((padded, cols), lambda i: (0, 0)),
            pl.BlockSpec((1, padded), lambda i: (0, 0)),
        ],
        out_specs=[
            pl.BlockSpec((block, cols), lambda i: (i, 0)),
            pl.BlockSpec((8, block), lambda i: (0, i)),
        ],
    )(query_rows, key_rows, value_rows, seen_row)


def tree_attend(queries, keys, values, seen):
    q = split_heads(queries)
    k = split_heads(keys)
    v = split_heads(values)
    scores = jnp.einsum("rthd,rshd->rhts", q, k, preferred_element_type=jnp.float32) * (
        1.0 / math.sqrt(HD)
    )
    scores = jnp.where(seen[:, None], scores, NEG_FILL)
    peaks = jnp.max(scores, axis=3, keepdims=True)
    raw = jnp.where(seen[:, None], jnp.exp(scores - peaks), 0.0)
    totals = jnp.sum(raw, axis=3)
    accum = jnp.einsum(
        "rhts,rshd->rthd", raw.astype(jnp.bfloat16), v, preferred_element_type=jnp.float32
    )
    return jnp.swapaxes(peaks[..., 0], 1, 2), jnp.swapaxes(totals, 1, 2), accum


def local(
    queries,
    tree_cache,
    tree_mask,
    dest_group,
    accepted_path,
    prompt_cache,
    first_len,
    spill_cache,
    spill_len,
    out_weight,
):
    req_here = queries.shape[0]
    local_cols = queries.shape[2]
    heads_here = local_cols // HD
    groups = lax.axis_size("rep")
    per_group = max(2, (req_here + groups - 1) // groups)
    n_slots = groups * per_group
    positions = jnp.arange(PCAP, dtype=jnp.int32)
    own_len = jnp.full((8, 128), spill_len[0], jnp.float32)

    target = dest_group[:, 0]
    same_target = target[:, None] == target[None, :]
    earlier = jnp.arange(req_here)[None, :] < jnp.arange(req_here)[:, None]
    rank_index = jnp.sum(jnp.logical_and(same_target, earlier), axis=1)
    slot_index = target * per_group + rank_index
    selector = (jnp.arange(n_slots, dtype=jnp.int32)[:, None] == slot_index[None, :]).astype(
        jnp.bfloat16
    )
    outbound = jnp.einsum(
        "sr,rtc->stc", selector, queries, preferred_element_type=jnp.float32
    ).astype(jnp.bfloat16)
    outbound = outbound.reshape(groups, per_group, TREE, local_cols)
    (inbound,), (partner_cache, partner_len) = exchange([outbound], 0, (spill_cache, own_len))
    routed_rows = inbound.reshape(n_slots * TREE, local_cols)

    key_rows = jnp.concatenate([prompt_cache[0, 0], partner_cache[0, 0]], axis=0)
    value_rows = jnp.concatenate([prompt_cache[0, 1], partner_cache[0, 1]], axis=0)
    seen = jnp.concatenate([positions < first_len[0], positions.astype(jnp.float32) < partner_len[0, 0]], axis=0)
    normed, lse = prompt_attend(routed_rows, key_rows, value_rows, seen)

    lse_width = per_group * TREE * heads_here
    lse_tile = -(-lse_width // 1024) * 1024
    lse = jnp.swapaxes(lse[:heads_here].reshape(heads_here, groups, per_group * TREE), 0, 1)
    lse_block = jnp.pad(lse.reshape(groups, lse_width), ((0, 0), (0, lse_tile - lse_width)))
    (back_out, back_lse), _ = exchange(
        [
            normed.reshape(groups, per_group, TREE, local_cols),
            lse_block.reshape(groups, lse_tile // 128, 128),
        ],
        1,
    )
    back_out = back_out.reshape(n_slots, TREE, local_cols)
    back_lse = back_lse.reshape(groups, lse_tile)[:, :lse_width]
    back_lse = jnp.moveaxis(back_lse.reshape(groups, heads_here, per_group, TREE), 1, 3)
    back_lse = back_lse.reshape(n_slots, TREE, heads_here)
    remote_out = split_heads(jnp.take(back_out, slot_index, axis=0)).astype(jnp.float32)
    remote_lse = jnp.take(back_lse, slot_index, axis=0)

    tree_max, tree_total, tree_accum = tree_attend(
        queries, tree_cache[:, 0], tree_cache[:, 1], tree_mask == 1
    )
    peaks = jnp.maximum(remote_lse, tree_max)
    factor_remote = jnp.exp(remote_lse - peaks)
    factor_tree = jnp.exp(tree_max - peaks)
    totals = factor_remote + tree_total * factor_tree
    accum = remote_out * factor_remote[..., None] + tree_accum * factor_tree[..., None]
    attn = jnp.moveaxis(accum / totals[..., None], 2, 0).astype(jnp.bfloat16)
    attn = attn.reshape(heads_here, req_here * TREE, HD)
    projected = gather_project(attn, out_weight).reshape(req_here, TREE, out_weight.shape[1])
    accepted_cache = jnp.take_along_axis(tree_cache, accepted_path[:, None, :, None], axis=2)
    return (projected, accepted_cache)


def solution(mesh):
    return jax.shard_map(
        local,
        mesh=mesh,
        in_specs=(
            P("rep", None, "tp"),
            P("rep", None, None, "tp"),
            P("rep", None, None),
            P("rep", None),
            P("rep", None),
            P("rep", None, None, "tp"),
            P("rep"),
            P("rep", None, None, "tp"),
            P("rep"),
            P(None, "tp"),
        ),
        out_specs=(P("rep", None, "tp"), P("rep", None, None, "tp")),
        check_vma=False,
    )
```

```python
import math

import jax
import jax.numpy as jnp
from jax import lax
from jax.experimental import pallas as pl
from jax.experimental.pallas import tpu as pltpu
from jax.sharding import PartitionSpec as P

MESH = pl.DeviceIdType.MESH

HD = 128
TREE = 48
PCAP = 152


NEG_FILL = -1e30


def exchange_kernel(n, count, paired, *refs):
    sources = refs[:count]
    pair_sources = refs[count : count + paired]
    targets = refs[count + paired : 2 * count + paired]
    pair_targets = refs[2 * count + paired : 2 * count + 2 * paired]
    send_sem, recv_sem, local_sem, pair_send, pair_recv = refs[2 * count + 2 * paired :]
    me = lax.axis_index("rep")
    partner = me + 1 - 2 * (me % 2)
    barrier = pltpu.get_barrier_semaphore()
    for offset in range(1, n):
        pl.semaphore_signal(
            barrier, inc=1, device_id={"rep": lax.rem(me + offset, n)}, device_id_type=MESH
        )
    pl.semaphore_wait(barrier, n - 1)
    copies = []
    for index in range(paired):
        remote = pltpu.make_async_remote_copy(
            src_ref=pair_sources[index],
            dst_ref=pair_targets[index],
            send_sem=pair_send.at[index],
            recv_sem=pair_recv.at[index],
            device_id={"rep": partner},
            device_id_type=MESH,
        )
        remote.start()
        copies.append(remote)
    for index in range(count):
        local = pltpu.make_async_copy(
            sources[index].at[me], targets[index].at[me], local_sem.at[index]
        )
        local.start()
        copies.append(local)
        for offset in range(1, n):
            peer = lax.rem(me + offset, n)
            remote = pltpu.make_async_remote_copy(
                src_ref=sources[index].at[peer],
                dst_ref=targets[index].at[me],
                send_sem=send_sem.at[index, offset],
                recv_sem=recv_sem.at[index, offset],
                device_id={"rep": peer},
                device_id_type=MESH,
            )
            remote.start()
            copies.append(remote)
    for copy in copies:
        copy.wait()


def exchange(arrays, tag, pairs=()):
    n = lax.axis_size("rep")
    count = len(arrays)
    paired = len(pairs)
    every = list(arrays) + list(pairs)
    outs = pl.pallas_call(
        lambda *refs: exchange_kernel(n, count, paired, *refs),
        out_shape=[jax.ShapeDtypeStruct(a.shape, a.dtype) for a in every],
        in_specs=[pl.BlockSpec(memory_space=pl.ANY)] * len(every),
        out_specs=[pl.BlockSpec(memory_space=pl.ANY)] * len(every),
        scratch_shapes=[
            pltpu.SemaphoreType.DMA((count, n)),
            pltpu.SemaphoreType.DMA((count, n)),
            pltpu.SemaphoreType.DMA((count,)),
            pltpu.SemaphoreType.DMA((max(paired, 1),)),
            pltpu.SemaphoreType.DMA((max(paired, 1),)),
        ],
        compiler_params=pltpu.CompilerParams(collective_id=tag, has_side_effects=True),
    )(*every)
    return outs[:count], outs[count:]


def gather_project_kernel(n_z, a_ref, w_ref, o_ref, slots, send_sem, recv_sem):
    me = lax.axis_index("tp")
    z = me // 2
    core = me % 2
    up = lax.rem(z + 1, n_z) * 2 + core
    down = lax.rem(z + n_z - 1, n_z) * 2 + core
    sibling = z * 2 + (1 - core)
    barrier = pltpu.get_barrier_semaphore()
    for peer in (up, down, sibling):
        pl.semaphore_signal(barrier, inc=1, device_id={"tp": peer}, device_id_type=MESH)
    pl.semaphore_wait(barrier, 3)
    slots[me] = a_ref[...]
    far = n_z // 2
    near = n_z - 1 - far
    chains = ((0, 1, up, down, far), (0, -1, down, up, near), (1, 1, up, down, near), (1, -1, down, up, far))
    width = a_ref.shape[2]
    halves = slots.shape[1]

    def product(slot, half, block):
        row = pl.multiple_of((slot * halves + half) * width, width)
        return jnp.dot(block, w_ref[pl.ds(row, width), :], preferred_element_type=jnp.float32)

    def arrival(slot, half, sender):
        pltpu.make_async_remote_copy(
            src_ref=slots.at[slot, half],
            dst_ref=slots.at[slot, half],
            send_sem=send_sem.at[0, 0, 0],
            recv_sem=recv_sem.at[slot, half],
            device_id={"tp": sender},
            device_id_type=MESH,
        ).wait_recv()

    total = jnp.zeros(o_ref.shape, jnp.float32)
    sends = []
    for step in range(far + 1):
        for chain, (half, direction, ahead, behind, hops) in enumerate(chains):
            if step > hops or (step == 0 and direction < 0):
                continue
            slot = lax.rem(z - step * direction + 2 * n_z, n_z) * 2 + core
            if step == 0:
                source = a_ref.at[half]
            else:
                arrival(slot, half, behind)
                source = slots.at[slot, half]
            targets = [(1, sibling)]
            if step < hops:
                targets = [(0, ahead)] + targets
            if step == 0:
                targets = targets + [(0, down)]
            for kind, peer in targets:
                copy = pltpu.make_async_remote_copy(
                    src_ref=source,
                    dst_ref=slots.at[slot, half],
                    send_sem=send_sem.at[chain + (1 if peer is down and step == 0 else 0), kind, step],
                    recv_sem=recv_sem.at[slot, half],
                    device_id={"tp": peer},
                    device_id_type=MESH,
                )
                copy.start()
                sends.append(copy)
            total = total + product(slot, half, source[...])
    for half, direction, ahead, behind, hops in chains:
        for step in range(hops + 1):
            if step == 0 and direction < 0:
                continue
            slot = lax.rem(z - step * direction + 2 * n_z, n_z) * 2 + (1 - core)
            arrival(slot, half, sibling)
            total = total + product(slot, half, slots[slot, half])
    for copy in sends:
        copy.wait_send()
    o_ref[...] = total.astype(o_ref.dtype)


def gather_project(attn, weight):
    tp_size = lax.axis_size("tp")
    halves, rows, width = attn.shape
    return pl.pallas_call(
        lambda *refs: gather_project_kernel(tp_size // 2, *refs),
        out_shape=jax.ShapeDtypeStruct((rows, weight.shape[1]), jnp.bfloat16),
        in_specs=[pl.BlockSpec(memory_space=pltpu.VMEM)] * 2,
        out_specs=pl.BlockSpec(memory_space=pltpu.VMEM),
        scratch_shapes=[
            pltpu.VMEM((tp_size, halves, rows, width), jnp.bfloat16),
            pltpu.SemaphoreType.DMA((4, 2, tp_size // 4 + 1)),
            pltpu.SemaphoreType.DMA((tp_size, halves)),
        ],
        compiler_params=pltpu.CompilerParams(collective_id=3, has_side_effects=True),
    )(attn, weight)


def split_heads(rows):
    return rows.reshape(rows.shape[:-1] + (rows.shape[-1] // HD, HD))


def prompt_kernel(q_ref, k_ref, v_ref, seen_ref, o_ref, lse_ref):
    rows = q_ref.shape[0]
    heads = q_ref.shape[1] // HD
    visible = seen_ref[...] > 0.5
    column = lax.broadcasted_iota(jnp.int32, (rows, 128), 1)
    lse_cols = jnp.zeros((rows, 128), jnp.float32)
    for head in range(heads):
        cols = slice(head * HD, (head + 1) * HD)
        scores = lax.dot_general(
            q_ref[:, cols],
            k_ref[:, cols],
            (((1,), (1,)), ((), ())),
            preferred_element_type=jnp.float32,
        ) * (1.0 / math.sqrt(HD))
        scores = jnp.where(visible, scores, NEG_FILL)
        peaks = jnp.max(scores, axis=1, keepdims=True)
        raw = jnp.exp(scores - peaks)
        totals = jnp.sum(raw, axis=1, keepdims=True)
        accum = jnp.dot(raw.astype(jnp.bfloat16), v_ref[:, cols], preferred_element_type=jnp.float32)
        o_ref[:, cols] = (accum / totals).astype(o_ref.dtype)
        lse_cols = jnp.where(column == head, peaks + jnp.log(totals), lse_cols)
    lse_ref[...] = jnp.transpose(lse_cols)[0:8, :]


def prompt_attend(query_rows, key_rows, value_rows, seen):
    n_rows, cols = query_rows.shape
    n_keys = key_rows.shape[0]
    padded = -(-n_keys // 128) * 128
    key_rows = jnp.pad(key_rows, ((0, padded - n_keys), (0, 0)))
    value_rows = jnp.pad(value_rows, ((0, padded - n_keys), (0, 0)))
    seen_row = jnp.pad(seen.astype(jnp.float32), (0, padded - n_keys)).reshape(1, padded)
    block = 768
    return pl.pallas_call(
        prompt_kernel,
        out_shape=[
            jax.ShapeDtypeStruct((n_rows, cols), jnp.bfloat16),
            jax.ShapeDtypeStruct((8, n_rows), jnp.float32),
        ],
        grid=(n_rows // block,),
        in_specs=[
            pl.BlockSpec((block, cols), lambda i: (i, 0)),
            pl.BlockSpec((padded, cols), lambda i: (0, 0)),
            pl.BlockSpec((padded, cols), lambda i: (0, 0)),
            pl.BlockSpec((1, padded), lambda i: (0, 0)),
        ],
        out_specs=[
            pl.BlockSpec((block, cols), lambda i: (i, 0)),
            pl.BlockSpec((8, block), lambda i: (0, i)),
        ],
    )(query_rows, key_rows, value_rows, seen_row)


def tree_attend(queries, keys, values, seen):
    q = split_heads(queries)
    k = split_heads(keys)
    v = split_heads(values)
    scores = jnp.einsum("rthd,rshd->rhts", q, k, preferred_element_type=jnp.float32) * (
        1.0 / math.sqrt(HD)
    )
    scores = jnp.where(seen[:, None], scores, NEG_FILL)
    peaks = jnp.max(scores, axis=3, keepdims=True)
    raw = jnp.where(seen[:, None], jnp.exp(scores - peaks), 0.0)
    totals = jnp.sum(raw, axis=3)
    accum = jnp.einsum(
        "rhts,rshd->rthd", raw.astype(jnp.bfloat16), v, preferred_element_type=jnp.float32
    )
    return jnp.swapaxes(peaks[..., 0], 1, 2), jnp.swapaxes(totals, 1, 2), accum


def local(
    queries,
    tree_cache,
    tree_mask,
    dest_group,
    accepted_path,
    prompt_cache,
    first_len,
    spill_cache,
    spill_len,
    out_weight,
):
    req_here = queries.shape[0]
    local_cols = queries.shape[2]
    heads_here = local_cols // HD
    groups = lax.axis_size("rep")
    per_group = max(2, (req_here + groups - 1) // groups)
    n_slots = groups * per_group
    positions = jnp.arange(PCAP, dtype=jnp.int32)
    own_len = jnp.full((8, 128), spill_len[0], jnp.float32)

    target = dest_group[:, 0]
    same_target = target[:, None] == target[None, :]
    earlier = jnp.arange(req_here)[None, :] < jnp.arange(req_here)[:, None]
    rank_index = jnp.sum(jnp.logical_and(same_target, earlier), axis=1)
    slot_index = target * per_group + rank_index
    selector = (jnp.arange(n_slots, dtype=jnp.int32)[:, None] == slot_index[None, :]).astype(
        jnp.bfloat16
    )
    outbound = jnp.einsum(
        "sr,rtc->stc", selector, queries, preferred_element_type=jnp.float32
    ).astype(jnp.bfloat16)
    outbound = outbound.reshape(groups, per_group, TREE, local_cols)
    (inbound,), (partner_cache, partner_len) = exchange([outbound], 0, (spill_cache, own_len))
    routed_rows = inbound.reshape(n_slots * TREE, local_cols)

    key_rows = jnp.concatenate([prompt_cache[0, 0], partner_cache[0, 0]], axis=0)
    value_rows = jnp.concatenate([prompt_cache[0, 1], partner_cache[0, 1]], axis=0)
    seen = jnp.concatenate([positions < first_len[0], positions.astype(jnp.float32) < partner_len[0, 0]], axis=0)
    normed, lse = prompt_attend(routed_rows, key_rows, value_rows, seen)

    lse_width = per_group * TREE * heads_here
    lse_tile = -(-lse_width // 1024) * 1024
    lse = jnp.swapaxes(lse[:heads_here].reshape(heads_here, groups, per_group * TREE), 0, 1)
    lse_block = jnp.pad(lse.reshape(groups, lse_width), ((0, 0), (0, lse_tile - lse_width)))
    (back_out, back_lse), _ = exchange(
        [
            normed.reshape(groups, per_group, TREE, local_cols),
            lse_block.reshape(groups, lse_tile // 128, 128),
        ],
        1,
    )
    back_out = back_out.reshape(n_slots, TREE, local_cols)
    back_lse = back_lse.reshape(groups, lse_tile)[:, :lse_width]
    back_lse = jnp.moveaxis(back_lse.reshape(groups, heads_here, per_group, TREE), 1, 3)
    back_lse = back_lse.reshape(n_slots, TREE, heads_here)
    remote_out = split_heads(jnp.take(back_out, slot_index, axis=0)).astype(jnp.float32)
    remote_lse = jnp.take(back_lse, slot_index, axis=0)

    tree_max, tree_total, tree_accum = tree_attend(
        queries, tree_cache[:, 0], tree_cache[:, 1], tree_mask == 1
    )
    peaks = jnp.maximum(remote_lse, tree_max)
    factor_remote = jnp.exp(remote_lse - peaks)
    factor_tree = jnp.exp(tree_max - peaks)
    totals = factor_remote + tree_total * factor_tree
    accum = remote_out * factor_remote[..., None] + tree_accum * factor_tree[..., None]
    attn = jnp.moveaxis(accum / totals[..., None], 2, 0).astype(jnp.bfloat16)
    attn = attn.reshape(heads_here, req_here * TREE, HD)
    projected = gather_project(attn, out_weight).reshape(req_here, TREE, out_weight.shape[1])
    accepted_cache = jnp.take_along_axis(tree_cache, accepted_path[:, None, :, None], axis=2)
    return (projected, accepted_cache)


def solution(mesh):
    return jax.shard_map(
        local,
        mesh=mesh,
        in_specs=(
            P("rep", None, "tp"),
            P("rep", None, None, "tp"),
            P("rep", None, None),
            P("rep", None),
            P("rep", None),
            P("rep", None, None, "tp"),
            P("rep"),
            P("rep", None, None, "tp"),
            P("rep"),
            P(None, "tp"),
        ),
        out_specs=(P("rep", None, "tp"), P("rep", None, None, "tp")),
        check_vma=False,
    )
```

```python
import math

import jax
import jax.numpy as jnp
from jax import lax
from jax.experimental import pallas as pl
from jax.experimental.pallas import tpu as pltpu
from jax.sharding import PartitionSpec as P

MESH = pl.DeviceIdType.MESH

HD = 128
TREE = 48
PCAP = 152


NEG_FILL = -1e30


def exchange_kernel(n, count, paired, *refs):
    sources = refs[:count]
    pair_sources = refs[count : count + paired]
    targets = refs[count + paired : 2 * count + paired]
    pair_targets = refs[2 * count + paired : 2 * count + 2 * paired]
    send_sem, recv_sem, local_sem, pair_send, pair_recv = refs[2 * count + 2 * paired :]
    me = lax.axis_index("rep")
    partner = me + 1 - 2 * (me % 2)
    barrier = pltpu.get_barrier_semaphore()
    for offset in range(1, n):
        pl.semaphore_signal(
            barrier, inc=1, device_id={"rep": lax.rem(me + offset, n)}, device_id_type=MESH
        )
    pl.semaphore_wait(barrier, n - 1)
    copies = []
    for index in range(paired):
        remote = pltpu.make_async_remote_copy(
            src_ref=pair_sources[index],
            dst_ref=pair_targets[index],
            send_sem=pair_send.at[index],
            recv_sem=pair_recv.at[index],
            device_id={"rep": partner},
            device_id_type=MESH,
        )
        remote.start()
        copies.append(remote)
    for index in range(count):
        local = pltpu.make_async_copy(
            sources[index].at[me], targets[index].at[me], local_sem.at[index]
        )
        local.start()
        copies.append(local)
        for offset in range(1, n):
            peer = lax.rem(me + offset, n)
            remote = pltpu.make_async_remote_copy(
                src_ref=sources[index].at[peer],
                dst_ref=targets[index].at[me],
                send_sem=send_sem.at[index, offset],
                recv_sem=recv_sem.at[index, offset],
                device_id={"rep": peer},
                device_id_type=MESH,
            )
            remote.start()
            copies.append(remote)
    for copy in copies:
        copy.wait()


def exchange(arrays, tag, pairs=()):
    n = lax.axis_size("rep")
    count = len(arrays)
    paired = len(pairs)
    every = list(arrays) + list(pairs)
    outs = pl.pallas_call(
        lambda *refs: exchange_kernel(n, count, paired, *refs),
        out_shape=[jax.ShapeDtypeStruct(a.shape, a.dtype) for a in every],
        in_specs=[pl.BlockSpec(memory_space=pl.ANY)] * len(every),
        out_specs=[pl.BlockSpec(memory_space=pl.ANY)] * len(every),
        scratch_shapes=[
            pltpu.SemaphoreType.DMA((count, n)),
            pltpu.SemaphoreType.DMA((count, n)),
            pltpu.SemaphoreType.DMA((count,)),
            pltpu.SemaphoreType.DMA((max(paired, 1),)),
            pltpu.SemaphoreType.DMA((max(paired, 1),)),
        ],
        compiler_params=pltpu.CompilerParams(collective_id=tag, has_side_effects=True),
    )(*every)
    return outs[:count], outs[count:]


def gather_project_kernel(n_z, a_ref, w_ref, o_ref, slots, send_sem, recv_sem):
    me = lax.axis_index("tp")
    z = me // 2
    core = me % 2
    up = lax.rem(z + 1, n_z) * 2 + core
    down = lax.rem(z + n_z - 1, n_z) * 2 + core
    sibling = z * 2 + (1 - core)
    barrier = pltpu.get_barrier_semaphore()
    for peer in (up, down, sibling):
        pl.semaphore_signal(barrier, inc=1, device_id={"tp": peer}, device_id_type=MESH)
    pl.semaphore_wait(barrier, 3)
    slots[me] = a_ref[...]
    far = n_z // 2
    near = n_z - 1 - far
    chains = ((0, 1, up, down, far), (0, -1, down, up, near), (1, 1, up, down, near), (1, -1, down, up, far))
    width = a_ref.shape[2]
    halves = slots.shape[1]

    def product(slot, half, block):
        row = pl.multiple_of((slot * halves + half) * width, width)
        return jnp.dot(block, w_ref[pl.ds(row, width), :], preferred_element_type=jnp.float32)

    def arrival(slot, half, sender):
        pltpu.make_async_remote_copy(
            src_ref=slots.at[slot, half],
            dst_ref=slots.at[slot, half],
            send_sem=send_sem.at[0, 0, 0],
            recv_sem=recv_sem.at[slot, half],
            device_id={"tp": sender},
            device_id_type=MESH,
        ).wait_recv()

    total = jnp.zeros(o_ref.shape, jnp.float32)
    sends = []
    for step in range(far + 1):
        for chain, (half, direction, ahead, behind, hops) in enumerate(chains):
            if step > hops or (step == 0 and direction < 0):
                continue
            slot = lax.rem(z - step * direction + 2 * n_z, n_z) * 2 + core
            if step == 0:
                source = a_ref.at[half]
            else:
                arrival(slot, half, behind)
                source = slots.at[slot, half]
            targets = [(1, sibling)]
            if step < hops:
                targets = [(0, ahead)] + targets
            if step == 0:
                targets = targets + [(0, down)]
            for kind, peer in targets:
                copy = pltpu.make_async_remote_copy(
                    src_ref=source,
                    dst_ref=slots.at[slot, half],
                    send_sem=send_sem.at[chain + (1 if peer is down and step == 0 else 0), kind, step],
                    recv_sem=recv_sem.at[slot, half],
                    device_id={"tp": peer},
                    device_id_type=MESH,
                )
                copy.start()
                sends.append(copy)
            total = total + product(slot, half, source[...])
    for half, direction, ahead, behind, hops in chains:
        for step in range(hops + 1):
            if step == 0 and direction < 0:
                continue
            slot = lax.rem(z - step * direction + 2 * n_z, n_z) * 2 + (1 - core)
            arrival(slot, half, sibling)
            total = total + product(slot, half, slots[slot, half])
    for copy in sends:
        copy.wait_send()
    o_ref[...] = total.astype(o_ref.dtype)


def gather_project(attn, weight):
    tp_size = lax.axis_size("tp")
    halves, rows, width = attn.shape
    return pl.pallas_call(
        lambda *refs: gather_project_kernel(tp_size // 2, *refs),
        out_shape=jax.ShapeDtypeStruct((rows, weight.shape[1]), jnp.bfloat16),
        in_specs=[pl.BlockSpec(memory_space=pltpu.VMEM)] * 2,
        out_specs=pl.BlockSpec(memory_space=pltpu.VMEM),
        scratch_shapes=[
            pltpu.VMEM((tp_size, halves, rows, width), jnp.bfloat16),
            pltpu.SemaphoreType.DMA((4, 2, tp_size // 4 + 1)),
            pltpu.SemaphoreType.DMA((tp_size, halves)),
        ],
        compiler_params=pltpu.CompilerParams(collective_id=3, has_side_effects=True),
    )(attn, weight)


def split_heads(rows):
    return rows.reshape(rows.shape[:-1] + (rows.shape[-1] // HD, HD))


def prompt_kernel(q_ref, k_ref, v_ref, seen_ref, o_ref, lse_ref):
    rows = q_ref.shape[0]
    heads = q_ref.shape[1] // HD
    visible = seen_ref[...] > 0.5
    column = lax.broadcasted_iota(jnp.int32, (rows, 128), 1)
    lse_cols = jnp.zeros((rows, 128), jnp.float32)
    for head in range(heads):
        cols = slice(head * HD, (head + 1) * HD)
        scores = lax.dot_general(
            q_ref[:, cols],
            k_ref[:, cols],
            (((1,), (1,)), ((), ())),
            preferred_element_type=jnp.float32,
        ) * (1.0 / math.sqrt(HD))
        scores = jnp.where(visible, scores, NEG_FILL)
        peaks = jnp.max(scores, axis=1, keepdims=True)
        raw = jnp.exp(scores - peaks)
        totals = jnp.sum(raw, axis=1, keepdims=True)
        accum = jnp.dot(raw.astype(jnp.bfloat16), v_ref[:, cols], preferred_element_type=jnp.float32)
        o_ref[:, cols] = (accum / totals).astype(o_ref.dtype)
        lse_cols = jnp.where(column == head, peaks + jnp.log(totals), lse_cols)
    lse_ref[...] = jnp.transpose(lse_cols)[0:8, :]


def prompt_attend(query_rows, key_rows, value_rows, seen):
    n_rows, cols = query_rows.shape
    n_keys = key_rows.shape[0]
    padded = -(-n_keys // 128) * 128
    key_rows = jnp.pad(key_rows, ((0, padded - n_keys), (0, 0)))
    value_rows = jnp.pad(value_rows, ((0, padded - n_keys), (0, 0)))
    seen_row = jnp.pad(seen.astype(jnp.float32), (0, padded - n_keys)).reshape(1, padded)
    block = 768
    return pl.pallas_call(
        prompt_kernel,
        out_shape=[
            jax.ShapeDtypeStruct((n_rows, cols), jnp.bfloat16),
            jax.ShapeDtypeStruct((8, n_rows), jnp.float32),
        ],
        grid=(n_rows // block,),
        in_specs=[
            pl.BlockSpec((block, cols), lambda i: (i, 0)),
            pl.BlockSpec((padded, cols), lambda i: (0, 0)),
            pl.BlockSpec((padded, cols), lambda i: (0, 0)),
            pl.BlockSpec((1, padded), lambda i: (0, 0)),
        ],
        out_specs=[
            pl.BlockSpec((block, cols), lambda i: (i, 0)),
            pl.BlockSpec((8, block), lambda i: (0, i)),
        ],
    )(query_rows, key_rows, value_rows, seen_row)


def tree_attend(queries, keys, values, seen):
    q = split_heads(queries)
    k = split_heads(keys)
    v = split_heads(values)
    scores = jnp.einsum("rthd,rshd->rhts", q, k, preferred_element_type=jnp.float32) * (
        1.0 / math.sqrt(HD)
    )
    scores = jnp.where(seen[:, None], scores, NEG_FILL)
    peaks = jnp.max(scores, axis=3, keepdims=True)
    raw = jnp.where(seen[:, None], jnp.exp(scores - peaks), 0.0)
    totals = jnp.sum(raw, axis=3)
    accum = jnp.einsum(
        "rhts,rshd->rthd", raw.astype(jnp.bfloat16), v, preferred_element_type=jnp.float32
    )
    return jnp.swapaxes(peaks[..., 0], 1, 2), jnp.swapaxes(totals, 1, 2), accum


def local(
    queries,
    tree_cache,
    tree_mask,
    dest_group,
    accepted_path,
    prompt_cache,
    first_len,
    spill_cache,
    spill_len,
    out_weight,
):
    req_here = queries.shape[0]
    local_cols = queries.shape[2]
    heads_here = local_cols // HD
    groups = lax.axis_size("rep")
    per_group = max(2, (req_here + groups - 1) // groups)
    n_slots = groups * per_group
    positions = jnp.arange(PCAP, dtype=jnp.int32)
    own_len = jnp.full((8, 128), spill_len[0], jnp.float32)

    target = dest_group[:, 0]
    same_target = target[:, None] == target[None, :]
    earlier = jnp.arange(req_here)[None, :] < jnp.arange(req_here)[:, None]
    rank_index = jnp.sum(jnp.logical_and(same_target, earlier), axis=1)
    slot_index = target * per_group + rank_index
    slot_source = (
        jnp.full((n_slots,), req_here, jnp.int32).at[slot_index].set(jnp.arange(req_here, dtype=jnp.int32))
    )
    padded_queries = jnp.concatenate([queries, jnp.zeros((1,) + queries.shape[1:], queries.dtype)], 0)
    outbound = jnp.take(padded_queries, slot_source, axis=0, mode="clip")
    outbound = outbound.reshape(groups, per_group, TREE, local_cols)
    (inbound,), (partner_cache, partner_len) = exchange([outbound], 0, (spill_cache, own_len))
    routed_rows = inbound.reshape(n_slots * TREE, local_cols)

    key_rows = jnp.concatenate([prompt_cache[0, 0], partner_cache[0, 0]], axis=0)
    value_rows = jnp.concatenate([prompt_cache[0, 1], partner_cache[0, 1]], axis=0)
    seen = jnp.concatenate([positions < first_len[0], positions.astype(jnp.float32) < partner_len[0, 0]], axis=0)
    normed, lse = prompt_attend(routed_rows, key_rows, value_rows, seen)

    lse_width = per_group * TREE * heads_here
    lse_tile = -(-lse_width // 1024) * 1024
    lse = jnp.swapaxes(lse[:heads_here].reshape(heads_here, groups, per_group * TREE), 0, 1)
    lse_block = jnp.pad(lse.reshape(groups, lse_width), ((0, 0), (0, lse_tile - lse_width)))
    (back_out, back_lse), _ = exchange(
        [
            normed.reshape(groups, per_group, TREE, local_cols),
            lse_block.reshape(groups, lse_tile // 128, 128),
        ],
        1,
    )
    back_out = back_out.reshape(n_slots, TREE, local_cols)
    back_lse = back_lse.reshape(groups, lse_tile)[:, :lse_width]
    back_lse = jnp.moveaxis(back_lse.reshape(groups, heads_here, per_group, TREE), 1, 3)
    back_lse = back_lse.reshape(n_slots, TREE, heads_here)
    remote_out = split_heads(jnp.take(back_out, slot_index, axis=0)).astype(jnp.float32)
    remote_lse = jnp.take(back_lse, slot_index, axis=0)

    tree_max, tree_total, tree_accum = tree_attend(
        queries, tree_cache[:, 0], tree_cache[:, 1], tree_mask == 1
    )
    peaks = jnp.maximum(remote_lse, tree_max)
    factor_remote = jnp.exp(remote_lse - peaks)
    factor_tree = jnp.exp(tree_max - peaks)
    totals = factor_remote + tree_total * factor_tree
    accum = remote_out * factor_remote[..., None] + tree_accum * factor_tree[..., None]
    attn = jnp.moveaxis(accum / totals[..., None], 2, 0).astype(jnp.bfloat16)
    attn = attn.reshape(heads_here, req_here * TREE, HD)
    projected = gather_project(attn, out_weight).reshape(req_here, TREE, out_weight.shape[1])
    accepted_cache = jnp.take_along_axis(tree_cache, accepted_path[:, None, :, None], axis=2)
    return (projected, accepted_cache)


def solution(mesh):
    return jax.shard_map(
        local,
        mesh=mesh,
        in_specs=(
            P("rep", None, "tp"),
            P("rep", None, None, "tp"),
            P("rep", None, None),
            P("rep", None),
            P("rep", None),
            P("rep", None, None, "tp"),
            P("rep"),
            P("rep", None, None, "tp"),
            P("rep"),
            P(None, "tp"),
        ),
        out_specs=(P("rep", None, "tp"), P("rep", None, None, "tp")),
        check_vma=False,
    )
```

```python
import math

import jax
import jax.numpy as jnp
from jax import lax
from jax.experimental import pallas as pl
from jax.experimental.pallas import tpu as pltpu
from jax.sharding import PartitionSpec as P

MESH = pl.DeviceIdType.MESH

HD = 128
TREE = 48
PCAP = 152


NEG_FILL = -1e30


def exchange_kernel(n, count, paired, *refs):
    sources = refs[:count]
    pair_sources = refs[count : count + paired]
    targets = refs[count + paired : 2 * count + paired]
    pair_targets = refs[2 * count + paired : 2 * count + 2 * paired]
    send_sem, recv_sem, local_sem, pair_send, pair_recv = refs[2 * count + 2 * paired :]
    me = lax.axis_index("rep")
    partner = me + 1 - 2 * (me % 2)
    barrier = pltpu.get_barrier_semaphore()
    for offset in range(1, n):
        pl.semaphore_signal(
            barrier, inc=1, device_id={"rep": lax.rem(me + offset, n)}, device_id_type=MESH
        )
    pl.semaphore_wait(barrier, n - 1)
    copies = []
    for index in range(paired):
        remote = pltpu.make_async_remote_copy(
            src_ref=pair_sources[index],
            dst_ref=pair_targets[index],
            send_sem=pair_send.at[index],
            recv_sem=pair_recv.at[index],
            device_id={"rep": partner},
            device_id_type=MESH,
        )
        remote.start()
        copies.append(remote)
    for index in range(count):
        local = pltpu.make_async_copy(
            sources[index].at[me], targets[index].at[me], local_sem.at[index]
        )
        local.start()
        copies.append(local)
        for offset in range(1, n):
            peer = lax.rem(me + offset, n)
            remote = pltpu.make_async_remote_copy(
                src_ref=sources[index].at[peer],
                dst_ref=targets[index].at[me],
                send_sem=send_sem.at[index, offset],
                recv_sem=recv_sem.at[index, offset],
                device_id={"rep": peer},
                device_id_type=MESH,
            )
            remote.start()
            copies.append(remote)
    for copy in copies:
        copy.wait()


def exchange(arrays, tag, pairs=()):
    n = lax.axis_size("rep")
    count = len(arrays)
    paired = len(pairs)
    every = list(arrays) + list(pairs)
    outs = pl.pallas_call(
        lambda *refs: exchange_kernel(n, count, paired, *refs),
        out_shape=[jax.ShapeDtypeStruct(a.shape, a.dtype) for a in every],
        in_specs=[pl.BlockSpec(memory_space=pl.ANY)] * len(every),
        out_specs=[pl.BlockSpec(memory_space=pl.ANY)] * len(every),
        scratch_shapes=[
            pltpu.SemaphoreType.DMA((count, n)),
            pltpu.SemaphoreType.DMA((count, n)),
            pltpu.SemaphoreType.DMA((count,)),
            pltpu.SemaphoreType.DMA((max(paired, 1),)),
            pltpu.SemaphoreType.DMA((max(paired, 1),)),
        ],
        compiler_params=pltpu.CompilerParams(collective_id=tag, has_side_effects=True),
    )(*every)
    return outs[:count], outs[count:]


def gather_project_kernel(n_z, a_ref, w_ref, o_ref, slots, send_sem, recv_sem):
    me = lax.axis_index("tp")
    z = me // 2
    core = me % 2
    up = lax.rem(z + 1, n_z) * 2 + core
    down = lax.rem(z + n_z - 1, n_z) * 2 + core
    sibling = z * 2 + (1 - core)
    barrier = pltpu.get_barrier_semaphore()
    for peer in (up, down, sibling):
        pl.semaphore_signal(barrier, inc=1, device_id={"tp": peer}, device_id_type=MESH)
    pl.semaphore_wait(barrier, 3)
    slots[me] = a_ref[...]
    far = n_z // 2
    near = n_z - 1 - far
    chains = ((0, 1, up, down, far), (0, -1, down, up, near), (1, 1, up, down, near), (1, -1, down, up, far))
    width = a_ref.shape[2]
    halves = slots.shape[1]

    def product(slot, half, block):
        row = pl.multiple_of((slot * halves + half) * width, width)
        return jnp.dot(block, w_ref[pl.ds(row, width), :], preferred_element_type=jnp.float32)

    def arrival(slot, half, sender):
        pltpu.make_async_remote_copy(
            src_ref=slots.at[slot, half],
            dst_ref=slots.at[slot, half],
            send_sem=send_sem.at[0, 0, 0],
            recv_sem=recv_sem.at[slot, half],
            device_id={"tp": sender},
            device_id_type=MESH,
        ).wait_recv()

    total = jnp.zeros(o_ref.shape, jnp.float32)
    sends = []
    for step in range(far + 1):
        for chain, (half, direction, ahead, behind, hops) in enumerate(chains):
            if step > hops or (step == 0 and direction < 0):
                continue
            slot = lax.rem(z - step * direction + 2 * n_z, n_z) * 2 + core
            if step == 0:
                source = a_ref.at[half]
            else:
                arrival(slot, half, behind)
                source = slots.at[slot, half]
            targets = [(1, sibling)]
            if step < hops:
                targets = [(0, ahead)] + targets
            if step == 0:
                targets = targets + [(0, down)]
            for kind, peer in targets:
                copy = pltpu.make_async_remote_copy(
                    src_ref=source,
                    dst_ref=slots.at[slot, half],
                    send_sem=send_sem.at[chain + (1 if peer is down and step == 0 else 0), kind, step],
                    recv_sem=recv_sem.at[slot, half],
                    device_id={"tp": peer},
                    device_id_type=MESH,
                )
                copy.start()
                sends.append(copy)
            total = total + product(slot, half, source[...])
    for half, direction, ahead, behind, hops in chains:
        for step in range(hops + 1):
            if step == 0 and direction < 0:
                continue
            slot = lax.rem(z - step * direction + 2 * n_z, n_z) * 2 + (1 - core)
            arrival(slot, half, sibling)
            total = total + product(slot, half, slots[slot, half])
    for copy in sends:
        copy.wait_send()
    o_ref[...] = total.astype(o_ref.dtype)


def gather_project(attn, weight):
    tp_size = lax.axis_size("tp")
    halves, rows, width = attn.shape
    return pl.pallas_call(
        lambda *refs: gather_project_kernel(tp_size // 2, *refs),
        out_shape=jax.ShapeDtypeStruct((rows, weight.shape[1]), jnp.bfloat16),
        in_specs=[pl.BlockSpec(memory_space=pltpu.VMEM)] * 2,
        out_specs=pl.BlockSpec(memory_space=pltpu.VMEM),
        scratch_shapes=[
            pltpu.VMEM((tp_size, halves, rows, width), jnp.bfloat16),
            pltpu.SemaphoreType.DMA((4, 2, tp_size // 4 + 1)),
            pltpu.SemaphoreType.DMA((tp_size, halves)),
        ],
        compiler_params=pltpu.CompilerParams(collective_id=3, has_side_effects=True),
    )(attn, weight)


def split_heads(rows):
    return rows.reshape(rows.shape[:-1] + (rows.shape[-1] // HD, HD))


def prompt_kernel(q_ref, k_ref, v_ref, seen_ref, o_ref, lse_ref):
    rows = q_ref.shape[0]
    heads = q_ref.shape[1] // HD
    visible = seen_ref[...] > 0.5
    column = lax.broadcasted_iota(jnp.int32, (rows, 128), 1)
    lse_cols = jnp.zeros((rows, 128), jnp.float32)
    for head in range(heads):
        cols = slice(head * HD, (head + 1) * HD)
        scores = lax.dot_general(
            q_ref[:, cols],
            k_ref[:, cols],
            (((1,), (1,)), ((), ())),
            preferred_element_type=jnp.float32,
        ) * (1.0 / math.sqrt(HD))
        scores = jnp.where(visible, scores, NEG_FILL)
        peaks = jnp.max(scores, axis=1, keepdims=True)
        raw = jnp.exp(scores - peaks)
        totals = jnp.sum(raw, axis=1, keepdims=True)
        accum = jnp.dot(raw.astype(jnp.bfloat16), v_ref[:, cols], preferred_element_type=jnp.float32)
        o_ref[:, cols] = (accum / totals).astype(o_ref.dtype)
        lse_cols = jnp.where(column == head, peaks + jnp.log(totals), lse_cols)
    lse_ref[...] = jnp.transpose(lse_cols)[0:8, :]


def prompt_attend(query_rows, key_rows, value_rows, seen):
    n_rows, cols = query_rows.shape
    n_keys = key_rows.shape[0]
    padded = -(-n_keys // 128) * 128
    key_rows = jnp.pad(key_rows, ((0, padded - n_keys), (0, 0)))
    value_rows = jnp.pad(value_rows, ((0, padded - n_keys), (0, 0)))
    seen_row = jnp.pad(seen.astype(jnp.float32), (0, padded - n_keys)).reshape(1, padded)
    block = 1536
    return pl.pallas_call(
        prompt_kernel,
        out_shape=[
            jax.ShapeDtypeStruct((n_rows, cols), jnp.bfloat16),
            jax.ShapeDtypeStruct((8, n_rows), jnp.float32),
        ],
        grid=(n_rows // block,),
        in_specs=[
            pl.BlockSpec((block, cols), lambda i: (i, 0)),
            pl.BlockSpec((padded, cols), lambda i: (0, 0)),
            pl.BlockSpec((padded, cols), lambda i: (0, 0)),
            pl.BlockSpec((1, padded), lambda i: (0, 0)),
        ],
        out_specs=[
            pl.BlockSpec((block, cols), lambda i: (i, 0)),
            pl.BlockSpec((8, block), lambda i: (0, i)),
        ],
    )(query_rows, key_rows, value_rows, seen_row)


def tree_attend(queries, keys, values, seen):
    q = split_heads(queries)
    k = split_heads(keys)
    v = split_heads(values)
    scores = jnp.einsum("rthd,rshd->rhts", q, k, preferred_element_type=jnp.float32) * (
        1.0 / math.sqrt(HD)
    )
    scores = jnp.where(seen[:, None], scores, NEG_FILL)
    peaks = jnp.max(scores, axis=3, keepdims=True)
    raw = jnp.where(seen[:, None], jnp.exp(scores - peaks), 0.0)
    totals = jnp.sum(raw, axis=3)
    accum = jnp.einsum(
        "rhts,rshd->rthd", raw.astype(jnp.bfloat16), v, preferred_element_type=jnp.float32
    )
    return jnp.swapaxes(peaks[..., 0], 1, 2), jnp.swapaxes(totals, 1, 2), accum


def local(
    queries,
    tree_cache,
    tree_mask,
    dest_group,
    accepted_path,
    prompt_cache,
    first_len,
    spill_cache,
    spill_len,
    out_weight,
):
    req_here = queries.shape[0]
    local_cols = queries.shape[2]
    heads_here = local_cols // HD
    groups = lax.axis_size("rep")
    per_group = max(2, (req_here + groups - 1) // groups)
    n_slots = groups * per_group
    positions = jnp.arange(PCAP, dtype=jnp.int32)
    own_len = jnp.full((8, 128), spill_len[0], jnp.float32)

    target = dest_group[:, 0]
    same_target = target[:, None] == target[None, :]
    earlier = jnp.arange(req_here)[None, :] < jnp.arange(req_here)[:, None]
    rank_index = jnp.sum(jnp.logical_and(same_target, earlier), axis=1)
    slot_index = target * per_group + rank_index
    selector = (jnp.arange(n_slots, dtype=jnp.int32)[:, None] == slot_index[None, :]).astype(
        jnp.bfloat16
    )
    outbound = jnp.einsum(
        "sr,rtc->stc", selector, queries, preferred_element_type=jnp.float32
    ).astype(jnp.bfloat16)
    outbound = outbound.reshape(groups, per_group, TREE, local_cols)
    (inbound,), (partner_cache, partner_len) = exchange([outbound], 0, (spill_cache, own_len))
    routed_rows = inbound.reshape(n_slots * TREE, local_cols)

    key_rows = jnp.concatenate([prompt_cache[0, 0], partner_cache[0, 0]], axis=0)
    value_rows = jnp.concatenate([prompt_cache[0, 1], partner_cache[0, 1]], axis=0)
    seen = jnp.concatenate([positions < first_len[0], positions.astype(jnp.float32) < partner_len[0, 0]], axis=0)
    normed, lse = prompt_attend(routed_rows, key_rows, value_rows, seen)

    lse_width = per_group * TREE * heads_here
    lse_tile = -(-lse_width // 1024) * 1024
    lse = jnp.swapaxes(lse[:heads_here].reshape(heads_here, groups, per_group * TREE), 0, 1)
    lse_block = jnp.pad(lse.reshape(groups, lse_width), ((0, 0), (0, lse_tile - lse_width)))
    (back_out, back_lse), _ = exchange(
        [
            normed.reshape(groups, per_group, TREE, local_cols),
            lse_block.reshape(groups, lse_tile // 128, 128),
        ],
        1,
    )
    back_out = back_out.reshape(n_slots, TREE, local_cols)
    back_lse = back_lse.reshape(groups, lse_tile)[:, :lse_width]
    back_lse = jnp.moveaxis(back_lse.reshape(groups, heads_here, per_group, TREE), 1, 3)
    back_lse = back_lse.reshape(n_slots, TREE, heads_here)
    remote_out = split_heads(jnp.take(back_out, slot_index, axis=0)).astype(jnp.float32)
    remote_lse = jnp.take(back_lse, slot_index, axis=0)

    tree_max, tree_total, tree_accum = tree_attend(
        queries, tree_cache[:, 0], tree_cache[:, 1], tree_mask == 1
    )
    peaks = jnp.maximum(remote_lse, tree_max)
    factor_remote = jnp.exp(remote_lse - peaks)
    factor_tree = jnp.exp(tree_max - peaks)
    totals = factor_remote + tree_total * factor_tree
    accum = remote_out * factor_remote[..., None] + tree_accum * factor_tree[..., None]
    attn = jnp.moveaxis(accum / totals[..., None], 2, 0).astype(jnp.bfloat16)
    attn = attn.reshape(heads_here, req_here * TREE, HD)
    projected = gather_project(attn, out_weight).reshape(req_here, TREE, out_weight.shape[1])
    accepted_cache = jnp.take_along_axis(tree_cache, accepted_path[:, None, :, None], axis=2)
    return (projected, accepted_cache)


def solution(mesh):
    return jax.shard_map(
        local,
        mesh=mesh,
        in_specs=(
            P("rep", None, "tp"),
            P("rep", None, None, "tp"),
            P("rep", None, None),
            P("rep", None),
            P("rep", None),
            P("rep", None, None, "tp"),
            P("rep"),
            P("rep", None, None, "tp"),
            P("rep"),
            P(None, "tp"),
        ),
        out_specs=(P("rep", None, "tp"), P("rep", None, None, "tp")),
        check_vma=False,
    )
```

```python
import math

import jax
import jax.numpy as jnp
from jax import lax
from jax.experimental import pallas as pl
from jax.experimental.pallas import tpu as pltpu
from jax.sharding import PartitionSpec as P

MESH = pl.DeviceIdType.MESH

HD = 128
TREE = 48
PCAP = 152


NEG_FILL = -1e30


def exchange_kernel(n, count, paired, *refs):
    sources = refs[:count]
    pair_sources = refs[count : count + paired]
    targets = refs[count + paired : 2 * count + paired]
    pair_targets = refs[2 * count + paired : 2 * count + 2 * paired]
    send_sem, recv_sem, local_sem, pair_send, pair_recv = refs[2 * count + 2 * paired :]
    me = lax.axis_index("rep")
    partner = me + 1 - 2 * (me % 2)
    barrier = pltpu.get_barrier_semaphore()
    for offset in range(1, n):
        pl.semaphore_signal(
            barrier, inc=1, device_id={"rep": lax.rem(me + offset, n)}, device_id_type=MESH
        )
    pl.semaphore_wait(barrier, n - 1)
    copies = []
    for index in range(paired):
        remote = pltpu.make_async_remote_copy(
            src_ref=pair_sources[index],
            dst_ref=pair_targets[index],
            send_sem=pair_send.at[index],
            recv_sem=pair_recv.at[index],
            device_id={"rep": partner},
            device_id_type=MESH,
        )
        remote.start()
        copies.append(remote)
    for index in range(count):
        local = pltpu.make_async_copy(
            sources[index].at[me], targets[index].at[me], local_sem.at[index]
        )
        local.start()
        copies.append(local)
        for offset in range(1, n):
            peer = lax.rem(me + offset, n)
            remote = pltpu.make_async_remote_copy(
                src_ref=sources[index].at[peer],
                dst_ref=targets[index].at[me],
                send_sem=send_sem.at[index, offset],
                recv_sem=recv_sem.at[index, offset],
                device_id={"rep": peer},
                device_id_type=MESH,
            )
            remote.start()
            copies.append(remote)
    for copy in copies:
        copy.wait()


def exchange(arrays, tag, pairs=()):
    n = lax.axis_size("rep")
    count = len(arrays)
    paired = len(pairs)
    every = list(arrays) + list(pairs)
    outs = pl.pallas_call(
        lambda *refs: exchange_kernel(n, count, paired, *refs),
        out_shape=[jax.ShapeDtypeStruct(a.shape, a.dtype) for a in every],
        in_specs=[pl.BlockSpec(memory_space=pl.ANY)] * len(every),
        out_specs=[pl.BlockSpec(memory_space=pl.ANY)] * len(every),
        scratch_shapes=[
            pltpu.SemaphoreType.DMA((count, n)),
            pltpu.SemaphoreType.DMA((count, n)),
            pltpu.SemaphoreType.DMA((count,)),
            pltpu.SemaphoreType.DMA((max(paired, 1),)),
            pltpu.SemaphoreType.DMA((max(paired, 1),)),
        ],
        compiler_params=pltpu.CompilerParams(collective_id=tag, has_side_effects=True),
    )(*every)
    return outs[:count], outs[count:]


def gather_project_kernel(n_z, a_ref, w_ref, o_ref, slots, send_sem, recv_sem):
    me = lax.axis_index("tp")
    z = me // 2
    core = me % 2
    up = lax.rem(z + 1, n_z) * 2 + core
    down = lax.rem(z + n_z - 1, n_z) * 2 + core
    sibling = z * 2 + (1 - core)
    barrier = pltpu.get_barrier_semaphore()
    for peer in (up, down, sibling):
        pl.semaphore_signal(barrier, inc=1, device_id={"tp": peer}, device_id_type=MESH)
    pl.semaphore_wait(barrier, 3)
    slots[me] = a_ref[...]
    far = n_z // 2
    near = n_z - 1 - far
    chains = ((0, 1, up, down, far), (0, -1, down, up, near), (1, 1, up, down, near), (1, -1, down, up, far))
    width = a_ref.shape[2]
    halves = slots.shape[1]

    def product(slot, half, block):
        row = pl.multiple_of((slot * halves + half) * width, width)
        return jnp.dot(block, w_ref[pl.ds(row, width), :], preferred_element_type=jnp.float32)

    def arrival(slot, half, sender):
        pltpu.make_async_remote_copy(
            src_ref=slots.at[slot, half],
            dst_ref=slots.at[slot, half],
            send_sem=send_sem.at[0, 0, 0],
            recv_sem=recv_sem.at[slot, half],
            device_id={"tp": sender},
            device_id_type=MESH,
        ).wait_recv()

    total = jnp.zeros(o_ref.shape, jnp.float32)
    sends = []
    for step in range(far + 1):
        for chain, (half, direction, ahead, behind, hops) in enumerate(chains):
            if step > hops or (step == 0 and direction < 0):
                continue
            slot = lax.rem(z - step * direction + 2 * n_z, n_z) * 2 + core
            if step == 0:
                source = a_ref.at[half]
            else:
                arrival(slot, half, behind)
                source = slots.at[slot, half]
            targets = [(1, sibling)]
            if step < hops:
                targets = [(0, ahead)] + targets
            if step == 0:
                targets = targets + [(0, down)]
            for kind, peer in targets:
                copy = pltpu.make_async_remote_copy(
                    src_ref=source,
                    dst_ref=slots.at[slot, half],
                    send_sem=send_sem.at[chain + (1 if peer is down and step == 0 else 0), kind, step],
                    recv_sem=recv_sem.at[slot, half],
                    device_id={"tp": peer},
                    device_id_type=MESH,
                )
                copy.start()
                sends.append(copy)
            total = total + product(slot, half, source[...])
    for half, direction, ahead, behind, hops in chains:
        for step in range(hops + 1):
            if step == 0 and direction < 0:
                continue
            slot = lax.rem(z - step * direction + 2 * n_z, n_z) * 2 + (1 - core)
            arrival(slot, half, sibling)
            total = total + product(slot, half, slots[slot, half])
    for copy in sends:
        copy.wait_send()
    o_ref[...] = total.astype(o_ref.dtype)


def gather_project(attn, weight):
    tp_size = lax.axis_size("tp")
    halves, rows, width = attn.shape
    return pl.pallas_call(
        lambda *refs: gather_project_kernel(tp_size // 2, *refs),
        out_shape=jax.ShapeDtypeStruct((rows, weight.shape[1]), jnp.bfloat16),
        in_specs=[pl.BlockSpec(memory_space=pltpu.VMEM)] * 2,
        out_specs=pl.BlockSpec(memory_space=pltpu.VMEM),
        scratch_shapes=[
            pltpu.VMEM((tp_size, halves, rows, width), jnp.bfloat16),
            pltpu.SemaphoreType.DMA((4, 2, tp_size // 4 + 1)),
            pltpu.SemaphoreType.DMA((tp_size, halves)),
        ],
        compiler_params=pltpu.CompilerParams(collective_id=3, has_side_effects=True),
    )(attn, weight)


def split_heads(rows):
    return rows.reshape(rows.shape[:-1] + (rows.shape[-1] // HD, HD))


def prompt_kernel(q_ref, k_ref, v_ref, seen_ref, o_ref, lse_ref):
    rows = q_ref.shape[0]
    heads = q_ref.shape[1] // HD
    visible = seen_ref[...] > 0.5
    column = lax.broadcasted_iota(jnp.int32, (rows, 128), 1)
    lse_cols = jnp.zeros((rows, 128), jnp.float32)
    for head in range(heads):
        cols = slice(head * HD, (head + 1) * HD)
        scores = lax.dot_general(
            q_ref[:, cols],
            k_ref[:, cols],
            (((1,), (1,)), ((), ())),
            preferred_element_type=jnp.float32,
        ) * (1.0 / math.sqrt(HD))
        scores = jnp.where(visible, scores, NEG_FILL)
        peaks = jnp.max(scores, axis=1, keepdims=True)
        raw = jnp.exp(scores - peaks)
        totals = jnp.sum(raw, axis=1, keepdims=True)
        accum = jnp.dot(raw.astype(jnp.bfloat16), v_ref[:, cols], preferred_element_type=jnp.float32)
        o_ref[:, cols] = (accum / totals).astype(o_ref.dtype)
        lse_cols = jnp.where(column == head, peaks + jnp.log(totals), lse_cols)
    lse_ref[...] = jnp.transpose(lse_cols)[0:8, :]


def prompt_attend(query_rows, key_rows, value_rows, seen):
    n_rows, cols = query_rows.shape
    n_keys = key_rows.shape[0]
    padded = -(-n_keys // 128) * 128
    key_rows = jnp.pad(key_rows, ((0, padded - n_keys), (0, 0)))
    value_rows = jnp.pad(value_rows, ((0, padded - n_keys), (0, 0)))
    seen_row = jnp.pad(seen.astype(jnp.float32), (0, padded - n_keys)).reshape(1, padded)
    block = 768
    return pl.pallas_call(
        prompt_kernel,
        out_shape=[
            jax.ShapeDtypeStruct((n_rows, cols), jnp.bfloat16),
            jax.ShapeDtypeStruct((8, n_rows), jnp.float32),
        ],
        grid=(n_rows // block,),
        in_specs=[
            pl.BlockSpec((block, cols), lambda i: (i, 0)),
            pl.BlockSpec((padded, cols), lambda i: (0, 0)),
            pl.BlockSpec((padded, cols), lambda i: (0, 0)),
            pl.BlockSpec((1, padded), lambda i: (0, 0)),
        ],
        out_specs=[
            pl.BlockSpec((block, cols), lambda i: (i, 0)),
            pl.BlockSpec((8, block), lambda i: (0, i)),
        ],
    )(query_rows, key_rows, value_rows, seen_row)


def tree_attend(queries, keys, values, seen):
    q = split_heads(queries)
    k = split_heads(keys)
    v = split_heads(values)
    scores = jnp.einsum("rthd,rshd->rhts", q, k, preferred_element_type=jnp.float32) * (
        1.0 / math.sqrt(HD)
    )
    scores = jnp.where(seen[:, None], scores, NEG_FILL)
    peaks = jnp.max(scores, axis=3, keepdims=True)
    raw = jnp.where(seen[:, None], jnp.exp(scores - peaks), 0.0)
    totals = jnp.sum(raw, axis=3)
    accum = jnp.einsum(
        "rhts,rshd->rthd", raw.astype(jnp.bfloat16), v, preferred_element_type=jnp.float32
    )
    return jnp.swapaxes(peaks[..., 0], 1, 2), jnp.swapaxes(totals, 1, 2), accum


def local(
    queries,
    tree_cache,
    tree_mask,
    dest_group,
    accepted_path,
    prompt_cache,
    first_len,
    spill_cache,
    spill_len,
    out_weight,
):
    req_here = queries.shape[0]
    local_cols = queries.shape[2]
    heads_here = local_cols // HD
    groups = lax.axis_size("rep")
    per_group = max(2, (req_here + groups - 1) // groups)
    n_slots = groups * per_group
    positions = jnp.arange(PCAP, dtype=jnp.int32)
    own_len = jnp.full((8, 128), spill_len[0], jnp.float32)

    target = dest_group[:, 0]
    same_target = target[:, None] == target[None, :]
    earlier = jnp.arange(req_here)[None, :] < jnp.arange(req_here)[:, None]
    rank_index = jnp.sum(jnp.logical_and(same_target, earlier), axis=1)
    slot_index = target * per_group + rank_index
    selector = (jnp.arange(n_slots, dtype=jnp.int32)[:, None] == slot_index[None, :]).astype(
        jnp.bfloat16
    )
    outbound = jnp.einsum(
        "sr,rtc->stc", selector, queries, preferred_element_type=jnp.float32
    ).astype(jnp.bfloat16)
    outbound = outbound.reshape(groups, per_group, TREE, local_cols)
    (inbound,), (partner_cache, partner_len) = exchange([outbound], 0, (spill_cache, own_len))
    routed_rows = inbound.reshape(n_slots * TREE, local_cols)

    key_rows = jnp.concatenate([prompt_cache[0, 0], partner_cache[0, 0]], axis=0)
    value_rows = jnp.concatenate([prompt_cache[0, 1], partner_cache[0, 1]], axis=0)
    seen = jnp.concatenate([positions < first_len[0], positions.astype(jnp.float32) < partner_len[0, 0]], axis=0)
    normed, lse = prompt_attend(routed_rows, key_rows, value_rows, seen)

    lse_width = per_group * TREE * heads_here
    lse_tile = -(-lse_width // 1024) * 1024
    lse = jnp.swapaxes(lse[:heads_here].reshape(heads_here, groups, per_group * TREE), 0, 1)
    lse_block = jnp.pad(lse.reshape(groups, lse_width), ((0, 0), (0, lse_tile - lse_width)))
    (back_out, back_lse), _ = exchange(
        [
            normed.reshape(groups, per_group, TREE, local_cols),
            lse_block.reshape(groups, lse_tile // 128, 128),
        ],
        1,
    )
    back_out = back_out.reshape(n_slots, TREE, local_cols)
    lse_index = (
        (slot_index // per_group)[:, None, None] * lse_tile
        + jnp.arange(heads_here, dtype=jnp.int32)[None, None, :] * (per_group * TREE)
        + (slot_index % per_group)[:, None, None] * TREE
        + jnp.arange(TREE, dtype=jnp.int32)[None, :, None]
    )
    remote_out = split_heads(jnp.take(back_out, slot_index, axis=0)).astype(jnp.float32)
    remote_lse = jnp.take(back_lse.reshape(groups * lse_tile), lse_index, mode="clip")

    tree_max, tree_total, tree_accum = tree_attend(
        queries, tree_cache[:, 0], tree_cache[:, 1], tree_mask == 1
    )
    peaks = jnp.maximum(remote_lse, tree_max)
    factor_remote = jnp.exp(remote_lse - peaks)
    factor_tree = jnp.exp(tree_max - peaks)
    totals = factor_remote + tree_total * factor_tree
    accum = remote_out * factor_remote[..., None] + tree_accum * factor_tree[..., None]
    attn = jnp.moveaxis(accum / totals[..., None], 2, 0).astype(jnp.bfloat16)
    attn = attn.reshape(heads_here, req_here * TREE, HD)
    projected = gather_project(attn, out_weight).reshape(req_here, TREE, out_weight.shape[1])
    accepted_cache = jnp.take_along_axis(tree_cache, accepted_path[:, None, :, None], axis=2)
    return (projected, accepted_cache)


def solution(mesh):
    return jax.shard_map(
        local,
        mesh=mesh,
        in_specs=(
            P("rep", None, "tp"),
            P("rep", None, None, "tp"),
            P("rep", None, None),
            P("rep", None),
            P("rep", None),
            P("rep", None, None, "tp"),
            P("rep"),
            P("rep", None, None, "tp"),
            P("rep"),
            P(None, "tp"),
        ),
        out_specs=(P("rep", None, "tp"), P("rep", None, None, "tp")),
        check_vma=False,
    )
```

```python
import math

import jax
import jax.numpy as jnp
from jax import lax
from jax.experimental import pallas as pl
from jax.experimental.pallas import tpu as pltpu
from jax.sharding import PartitionSpec as P

MESH = pl.DeviceIdType.MESH

HD = 128
TREE = 48
PCAP = 152


NEG_FILL = -1e30


def exchange_kernel(n, count, paired, *refs):
    sources = refs[:count]
    pair_sources = refs[count : count + paired]
    targets = refs[count + paired : 2 * count + paired]
    pair_targets = refs[2 * count + paired : 2 * count + 2 * paired]
    send_sem, recv_sem, local_sem, pair_send, pair_recv = refs[2 * count + 2 * paired :]
    me = lax.axis_index("rep")
    partner = me + 1 - 2 * (me % 2)
    barrier = pltpu.get_barrier_semaphore()
    for offset in range(1, n):
        pl.semaphore_signal(
            barrier, inc=1, device_id={"rep": lax.rem(me + offset, n)}, device_id_type=MESH
        )
    pl.semaphore_wait(barrier, n - 1)
    copies = []
    for index in range(paired):
        remote = pltpu.make_async_remote_copy(
            src_ref=pair_sources[index],
            dst_ref=pair_targets[index],
            send_sem=pair_send.at[index],
            recv_sem=pair_recv.at[index],
            device_id={"rep": partner},
            device_id_type=MESH,
        )
        remote.start()
        copies.append(remote)
    for index in range(count):
        local = pltpu.make_async_copy(
            sources[index].at[me], targets[index].at[me], local_sem.at[index]
        )
        local.start()
        copies.append(local)
        for offset in range(1, n):
            peer = lax.rem(me + offset, n)
            remote = pltpu.make_async_remote_copy(
                src_ref=sources[index].at[peer],
                dst_ref=targets[index].at[me],
                send_sem=send_sem.at[index, offset],
                recv_sem=recv_sem.at[index, offset],
                device_id={"rep": peer},
                device_id_type=MESH,
            )
            remote.start()
            copies.append(remote)
    for copy in copies:
        copy.wait()


def exchange(arrays, tag, pairs=()):
    n = lax.axis_size("rep")
    count = len(arrays)
    paired = len(pairs)
    every = list(arrays) + list(pairs)
    outs = pl.pallas_call(
        lambda *refs: exchange_kernel(n, count, paired, *refs),
        out_shape=[jax.ShapeDtypeStruct(a.shape, a.dtype) for a in every],
        in_specs=[pl.BlockSpec(memory_space=pl.ANY)] * len(every),
        out_specs=[pl.BlockSpec(memory_space=pl.ANY)] * len(every),
        scratch_shapes=[
            pltpu.SemaphoreType.DMA((count, n)),
            pltpu.SemaphoreType.DMA((count, n)),
            pltpu.SemaphoreType.DMA((count,)),
            pltpu.SemaphoreType.DMA((max(paired, 1),)),
            pltpu.SemaphoreType.DMA((max(paired, 1),)),
        ],
        compiler_params=pltpu.CompilerParams(collective_id=tag, has_side_effects=True),
    )(*every)
    return outs[:count], outs[count:]


def gather_project_kernel(n_z, a_ref, w_ref, o_ref, slots, send_sem, recv_sem):
    me = lax.axis_index("tp")
    z = me // 2
    core = me % 2
    up = lax.rem(z + 1, n_z) * 2 + core
    down = lax.rem(z + n_z - 1, n_z) * 2 + core
    sibling = z * 2 + (1 - core)
    barrier = pltpu.get_barrier_semaphore()
    for peer in (up, down, sibling):
        pl.semaphore_signal(barrier, inc=1, device_id={"tp": peer}, device_id_type=MESH)
    pl.semaphore_wait(barrier, 3)
    slots[me] = a_ref[...]
    far = n_z // 2
    near = n_z - 1 - far
    chains = ((0, 1, up, down, far), (0, -1, down, up, near), (1, 1, up, down, near), (1, -1, down, up, far))
    width = a_ref.shape[2]
    halves = slots.shape[1]
    rows = a_ref.shape[1]
    first = -(-rows // 32) * 16
    pieces = ((0, first), (first, rows - first))

    def product(slot, half, block):
        row = pl.multiple_of((slot * halves + half) * width, width)
        return jnp.dot(block, w_ref[pl.ds(row, width), :], preferred_element_type=jnp.float32)

    def arrival(slot, half, piece, sender):
        begin, size = pieces[piece]
        pltpu.make_async_remote_copy(
            src_ref=slots.at[slot, half, pl.ds(begin, size)],
            dst_ref=slots.at[slot, half, pl.ds(begin, size)],
            send_sem=send_sem.at[0, 0, 0, 0],
            recv_sem=recv_sem.at[slot, half, piece],
            device_id={"tp": sender},
            device_id_type=MESH,
        ).wait_recv()

    totals = [jnp.zeros((size, o_ref.shape[1]), jnp.float32) for _, size in pieces]
    sends = []
    for step in range(far + 1):
        for piece, (begin, size) in enumerate(pieces):
            part = pl.ds(begin, size)
            for chain, (half, direction, ahead, behind, hops) in enumerate(chains):
                if step > hops or (step == 0 and direction < 0):
                    continue
                slot = lax.rem(z - step * direction + 2 * n_z, n_z) * 2 + core
                if step == 0:
                    source = a_ref.at[half, part]
                else:
                    arrival(slot, half, piece, behind)
                    source = slots.at[slot, half, part]
                targets = [(1, sibling)]
                if step < hops:
                    targets = [(0, ahead)] + targets
                if step == 0:
                    targets = targets + [(0, down)]
                for kind, peer in targets:
                    lane = chain + (1 if peer is down and step == 0 else 0)
                    copy = pltpu.make_async_remote_copy(
                        src_ref=source,
                        dst_ref=slots.at[slot, half, part],
                        send_sem=send_sem.at[lane, piece, kind, step],
                        recv_sem=recv_sem.at[slot, half, piece],
                        device_id={"tp": peer},
                        device_id_type=MESH,
                    )
                    copy.start()
                    sends.append(copy)
                totals[piece] = totals[piece] + product(slot, half, source[...])
    for piece, (begin, size) in enumerate(pieces):
        for half, direction, ahead, behind, hops in chains:
            for step in range(hops + 1):
                if step == 0 and direction < 0:
                    continue
                slot = lax.rem(z - step * direction + 2 * n_z, n_z) * 2 + (1 - core)
                arrival(slot, half, piece, sibling)
                totals[piece] = totals[piece] + product(
                    slot, half, slots[slot, half, pl.ds(begin, size)]
                )
    for copy in sends:
        copy.wait_send()
    for piece, (begin, size) in enumerate(pieces):
        o_ref[pl.ds(begin, size), :] = totals[piece].astype(o_ref.dtype)


def gather_project(attn, weight):
    tp_size = lax.axis_size("tp")
    halves, rows, width = attn.shape
    return pl.pallas_call(
        lambda *refs: gather_project_kernel(tp_size // 2, *refs),
        out_shape=jax.ShapeDtypeStruct((rows, weight.shape[1]), jnp.bfloat16),
        in_specs=[pl.BlockSpec(memory_space=pltpu.VMEM)] * 2,
        out_specs=pl.BlockSpec(memory_space=pltpu.VMEM),
        scratch_shapes=[
            pltpu.VMEM((tp_size, halves, rows, width), jnp.bfloat16),
            pltpu.SemaphoreType.DMA((4, 2, 2, tp_size // 4 + 1)),
            pltpu.SemaphoreType.DMA((tp_size, halves, 2)),
        ],
        compiler_params=pltpu.CompilerParams(collective_id=3, has_side_effects=True),
    )(attn, weight)


def split_heads(rows):
    return rows.reshape(rows.shape[:-1] + (rows.shape[-1] // HD, HD))


def prompt_kernel(q_ref, k_ref, v_ref, seen_ref, o_ref, lse_ref):
    rows = q_ref.shape[0]
    heads = q_ref.shape[1] // HD
    visible = seen_ref[...] > 0.5
    column = lax.broadcasted_iota(jnp.int32, (rows, 128), 1)
    lse_cols = jnp.zeros((rows, 128), jnp.float32)
    for head in range(heads):
        cols = slice(head * HD, (head + 1) * HD)
        scores = lax.dot_general(
            q_ref[:, cols],
            k_ref[:, cols],
            (((1,), (1,)), ((), ())),
            preferred_element_type=jnp.float32,
        ) * (1.0 / math.sqrt(HD))
        scores = jnp.where(visible, scores, NEG_FILL)
        peaks = jnp.max(scores, axis=1, keepdims=True)
        raw = jnp.exp(scores - peaks)
        totals = jnp.sum(raw, axis=1, keepdims=True)
        accum = jnp.dot(raw.astype(jnp.bfloat16), v_ref[:, cols], preferred_element_type=jnp.float32)
        o_ref[:, cols] = (accum / totals).astype(o_ref.dtype)
        lse_cols = jnp.where(column == head, peaks + jnp.log(totals), lse_cols)
    lse_ref[...] = jnp.transpose(lse_cols)[0:8, :]


def prompt_attend(query_rows, key_rows, value_rows, seen):
    n_rows, cols = query_rows.shape
    n_keys = key_rows.shape[0]
    padded = -(-n_keys // 128) * 128
    key_rows = jnp.pad(key_rows, ((0, padded - n_keys), (0, 0)))
    value_rows = jnp.pad(value_rows, ((0, padded - n_keys), (0, 0)))
    seen_row = jnp.pad(seen.astype(jnp.float32), (0, padded - n_keys)).reshape(1, padded)
    block = 768
    return pl.pallas_call(
        prompt_kernel,
        out_shape=[
            jax.ShapeDtypeStruct((n_rows, cols), jnp.bfloat16),
            jax.ShapeDtypeStruct((8, n_rows), jnp.float32),
        ],
        grid=(n_rows // block,),
        in_specs=[
            pl.BlockSpec((block, cols), lambda i: (i, 0)),
            pl.BlockSpec((padded, cols), lambda i: (0, 0)),
            pl.BlockSpec((padded, cols), lambda i: (0, 0)),
            pl.BlockSpec((1, padded), lambda i: (0, 0)),
        ],
        out_specs=[
            pl.BlockSpec((block, cols), lambda i: (i, 0)),
            pl.BlockSpec((8, block), lambda i: (0, i)),
        ],
    )(query_rows, key_rows, value_rows, seen_row)


def tree_attend(queries, keys, values, seen):
    q = split_heads(queries)
    k = split_heads(keys)
    v = split_heads(values)
    scores = jnp.einsum("rthd,rshd->rhts", q, k, preferred_element_type=jnp.float32) * (
        1.0 / math.sqrt(HD)
    )
    scores = jnp.where(seen[:, None], scores, NEG_FILL)
    peaks = jnp.max(scores, axis=3, keepdims=True)
    raw = jnp.where(seen[:, None], jnp.exp(scores - peaks), 0.0)
    totals = jnp.sum(raw, axis=3)
    accum = jnp.einsum(
        "rhts,rshd->rthd", raw.astype(jnp.bfloat16), v, preferred_element_type=jnp.float32
    )
    return jnp.swapaxes(peaks[..., 0], 1, 2), jnp.swapaxes(totals, 1, 2), accum


def local(
    queries,
    tree_cache,
    tree_mask,
    dest_group,
    accepted_path,
    prompt_cache,
    first_len,
    spill_cache,
    spill_len,
    out_weight,
):
    req_here = queries.shape[0]
    local_cols = queries.shape[2]
    heads_here = local_cols // HD
    groups = lax.axis_size("rep")
    per_group = max(2, (req_here + groups - 1) // groups)
    n_slots = groups * per_group
    positions = jnp.arange(PCAP, dtype=jnp.int32)
    own_len = jnp.full((8, 128), spill_len[0], jnp.float32)

    target = dest_group[:, 0]
    same_target = target[:, None] == target[None, :]
    earlier = jnp.arange(req_here)[None, :] < jnp.arange(req_here)[:, None]
    rank_index = jnp.sum(jnp.logical_and(same_target, earlier), axis=1)
    slot_index = target * per_group + rank_index
    selector = (jnp.arange(n_slots, dtype=jnp.int32)[:, None] == slot_index[None, :]).astype(
        jnp.bfloat16
    )
    outbound = jnp.einsum(
        "sr,rtc->stc", selector, queries, preferred_element_type=jnp.float32
    ).astype(jnp.bfloat16)
    outbound = outbound.reshape(groups, per_group, TREE, local_cols)
    (inbound,), (partner_cache, partner_len) = exchange([outbound], 0, (spill_cache, own_len))
    routed_rows = inbound.reshape(n_slots * TREE, local_cols)

    key_rows = jnp.concatenate([prompt_cache[0, 0], partner_cache[0, 0]], axis=0)
    value_rows = jnp.concatenate([prompt_cache[0, 1], partner_cache[0, 1]], axis=0)
    seen = jnp.concatenate([positions < first_len[0], positions.astype(jnp.float32) < partner_len[0, 0]], axis=0)
    normed, lse = prompt_attend(routed_rows, key_rows, value_rows, seen)

    lse_width = per_group * TREE * heads_here
    lse_tile = -(-lse_width // 1024) * 1024
    lse = jnp.swapaxes(lse[:heads_here].reshape(heads_here, groups, per_group * TREE), 0, 1)
    lse_block = jnp.pad(lse.reshape(groups, lse_width), ((0, 0), (0, lse_tile - lse_width)))
    (back_out, back_lse), _ = exchange(
        [
            normed.reshape(groups, per_group, TREE, local_cols),
            lse_block.reshape(groups, lse_tile // 128, 128),
        ],
        1,
    )
    back_out = back_out.reshape(n_slots, TREE, local_cols)
    back_lse = back_lse.reshape(groups, lse_tile)[:, :lse_width]
    back_lse = jnp.moveaxis(back_lse.reshape(groups, heads_here, per_group, TREE), 1, 3)
    back_lse = back_lse.reshape(n_slots, TREE, heads_here)
    remote_out = split_heads(jnp.take(back_out, slot_index, axis=0)).astype(jnp.float32)
    remote_lse = jnp.take(back_lse, slot_index, axis=0)

    tree_max, tree_total, tree_accum = tree_attend(
        queries, tree_cache[:, 0], tree_cache[:, 1], tree_mask == 1
    )
    peaks = jnp.maximum(remote_lse, tree_max)
    factor_remote = jnp.exp(remote_lse - peaks)
    factor_tree = jnp.exp(tree_max - peaks)
    totals = factor_remote + tree_total * factor_tree
    accum = remote_out * factor_remote[..., None] + tree_accum * factor_tree[..., None]
    attn = jnp.moveaxis(accum / totals[..., None], 2, 0).astype(jnp.bfloat16)
    attn = attn.reshape(heads_here, req_here * TREE, HD)
    projected = gather_project(attn, out_weight).reshape(req_here, TREE, out_weight.shape[1])
    accepted_cache = jnp.take_along_axis(tree_cache, accepted_path[:, None, :, None], axis=2)
    return (projected, accepted_cache)


def solution(mesh):
    return jax.shard_map(
        local,
        mesh=mesh,
        in_specs=(
            P("rep", None, "tp"),
            P("rep", None, None, "tp"),
            P("rep", None, None),
            P("rep", None),
            P("rep", None),
            P("rep", None, None, "tp"),
            P("rep"),
            P("rep", None, None, "tp"),
            P("rep"),
            P(None, "tp"),
        ),
        out_specs=(P("rep", None, "tp"), P("rep", None, None, "tp")),
        check_vma=False,
    )
```

```python
import math

import jax
import jax.numpy as jnp
from jax import lax
from jax.experimental import pallas as pl
from jax.experimental.pallas import tpu as pltpu
from jax.sharding import PartitionSpec as P

MESH = pl.DeviceIdType.MESH

HD = 128
TREE = 48
PCAP = 152


NEG_FILL = -1e30


def exchange_kernel(n, count, paired, *refs):
    sources = refs[:count]
    pair_sources = refs[count : count + paired]
    targets = refs[count + paired : 2 * count + paired]
    pair_targets = refs[2 * count + paired : 2 * count + 2 * paired]
    send_sem, recv_sem, local_sem, pair_send, pair_recv = refs[2 * count + 2 * paired :]
    me = lax.axis_index("rep")
    partner = me + 1 - 2 * (me % 2)
    barrier = pltpu.get_barrier_semaphore()
    for offset in range(1, n):
        pl.semaphore_signal(
            barrier, inc=1, device_id={"rep": lax.rem(me + offset, n)}, device_id_type=MESH
        )
    pl.semaphore_wait(barrier, n - 1)
    copies = []
    for index in range(paired):
        remote = pltpu.make_async_remote_copy(
            src_ref=pair_sources[index],
            dst_ref=pair_targets[index],
            send_sem=pair_send.at[index],
            recv_sem=pair_recv.at[index],
            device_id={"rep": partner},
            device_id_type=MESH,
        )
        remote.start()
        copies.append(remote)
    for index in range(count):
        for offset in range(1, n):
            peer = lax.rem(me + offset, n)
            remote = pltpu.make_async_remote_copy(
                src_ref=sources[index].at[peer],
                dst_ref=targets[index].at[me],
                send_sem=send_sem.at[index, offset],
                recv_sem=recv_sem.at[index, offset],
                device_id={"rep": peer},
                device_id_type=MESH,
            )
            remote.start()
            copies.append(remote)
    for copy in copies:
        copy.wait()


def exchange(arrays, tag, pairs=()):
    n = lax.axis_size("rep")
    count = len(arrays)
    paired = len(pairs)
    every = list(arrays) + list(pairs)
    outs = pl.pallas_call(
        lambda *refs: exchange_kernel(n, count, paired, *refs),
        out_shape=[jax.ShapeDtypeStruct(a.shape, a.dtype) for a in every],
        in_specs=[pl.BlockSpec(memory_space=pl.ANY)] * len(every),
        out_specs=[pl.BlockSpec(memory_space=pl.ANY)] * len(every),
        scratch_shapes=[
            pltpu.SemaphoreType.DMA((count, n)),
            pltpu.SemaphoreType.DMA((count, n)),
            pltpu.SemaphoreType.DMA((count,)),
            pltpu.SemaphoreType.DMA((max(paired, 1),)),
            pltpu.SemaphoreType.DMA((max(paired, 1),)),
        ],
        compiler_params=pltpu.CompilerParams(collective_id=tag, has_side_effects=True),
    )(*every)
    me = lax.axis_index("rep")
    placed = [
        lax.dynamic_update_index_in_dim(out, lax.dynamic_index_in_dim(a, me, 0), me, 0)
        for out, a in zip(outs[:count], arrays)
    ]
    return placed, outs[count:]


def gather_project_kernel(n_z, a_ref, w_ref, o_ref, slots, send_sem, recv_sem):
    me = lax.axis_index("tp")
    z = me // 2
    core = me % 2
    up = lax.rem(z + 1, n_z) * 2 + core
    down = lax.rem(z + n_z - 1, n_z) * 2 + core
    sibling = z * 2 + (1 - core)
    barrier = pltpu.get_barrier_semaphore()
    for peer in (up, down, sibling):
        pl.semaphore_signal(barrier, inc=1, device_id={"tp": peer}, device_id_type=MESH)
    pl.semaphore_wait(barrier, 3)
    slots[me] = a_ref[...]
    far = n_z // 2
    near = n_z - 1 - far
    chains = ((0, 1, up, down, far), (0, -1, down, up, near), (1, 1, up, down, near), (1, -1, down, up, far))
    width = a_ref.shape[2]
    halves = slots.shape[1]

    def product(slot, half, block):
        row = pl.multiple_of((slot * halves + half) * width, width)
        return jnp.dot(block, w_ref[pl.ds(row, width), :], preferred_element_type=jnp.float32)

    def arrival(slot, half, sender):
        pltpu.make_async_remote_copy(
            src_ref=slots.at[slot, half],
            dst_ref=slots.at[slot, half],
            send_sem=send_sem.at[0, 0, 0],
            recv_sem=recv_sem.at[slot, half],
            device_id={"tp": sender},
            device_id_type=MESH,
        ).wait_recv()

    total = jnp.zeros(o_ref.shape, jnp.float32)
    sends = []
    for step in range(far + 1):
        for chain, (half, direction, ahead, behind, hops) in enumerate(chains):
            if step > hops or (step == 0 and direction < 0):
                continue
            slot = lax.rem(z - step * direction + 2 * n_z, n_z) * 2 + core
            if step == 0:
                source = a_ref.at[half]
            else:
                arrival(slot, half, behind)
                source = slots.at[slot, half]
            targets = [(1, sibling)]
            if step < hops:
                targets = [(0, ahead)] + targets
            if step == 0:
                targets = targets + [(0, down)]
            for kind, peer in targets:
                copy = pltpu.make_async_remote_copy(
                    src_ref=source,
                    dst_ref=slots.at[slot, half],
                    send_sem=send_sem.at[chain + (1 if peer is down and step == 0 else 0), kind, step],
                    recv_sem=recv_sem.at[slot, half],
                    device_id={"tp": peer},
                    device_id_type=MESH,
                )
                copy.start()
                sends.append(copy)
            total = total + product(slot, half, source[...])
    for half, direction, ahead, behind, hops in chains:
        for step in range(hops + 1):
            if step == 0 and direction < 0:
                continue
            slot = lax.rem(z - step * direction + 2 * n_z, n_z) * 2 + (1 - core)
            arrival(slot, half, sibling)
            total = total + product(slot, half, slots[slot, half])
    for copy in sends:
        copy.wait_send()
    o_ref[...] = total.astype(o_ref.dtype)


def gather_project(attn, weight):
    tp_size = lax.axis_size("tp")
    halves, rows, width = attn.shape
    return pl.pallas_call(
        lambda *refs: gather_project_kernel(tp_size // 2, *refs),
        out_shape=jax.ShapeDtypeStruct((rows, weight.shape[1]), jnp.bfloat16),
        in_specs=[pl.BlockSpec(memory_space=pltpu.VMEM)] * 2,
        out_specs=pl.BlockSpec(memory_space=pltpu.VMEM),
        scratch_shapes=[
            pltpu.VMEM((tp_size, halves, rows, width), jnp.bfloat16),
            pltpu.SemaphoreType.DMA((4, 2, tp_size // 4 + 1)),
            pltpu.SemaphoreType.DMA((tp_size, halves)),
        ],
        compiler_params=pltpu.CompilerParams(collective_id=3, has_side_effects=True),
    )(attn, weight)


def split_heads(rows):
    return rows.reshape(rows.shape[:-1] + (rows.shape[-1] // HD, HD))


def prompt_kernel(q_ref, k_ref, v_ref, seen_ref, o_ref, lse_ref):
    rows = q_ref.shape[0]
    heads = q_ref.shape[1] // HD
    visible = seen_ref[...] > 0.5
    column = lax.broadcasted_iota(jnp.int32, (rows, 128), 1)
    lse_cols = jnp.zeros((rows, 128), jnp.float32)
    for head in range(heads):
        cols = slice(head * HD, (head + 1) * HD)
        scores = lax.dot_general(
            q_ref[:, cols],
            k_ref[:, cols],
            (((1,), (1,)), ((), ())),
            preferred_element_type=jnp.float32,
        ) * (1.0 / math.sqrt(HD))
        scores = jnp.where(visible, scores, NEG_FILL)
        peaks = jnp.max(scores, axis=1, keepdims=True)
        raw = jnp.exp(scores - peaks)
        totals = jnp.sum(raw, axis=1, keepdims=True)
        accum = jnp.dot(raw.astype(jnp.bfloat16), v_ref[:, cols], preferred_element_type=jnp.float32)
        o_ref[:, cols] = (accum / totals).astype(o_ref.dtype)
        lse_cols = jnp.where(column == head, peaks + jnp.log(totals), lse_cols)
    lse_ref[...] = jnp.transpose(lse_cols)[0:8, :]


def prompt_attend(query_rows, key_rows, value_rows, seen):
    n_rows, cols = query_rows.shape
    n_keys = key_rows.shape[0]
    padded = -(-n_keys // 128) * 128
    key_rows = jnp.pad(key_rows, ((0, padded - n_keys), (0, 0)))
    value_rows = jnp.pad(value_rows, ((0, padded - n_keys), (0, 0)))
    seen_row = jnp.pad(seen.astype(jnp.float32), (0, padded - n_keys)).reshape(1, padded)
    block = 768
    return pl.pallas_call(
        prompt_kernel,
        out_shape=[
            jax.ShapeDtypeStruct((n_rows, cols), jnp.bfloat16),
            jax.ShapeDtypeStruct((8, n_rows), jnp.float32),
        ],
        grid=(n_rows // block,),
        in_specs=[
            pl.BlockSpec((block, cols), lambda i: (i, 0)),
            pl.BlockSpec((padded, cols), lambda i: (0, 0)),
            pl.BlockSpec((padded, cols), lambda i: (0, 0)),
            pl.BlockSpec((1, padded), lambda i: (0, 0)),
        ],
        out_specs=[
            pl.BlockSpec((block, cols), lambda i: (i, 0)),
            pl.BlockSpec((8, block), lambda i: (0, i)),
        ],
    )(query_rows, key_rows, value_rows, seen_row)


def tree_attend(queries, keys, values, seen):
    q = split_heads(queries)
    k = split_heads(keys)
    v = split_heads(values)
    scores = jnp.einsum("rthd,rshd->rhts", q, k, preferred_element_type=jnp.float32) * (
        1.0 / math.sqrt(HD)
    )
    scores = jnp.where(seen[:, None], scores, NEG_FILL)
    peaks = jnp.max(scores, axis=3, keepdims=True)
    raw = jnp.where(seen[:, None], jnp.exp(scores - peaks), 0.0)
    totals = jnp.sum(raw, axis=3)
    accum = jnp.einsum(
        "rhts,rshd->rthd", raw.astype(jnp.bfloat16), v, preferred_element_type=jnp.float32
    )
    return jnp.swapaxes(peaks[..., 0], 1, 2), jnp.swapaxes(totals, 1, 2), accum


def local(
    queries,
    tree_cache,
    tree_mask,
    dest_group,
    accepted_path,
    prompt_cache,
    first_len,
    spill_cache,
    spill_len,
    out_weight,
):
    req_here = queries.shape[0]
    local_cols = queries.shape[2]
    heads_here = local_cols // HD
    groups = lax.axis_size("rep")
    per_group = max(2, (req_here + groups - 1) // groups)
    n_slots = groups * per_group
    positions = jnp.arange(PCAP, dtype=jnp.int32)
    own_len = jnp.full((8, 128), spill_len[0], jnp.float32)

    target = dest_group[:, 0]
    same_target = target[:, None] == target[None, :]
    earlier = jnp.arange(req_here)[None, :] < jnp.arange(req_here)[:, None]
    rank_index = jnp.sum(jnp.logical_and(same_target, earlier), axis=1)
    slot_index = target * per_group + rank_index
    selector = (jnp.arange(n_slots, dtype=jnp.int32)[:, None] == slot_index[None, :]).astype(
        jnp.bfloat16
    )
    outbound = jnp.einsum(
        "sr,rtc->stc", selector, queries, preferred_element_type=jnp.float32
    ).astype(jnp.bfloat16)
    outbound = outbound.reshape(groups, per_group, TREE, local_cols)
    (inbound,), (partner_cache, partner_len) = exchange([outbound], 0, (spill_cache, own_len))
    routed_rows = inbound.reshape(n_slots * TREE, local_cols)

    key_rows = jnp.concatenate([prompt_cache[0, 0], partner_cache[0, 0]], axis=0)
    value_rows = jnp.concatenate([prompt_cache[0, 1], partner_cache[0, 1]], axis=0)
    seen = jnp.concatenate([positions < first_len[0], positions.astype(jnp.float32) < partner_len[0, 0]], axis=0)
    normed, lse = prompt_attend(routed_rows, key_rows, value_rows, seen)

    lse_width = per_group * TREE * heads_here
    lse_tile = -(-lse_width // 1024) * 1024
    lse = jnp.swapaxes(lse[:heads_here].reshape(heads_here, groups, per_group * TREE), 0, 1)
    lse_block = jnp.pad(lse.reshape(groups, lse_width), ((0, 0), (0, lse_tile - lse_width)))
    (back_out, back_lse), _ = exchange(
        [
            normed.reshape(groups, per_group, TREE, local_cols),
            lse_block.reshape(groups, lse_tile // 128, 128),
        ],
        1,
    )
    back_out = back_out.reshape(n_slots, TREE, local_cols)
    back_lse = back_lse.reshape(groups, lse_tile)[:, :lse_width]
    back_lse = jnp.moveaxis(back_lse.reshape(groups, heads_here, per_group, TREE), 1, 3)
    back_lse = back_lse.reshape(n_slots, TREE, heads_here)
    remote_out = split_heads(jnp.take(back_out, slot_index, axis=0)).astype(jnp.float32)
    remote_lse = jnp.take(back_lse, slot_index, axis=0)

    tree_max, tree_total, tree_accum = tree_attend(
        queries, tree_cache[:, 0], tree_cache[:, 1], tree_mask == 1
    )
    peaks = jnp.maximum(remote_lse, tree_max)
    factor_remote = jnp.exp(remote_lse - peaks)
    factor_tree = jnp.exp(tree_max - peaks)
    totals = factor_remote + tree_total * factor_tree
    accum = remote_out * factor_remote[..., None] + tree_accum * factor_tree[..., None]
    attn = jnp.moveaxis(accum / totals[..., None], 2, 0).astype(jnp.bfloat16)
    attn = attn.reshape(heads_here, req_here * TREE, HD)
    projected = gather_project(attn, out_weight).reshape(req_here, TREE, out_weight.shape[1])
    accepted_cache = jnp.take_along_axis(tree_cache, accepted_path[:, None, :, None], axis=2)
    return (projected, accepted_cache)


def solution(mesh):
    return jax.shard_map(
        local,
        mesh=mesh,
        in_specs=(
            P("rep", None, "tp"),
            P("rep", None, None, "tp"),
            P("rep", None, None),
            P("rep", None),
            P("rep", None),
            P("rep", None, None, "tp"),
            P("rep"),
            P("rep", None, None, "tp"),
            P("rep"),
            P(None, "tp"),
        ),
        out_specs=(P("rep", None, "tp"), P("rep", None, None, "tp")),
        check_vma=False,
    )
```
